32 devices in a mesh: seq: 4 (over z), fsdp: 8 (over y, x, core).
Axes of the slice: x: 2, y: 2, z: 4, core: 2. Of those that a mesh axis runs over, the one named last changes fastest.
Arguments:
- block_input: bfloat16 [8, 512, 1152], P('fsdp', 'seq'), may hold values from -60 to 60
- grad_output: bfloat16 [8, 512, 1152], P('fsdp', 'seq'), may hold values from -6 to 6
- attn_norm_gain: bfloat16 [2, 1152], P(None, 'fsdp'), may hold values from 0.25 to 1.75
- attn_norm_bias: bfloat16 [2, 1152], P(None, 'fsdp'), may hold values from -3 to 3
- qkv_weight: bfloat16 [2, 1152, 3456], P(None, 'fsdp'), may hold values from -0.19939321 to 0.19939321
- qv_bias: bfloat16 [2, 2, 1152], P(None, None, 'fsdp'), may hold values from -3 to 3
- out_weight: bfloat16 [2, 1152, 1152], P(None, 'fsdp'), may hold values from -6 to 6
- out_bias: bfloat16 [2, 1152], P(None, 'fsdp'), may hold values from -3 to 3
- mlp_norm_gain: bfloat16 [2, 1152], P(None, 'fsdp'), may hold values from 0.25 to 1.75
- mlp_norm_bias: bfloat16 [2, 1152], P(None, 'fsdp'), may hold values from -3 to 3
- up_weight: bfloat16 [2, 1152, 4304], P(None, 'fsdp'), may hold values from -0.1875 to 0.1875
- up_bias: bfloat16 [2, 4304], P(None, 'fsdp'), may hold values from -3 to 3
- down_weight: bfloat16 [2, 4304, 1152], P(None, 'fsdp'), may hold values from -0.09375 to 0.09375
- down_bias: bfloat16 [2, 1152], P(None, 'fsdp'), may hold values from -3 to 3
Outputs:
- block_output: bfloat16 [8, 512, 1152], P('fsdp', 'seq')
- grad_input: float32 [8, 512, 1152], P('fsdp', 'seq')
- grad_attn_norm_gain: float32 [2, 1152], P(None, 'fsdp')
- grad_attn_norm_bias: float32 [2, 1152], P(None, 'fsdp')
- grad_qkv_weight: float32 [2, 1152, 3456], P(None, 'fsdp')
- grad_qv_bias: float32 [2, 2, 1152], P(None, None, 'fsdp')
- grad_out_weight: float32 [2, 1152, 1152], P(None, 'fsdp')
- grad_out_bias: float32 [2, 1152], P(None, 'fsdp')
- grad_mlp_norm_gain: float32 [2, 1152], P(None, 'fsdp')
- grad_mlp_norm_bias: float32 [2, 1152], P(None, 'fsdp')
- grad_up_weight: float32 [2, 1152, 4304], P(None, 'fsdp')
- grad_up_bias: float32 [2, 4304], P(None, 'fsdp')
- grad_down_weight: float32 [2, 4304, 1152], P(None, 'fsdp')
- grad_down_bias: float32 [2, 1152], P(None, 'fsdp')
The draws below stay inside these ranges and needn't reach their ends.
All inputs are finite; a program needn't handle non-finite values.
Results may differ from the reference program's by a relative error of at most 0.018.
The reference program's roundings to bfloat16 on the way count: a program that leaves them out, or rounds other values in their place, can miss the bound.
Values may be sent and summed in bfloat16 or wider, within the bound.
No kernel may reach another device: no remote copies, remote signals or barrier semaphores. Data moves between devices by JAX's collectives and lax.ppermute only.
A program may use at most 384 MiB of HBM per device.

```python
import jax
import jax.numpy as jnp
from jax import lax

D = 1152
HEADS = 16
HEAD_DIM = 72
FF = 4304
LAYERS = 2
IMAGES = 8
SEQ_LEN = 512
QUERY_BLOCK = 512


def draw_block_input(key, part):
    key_list = jax.random.split(key, 1)
    values = jnp.clip(jax.random.normal(key_list[0], (IMAGES, SEQ_LEN, D), jnp.float32), -6.0, 6.0)
    return values.astype(jnp.bfloat16)


def draw_qkv_weight(key, part):
    key_list = jax.random.split(key, 1)
    matrix = jnp.clip(jax.random.normal(key_list[0], (LAYERS, D, 3 * D), jnp.float32), -6.0, 6.0) * D ** (-0.5)
    return matrix.astype(jnp.bfloat16)


def spiked(values, stream_key, source, target, parts, factor):
    owner, partner = [(jnp.arange(values.shape[dim]) // (values.shape[dim] // parts)).reshape([-1 if axis == dim else 1 for axis in range(values.ndim)]) for dim in (source, target)]
    chosen = jax.random.permutation(stream_key, parts)[partner]
    strong = (owner == chosen) | (owner == (partner + parts // 2) % parts)
    return jnp.where(strong, factor * values, values)


def shard_levels(rng, shape, cuts, low, high):
    level = 1.0
    for axis_at, shards_of in cuts:
        draws = jax.random.uniform(jax.random.fold_in(jax.random.fold_in(rng, 6), axis_at), (shards_of,), jnp.float32, low / len(cuts), high / len(cuts))
        level = level * jnp.repeat(jnp.exp(draws), shape[axis_at] // shards_of).reshape((-1,) + (1,) * (len(shape) - 1 - axis_at))
    return level


def gaussian(key, shape, scale, most, cuts=(), kind=jnp.bfloat16):
    values = scale * jax.random.normal(key, shape, jnp.float32)
    if cuts:
        values = values * shard_levels(key, shape, cuts, -0.22, 0.18)
    return jnp.clip(values, -most, most).astype(kind)


def bell_draw_with(stream_key, dims, width, most, cuts, heavy, held_as=jnp.bfloat16):
    entries = width * jax.random.normal(stream_key, dims, jnp.float32)
    if cuts:
        entries = entries * shard_levels(stream_key, dims, cuts, -0.22, 0.18)
    return jnp.clip(spiked(entries, jax.random.fold_in(stream_key, 3), *heavy), -most, most).astype(held_as)


def setup_inputs(seed: int = 0) -> dict:
    streams_of = jax.random.split(jax.random.key(seed), 15)
    return {
        "block_input": draw_block_input(jax.random.fold_in(streams_of[14], 71), 0),
        "grad_output": bell_draw_with(streams_of[1], (IMAGES, SEQ_LEN, D), 1.0, 6.0, ((0, 8), (1, 4)), (0, 2, 8, 2.0)),
        "attn_norm_gain": jnp.clip(1.0 + 0.15 * jax.random.normal(streams_of[2], (LAYERS, D), jnp.float32), 0.25, 1.75).astype(jnp.bfloat16),
        "attn_norm_bias": gaussian(streams_of[3], (LAYERS, D), 0.5, 3.0, ((1, 8),)),
        "qkv_weight": draw_qkv_weight(jax.random.fold_in(streams_of[14], 71), 0),
        "qv_bias": gaussian(streams_of[5], (LAYERS, 2, D), 0.5, 3.0, ((2, 8),)),
        "out_weight": gaussian(streams_of[6], (LAYERS, D, D), (0.6 * SEQ_LEN ** 0.5 * D ** -0.5), 6.0, ((1, 8),)),
        "out_bias": gaussian(streams_of[7], (LAYERS, D), 0.5, 3.0, ((1, 8),)),
        "mlp_norm_gain": jnp.clip(1.0 + 0.15 * jax.random.normal(streams_of[8], (LAYERS, D), jnp.float32), 0.25, 1.75).astype(jnp.bfloat16),
        "mlp_norm_bias": gaussian(streams_of[9], (LAYERS, D), 0.5, 3.0, ((1, 8),)),
        "up_weight": gaussian(streams_of[10], (LAYERS, D, FF), D ** -0.5, 0.1875, ((1, 8),)),
        "up_bias": gaussian(streams_of[11], (LAYERS, FF), 0.5, 3.0, ((1, 8),)),
        "down_weight": gaussian(streams_of[12], (LAYERS, FF, D), FF ** -0.5, 0.09375, ((1, 8),)),
        "down_bias": gaussian(streams_of[13], (LAYERS, D), 0.5, 3.0, ((1, 8),)),
    }


EPSILON = 1e-06

def round_low(values):
    return lax.optimization_barrier(values.astype(jnp.bfloat16))

def normalize(hidden, norm_gain, norm_offset):
    center = hidden - lax.optimization_barrier(jnp.mean(hidden, axis=-1, keepdims=True))
    variance = lax.optimization_barrier(jnp.mean(center * center, axis=-1, keepdims=True))
    inverse_std = lax.rsqrt(variance + EPSILON)
    normed = center * inverse_std
    return (normed * norm_gain.astype(jnp.float32) + norm_offset.astype(jnp.float32), normed, inverse_std)

def normalize_back(upstream, normed, inverse_std, norm_gain):
    scaled = upstream * norm_gain.astype(jnp.float32)
    grad_hidden = inverse_std * (scaled - lax.optimization_barrier(jnp.mean(scaled, axis=-1, keepdims=True)) - normed * lax.optimization_barrier(jnp.mean(scaled * normed, axis=-1, keepdims=True)))
    return (grad_hidden, lax.optimization_barrier(jnp.sum(upstream * normed, axis=0)), lax.optimization_barrier(jnp.sum(upstream, axis=0)))

def tangent_gelu(values):
    return jax.nn.gelu(values, approximate=True)

def gelu_back(values, upstream):
    return jax.vjp(tangent_gelu, values)[1](upstream)[0]

def attend_forward(query_block, key_heads, value_heads, scaling):
    scores = jnp.einsum('qhd,khd->hqk', query_block.astype(jnp.float32), key_heads.astype(jnp.float32)) * scaling
    row_peak = lax.optimization_barrier(jnp.max(scores, axis=-1, keepdims=True))
    logsum = row_peak + jnp.log(lax.optimization_barrier(jnp.sum(jnp.exp(scores - row_peak), axis=-1, keepdims=True)))
    probability = round_low(jnp.exp(scores - logsum))
    output = jnp.einsum('hqk,khd->qhd', probability.astype(jnp.float32), value_heads.astype(jnp.float32))
    return (round_low(output), logsum[..., 0])

def attend_backward(query_block, key_heads, value_heads, grad_block, logsum_block, scaling):
    scores = jnp.einsum('qhd,khd->hqk', query_block.astype(jnp.float32), key_heads.astype(jnp.float32)) * scaling
    probability = jnp.exp(scores - logsum_block[..., None])
    prob_low = round_low(probability)
    grad_value = jnp.einsum('hqk,qhd->khd', prob_low.astype(jnp.float32), grad_block.astype(jnp.float32))
    grad_prob = jnp.einsum('qhd,khd->hqk', grad_block.astype(jnp.float32), value_heads.astype(jnp.float32))
    row_inner = lax.optimization_barrier(jnp.sum(probability * grad_prob, axis=-1, keepdims=True))
    grad_scores = round_low(probability * (grad_prob - row_inner)).astype(jnp.float32)
    grad_query = jnp.einsum('hqk,khd->qhd', grad_scores, key_heads.astype(jnp.float32)) * scaling
    grad_key = jnp.einsum('hqk,qhd->khd', grad_scores, query_block.astype(jnp.float32)) * scaling
    return (round_low(grad_query), grad_key, grad_value)

def attention_forward(queries, keys_tok, values_tok):
    block_count = SEQ_LEN // QUERY_BLOCK
    query_blocks = queries.reshape(block_count, QUERY_BLOCK, HEADS, HEAD_DIM)
    key_heads = keys_tok.reshape(SEQ_LEN, HEADS, HEAD_DIM)
    value_heads = values_tok.reshape(SEQ_LEN, HEADS, HEAD_DIM)
    outputs, logsums = lax.map(lambda query_block: attend_forward(query_block, key_heads, value_heads, HEAD_DIM ** (-0.5)), query_blocks)
    return (outputs.reshape(SEQ_LEN, D), logsums)

def attention_backward(queries, keys_tok, values_tok, grad_tok, logsums):
    block_count = SEQ_LEN // QUERY_BLOCK
    query_blocks = queries.reshape(block_count, QUERY_BLOCK, HEADS, HEAD_DIM)
    grad_blocks = grad_tok.reshape(block_count, QUERY_BLOCK, HEADS, HEAD_DIM)
    key_heads = keys_tok.reshape(SEQ_LEN, HEADS, HEAD_DIM)
    value_heads = values_tok.reshape(SEQ_LEN, HEADS, HEAD_DIM)

    def step(totals, inputs):
        query_block, grad_block, logsum_block = inputs
        grad_query, grad_key, grad_value = attend_backward(query_block, key_heads, value_heads, grad_block, logsum_block, HEAD_DIM ** (-0.5))
        return ((totals[0] + grad_key, totals[1] + grad_value), grad_query)
    start = jnp.zeros((SEQ_LEN, HEADS, HEAD_DIM), jnp.float32)
    (grad_keys, grad_values), grad_queries = lax.scan(step, (start, start), (query_blocks, grad_blocks, logsums))
    return (grad_queries.reshape(SEQ_LEN, D), round_low(grad_keys).reshape(SEQ_LEN, D), round_low(grad_values).reshape(SEQ_LEN, D))

def run_image(image_tokens, image_grad, params):
    attn_norm_gain, attn_norm_bias, qkv_weight, qv_bias, out_weight, out_bias, mlp_norm_gain, mlp_norm_bias, up_weight, up_bias, down_weight, down_bias = params
    hidden = image_tokens.astype(jnp.float32)
    stored = []
    for layer_number in range(LAYERS):
        normed_in, normed_one, inverse_one = normalize(hidden, attn_norm_gain[layer_number], attn_norm_bias[layer_number])
        attn_in = round_low(normed_in)
        bias_row = jnp.concatenate([qv_bias[layer_number, 0].astype(jnp.float32), jnp.zeros((D,), jnp.float32), qv_bias[layer_number, 1].astype(jnp.float32)])
        projected = jnp.dot(attn_in, qkv_weight[layer_number], preferred_element_type=jnp.float32) + bias_row
        queries = round_low(projected[:, :D])
        keys_tok = round_low(projected[:, D:2 * D])
        values_tok = round_low(projected[:, 2 * D:])
        attended, logsums = attention_forward(queries, keys_tok, values_tok)
        after_attn = hidden + jnp.dot(attended, out_weight[layer_number], preferred_element_type=jnp.float32) + out_bias[layer_number].astype(jnp.float32)
        normed_mid, normed_two, inverse_two = normalize(after_attn, mlp_norm_gain[layer_number], mlp_norm_bias[layer_number])
        mlp_in = round_low(normed_mid)
        pre_act = jnp.dot(mlp_in, up_weight[layer_number], preferred_element_type=jnp.float32) + up_bias[layer_number].astype(jnp.float32)
        activated = round_low(tangent_gelu(pre_act))
        hidden = after_attn + jnp.dot(activated, down_weight[layer_number], preferred_element_type=jnp.float32) + down_bias[layer_number].astype(jnp.float32)
        stored.append((normed_one, inverse_one, attn_in, queries, keys_tok, values_tok, logsums, attended, normed_two, inverse_two, mlp_in, pre_act, activated))
    result = hidden.astype(jnp.bfloat16)
    grad_hidden = image_grad.astype(jnp.float32)
    per_layer = [None] * LAYERS
    for layer_number in reversed(range(LAYERS)):
        normed_one, inverse_one, attn_in, queries, keys_tok, values_tok, logsums, attended, normed_two, inverse_two, mlp_in, pre_act, activated = stored[layer_number]
        grad_low = round_low(grad_hidden)
        g_down_bias = lax.optimization_barrier(jnp.sum(grad_hidden, axis=0))
        g_down = jnp.dot(activated.T, grad_low, preferred_element_type=jnp.float32)
        grad_act = jnp.dot(grad_low, down_weight[layer_number].T, preferred_element_type=jnp.float32)
        grad_pre = gelu_back(pre_act, grad_act)
        g_up_bias = lax.optimization_barrier(jnp.sum(grad_pre, axis=0))
        grad_pre_low = round_low(grad_pre)
        g_up = jnp.dot(mlp_in.T, grad_pre_low, preferred_element_type=jnp.float32)
        grad_mid = jnp.dot(grad_pre_low, up_weight[layer_number].T, preferred_element_type=jnp.float32)
        grad_norm_two, g_gain_two, g_offset_two = normalize_back(grad_mid, normed_two, inverse_two, mlp_norm_gain[layer_number])
        grad_after = grad_hidden + grad_norm_two
        g_out_bias = lax.optimization_barrier(jnp.sum(grad_after, axis=0))
        after_low = round_low(grad_after)
        g_out = jnp.dot(attended.T, after_low, preferred_element_type=jnp.float32)
        grad_attended = round_low(jnp.dot(after_low, out_weight[layer_number].T, preferred_element_type=jnp.float32))
        grad_q, grad_k, grad_v = attention_backward(queries, keys_tok, values_tok, grad_attended, logsums)
        grad_proj = jnp.concatenate([grad_q, grad_k, grad_v], axis=1)
        g_qkv = jnp.dot(attn_in.T, grad_proj, preferred_element_type=jnp.float32)
        g_qv_bias = jnp.stack([lax.optimization_barrier(jnp.sum(grad_q.astype(jnp.float32), axis=0)), lax.optimization_barrier(jnp.sum(grad_v.astype(jnp.float32), axis=0))])
        grad_in = jnp.dot(grad_proj, qkv_weight[layer_number].T, preferred_element_type=jnp.float32)
        grad_norm_one, g_gain_one, g_offset_one = normalize_back(grad_in, normed_one, inverse_one, attn_norm_gain[layer_number])
        grad_hidden = grad_after + grad_norm_one
        per_layer[layer_number] = (g_gain_one, g_offset_one, g_qkv, g_qv_bias, g_out, g_out_bias, g_gain_two, g_offset_two, g_up, g_up_bias, g_down, g_down_bias)
    grads = tuple((jnp.stack([entry[member] for entry in per_layer]) for member in range(12)))
    return (result, grad_hidden, grads)

def reference(block_input, grad_output, attn_norm_gain, attn_norm_bias, qkv_weight, qv_bias, out_weight, out_bias, mlp_norm_gain, mlp_norm_bias, up_weight, up_bias, down_weight, down_bias):
    params = (attn_norm_gain, attn_norm_bias, qkv_weight, qv_bias, out_weight, out_bias, mlp_norm_gain, mlp_norm_bias, up_weight, up_bias, down_weight, down_bias)

    def image_pass(totals, inputs):
        image_tokens, image_grad = inputs
        result, grad_in, grads = run_image(image_tokens, image_grad, params)
        return (jax.tree.map(lambda left, right: left + right, totals, grads), (result, grad_in))
    start = tuple((jnp.zeros(weight_arg.shape, jnp.float32) for weight_arg in params))
    totals, (outputs, grad_inputs) = lax.scan(image_pass, start, (block_input, grad_output))
    return (outputs, grad_inputs, totals[0], totals[1], totals[2], totals[3], totals[4], totals[5], totals[6], totals[7], totals[8], totals[9], totals[10], totals[11])
```

```python
import functools

import jax
import jax.numpy as jnp
from jax import lax
from jax.experimental import pallas as pl
from jax.experimental.pallas import tpu as pltpu
from jax.sharding import PartitionSpec as P

HEAD_DIM = 72
EPSILON = 1e-06
LOW = jnp.bfloat16
FULL = jnp.float32


def normalize(hidden):
    center = hidden - jnp.mean(hidden, axis=-1, keepdims=True)
    variance = jnp.mean(center * center, axis=-1, keepdims=True)
    inverse_std = lax.rsqrt(variance + EPSILON)
    return center * inverse_std, inverse_std


def normalize_back(upstream, normed, inverse_std, gain):
    scaled = upstream * gain
    grad_hidden = inverse_std * (
        scaled
        - jnp.mean(scaled, axis=-1, keepdims=True)
        - normed * jnp.mean(scaled * normed, axis=-1, keepdims=True)
    )
    return grad_hidden, jnp.sum(upstream * normed, axis=0), jnp.sum(upstream, axis=0)


def tangent_gelu(values):
    return jax.nn.gelu(values, approximate=True)


def gelu_back(values, upstream):
    return jax.vjp(tangent_gelu, values)[1](upstream)[0]


def mm(left, right):
    return jnp.dot(left, right, preferred_element_type=FULL)


def mm_rows(left, right):
    return lax.dot_general(left, right, (((0,), (0,)), ((), ())), preferred_element_type=FULL)


def mm_cols(left, right):
    return lax.dot_general(left, right, (((1,), (1,)), ((), ())), preferred_element_type=FULL)


def head_window(head, width):
    low = head * HEAD_DIM // 128 * 128
    high = min(-(-(head + 1) * HEAD_DIM // 128) * 128, width)
    return low, high


def head_mask(head, low, high):
    lane = lax.broadcasted_iota(jnp.int32, (1, high - low), 1) + low
    return (lane >= head * HEAD_DIM) & (lane < (head + 1) * HEAD_DIM)


def attend_forward_kernel(qkv_ref, o_ref, lse_ref, acc_ref):
    tokens, width = o_ref.shape
    rows = min(256, tokens)
    scaling = HEAD_DIM ** (-0.5)
    acc_ref[...] = jnp.zeros_like(acc_ref)
    for head in range(width // HEAD_DIM):
        low, high = head_window(head, width)
        mask = head_mask(head, low, high)
        keys = qkv_ref[1, :, low:high]
        values = jnp.where(mask, qkv_ref[2, :, low:high], jnp.zeros((), LOW))
        for start in range(0, tokens, rows):
            queries = jnp.where(mask, qkv_ref[0, start : start + rows, low:high], jnp.zeros((), LOW))
            scores = mm_cols(queries, keys) * scaling
            peak = jnp.max(scores, axis=-1, keepdims=True)
            total = jnp.sum(jnp.exp(scores - peak), axis=-1, keepdims=True)
            lse = peak + jnp.log(total)
            probability = jnp.exp(scores - lse).astype(LOW)
            acc_ref[start : start + rows, low:high] += mm(probability, values)
            lse_ref[start : start + rows, head : head + 1] = lse
    o_ref[...] = acc_ref[...].astype(LOW)


def attend_forward(qkv):
    _, tokens, width = qkv.shape
    heads = width // HEAD_DIM
    return pl.pallas_call(
        attend_forward_kernel,
        out_shape=(
            jax.ShapeDtypeStruct((tokens, width), LOW),
            jax.ShapeDtypeStruct((tokens, heads), FULL),
        ),
        in_specs=[pl.BlockSpec(memory_space=pltpu.VMEM)],
        out_specs=(pl.BlockSpec(memory_space=pltpu.VMEM),) * 2,
        scratch_shapes=[pltpu.VMEM((tokens, width), FULL)],
        compiler_params=pltpu.CompilerParams(vmem_limit_bytes=40 << 20),
        cost_estimate=pl.CostEstimate(
            flops=4 * heads * tokens * tokens * 128,
            transcendentals=2 * heads * tokens * tokens,
            bytes_accessed=8 * tokens * width,
        ),
        name="attend_forward",
    )(qkv)


def attend_backward_kernel(qkv_ref, do_ref, lse_ref, grad_ref, dq_ref, dk_ref, dv_ref):
    tokens, width = do_ref.shape
    rows = min(256, tokens)
    scaling = HEAD_DIM ** (-0.5)
    for ref in (dq_ref, dk_ref, dv_ref):
        ref[...] = jnp.zeros_like(ref)
    zero = jnp.zeros((), LOW)
    for head in range(width // HEAD_DIM):
        low, high = head_window(head, width)
        mask = head_mask(head, low, high)
        keys = qkv_ref[1, :, low:high]
        values = qkv_ref[2, :, low:high]
        keys_masked = jnp.where(mask, keys, zero)
        for start in range(0, tokens, rows):
            span = slice(start, start + rows)
            queries = jnp.where(mask, qkv_ref[0, span, low:high], zero)
            upstream = jnp.where(mask, do_ref[span, low:high], zero)
            scores = mm_cols(queries, keys) * scaling
            probability = jnp.exp(scores - lse_ref[span, head : head + 1])
            grad_prob = mm_cols(upstream, values)
            inner = jnp.sum(probability * grad_prob, axis=-1, keepdims=True)
            grad_scores = (probability * (grad_prob - inner)).astype(LOW)
            dv_ref[:, low:high] += mm_rows(probability.astype(LOW), upstream)
            dk_ref[:, low:high] += mm_rows(grad_scores, queries)
            dq_ref[span, low:high] += mm(grad_scores, keys_masked)
    grad_ref[0] = (dq_ref[...] * scaling).astype(LOW)
    grad_ref[1] = (dk_ref[...] * scaling).astype(LOW)
    grad_ref[2] = dv_ref[...].astype(LOW)


def attend_backward(qkv, upstream, lse):
    _, tokens, width = qkv.shape
    heads = width // HEAD_DIM
    return pl.pallas_call(
        attend_backward_kernel,
        out_shape=jax.ShapeDtypeStruct((3, tokens, width), LOW),
        in_specs=[pl.BlockSpec(memory_space=pltpu.VMEM)] * 3,
        out_specs=pl.BlockSpec(memory_space=pltpu.VMEM),
        scratch_shapes=[pltpu.VMEM((tokens, width), FULL)] * 3,
        compiler_params=pltpu.CompilerParams(vmem_limit_bytes=48 << 20),
        cost_estimate=pl.CostEstimate(
            flops=10 * heads * tokens * tokens * 128,
            transcendentals=heads * tokens * tokens,
            bytes_accessed=14 * tokens * width,
        ),
        name="attend_backward",
    )(qkv, upstream, lse)


def make_body(ranks, owners):
    pairs = ranks // 2

    def shift(value, step):
        return lax.ppermute(value, "seq", [(i, (i + step) % ranks) for i in range(ranks)])

    def swap(value):
        return lax.ppermute(value, "seq", [(i, i ^ 1) for i in range(ranks)])

    def pair_shift(value, step):
        return lax.ppermute(value, "seq", [(i, (i + 2 * step) % ranks) for i in range(ranks)])

    def gather_tokens(mine):
        return jnp.concatenate([mine] + [shift(mine, j) for j in range(1, ranks)], axis=0)

    def body(
        block_input,
        grad_output,
        attn_norm_gain,
        attn_norm_bias,
        qkv_weight,
        qv_bias,
        out_weight,
        out_bias,
        mlp_norm_gain,
        mlp_norm_bias,
        up_weight,
        up_bias,
        down_weight,
        down_bias,
    ):
        layers = qkv_weight.shape[0]
        tokens, width = block_input.shape[1:]
        slab = width // ranks
        part = qkv_weight.shape[1]
        hidden_part = down_weight.shape[1]
        half = -(-hidden_part // 32) * 16
        me = lax.axis_index("seq")
        side = me % 2
        pair = me // 2

        def rank_at(j):
            return (me + j) % ranks

        def by_fsdp(value):
            return lax.all_gather(value, "fsdp", axis=0, tiled=True)

        def qkv_share(layer):
            blocks = qkv_weight[layer].reshape(part, 3, width)
            return lax.dynamic_slice(blocks, (0, 0, me * slab), (part, 3, slab)).reshape(part, 3 * slab)

        def up_share(layer):
            blocks = jnp.pad(
                up_weight[layer].reshape(part, owners, hidden_part),
                ((0, 0), (0, 0), (0, 2 * half - hidden_part)),
            )
            return lax.dynamic_slice(blocks, (0, 0, side * half), (part, owners, half)).reshape(
                part, owners * half
            )

        def down_share(layer):
            padded = jnp.pad(down_weight[layer], ((0, 2 * half - hidden_part), (0, 0)))
            return lax.dynamic_slice(padded, (side * half, 0), (half, width))

        up_rows = -(-hidden_part // part)
        small = []
        for layer in range(layers):
            small += [
                attn_norm_gain[layer],
                attn_norm_bias[layer],
                qv_bias[layer, 0],
                qv_bias[layer, 1],
                out_bias[layer],
                mlp_norm_gain[layer],
                mlp_norm_bias[layer],
                down_bias[layer],
            ]
            padded = jnp.pad(up_bias[layer], (0, up_rows * part - hidden_part))
            small += [padded[i * part : (i + 1) * part] for i in range(up_rows)]
        per_layer = 8 + up_rows
        small = jnp.stack(small, axis=1)

        gathered = []
        for layer in range(layers):
            pieces = [out_weight[layer], qkv_share(layer)]
            if layer == 0:
                pieces.append(small)
            attn = by_fsdp(jnp.concatenate(pieces, axis=1))
            gathered.append((attn, by_fsdp(up_share(layer)), by_fsdp(down_share(layer))))
        small_all = gathered[0][0][:, width + 3 * slab :].T.astype(FULL)

        vectors = []
        for layer in range(layers):
            rows = small_all[layer * per_layer : (layer + 1) * per_layer]
            up_all = rows[8:].reshape(up_rows, owners, part).transpose(1, 0, 2).reshape(owners, up_rows * part)
            up_all = jnp.pad(up_all[:, :hidden_part], ((0, 0), (0, 2 * half - hidden_part)))
            up_half = lax.dynamic_slice(up_all, (0, side * half), (owners, half)).reshape(owners * half)
            q_mine = lax.dynamic_slice(rows[2], (me * slab,), (slab,))
            v_mine = lax.dynamic_slice(rows[3], (me * slab,), (slab,))
            vectors.append(
                dict(
                    gain_one=rows[0],
                    bias_one=rows[1],
                    bias_q=q_mine,
                    bias_v=v_mine,
                    bias_out=rows[4],
                    gain_two=rows[5],
                    bias_two=rows[6],
                    bias_down=rows[7],
                    bias_up=up_half,
                )
            )

        hidden = block_input[0].astype(FULL)
        all_input = gather_tokens(block_input[0])
        stored = []
        for layer in range(layers):
            v = vectors[layer]
            attn, proj_up, proj_down = gathered[layer]
            proj_out = attn[:, :width].reshape(ranks, slab, width)
            proj_qkv = attn[:, width : width + 3 * slab]
            normed_one, inverse_one = normalize(hidden)
            if layer == 0:
                normed_all, _ = normalize(all_input.astype(FULL))
                attn_in = (normed_all * v["gain_one"] + v["bias_one"]).astype(LOW)
            else:
                attn_in = gather_tokens((normed_one * v["gain_one"] + v["bias_one"]).astype(LOW))
            bias_row = jnp.concatenate([v["bias_q"], jnp.zeros((slab,), FULL), v["bias_v"]])
            projected = (mm(attn_in, proj_qkv) + bias_row).astype(LOW)
            qkv = jnp.stack([projected[:, i * slab : (i + 1) * slab] for i in range(3)])
            out_heads, lse = attend_forward(qkv)
            attended = jnp.zeros((ranks, tokens, slab), LOW)
            for j in range(ranks):
                piece = out_heads[j * tokens : (j + 1) * tokens]
                piece = shift(piece, -j) if j else piece
                attended = lax.dynamic_update_slice(attended, piece[None], (rank_at(j), 0, 0))
            after_attn = (
                hidden
                + lax.dot_general(
                    attended, proj_out, (((0, 2), (0, 1)), ((), ())), preferred_element_type=FULL
                )
                + v["bias_out"]
            )
            normed_two, inverse_two = normalize(after_attn)
            mlp_mine = (normed_two * v["gain_two"] + v["bias_two"]).astype(LOW)
            mlp_in = jnp.concatenate([mlp_mine, swap(mlp_mine)], axis=0)
            pre_act = mm(mlp_in, proj_up) + v["bias_up"]
            activated = tangent_gelu(pre_act).astype(LOW)
            mixed = mm(activated, proj_down)
            other = swap(mixed[tokens:].astype(LOW))
            hidden = after_attn + mixed[:tokens] + other.astype(FULL) + v["bias_down"]
            stored.append(
                (normed_one, inverse_one, attn_in, qkv, lse, attended, normed_two, inverse_two, mlp_in, pre_act, activated)
            )
        block_output = hidden.astype(LOW)[None]

        def scatter(value):
            return lax.psum_scatter(value.astype(LOW), "fsdp", scatter_dimension=0, tiled=True)

        def sum_ranks(value):
            blocks = value.reshape((ranks, value.shape[0] // ranks) + value.shape[1:])
            mine = lax.dynamic_index_in_dim(blocks, me, 0, keepdims=False).astype(FULL)
            for j in range(1, ranks):
                mine += shift(lax.dynamic_index_in_dim(blocks, rank_at(j), 0, keepdims=False), j).astype(FULL)
            return gather_ranks(mine.astype(LOW)).reshape(value.shape)

        def gather_ranks(mine):
            result = jnp.zeros((ranks,) + mine.shape, mine.dtype)
            for j in range(ranks):
                piece = shift(mine, j) if j else mine
                result = lax.dynamic_update_slice(result, piece[None], (rank_at(-j),) + (0,) * mine.ndim)
            return result

        def sum_pairs(value):
            count = value.shape[0] // pairs
            blocks = value.reshape((pairs, count) + value.shape[1:])
            mine = lax.dynamic_index_in_dim(blocks, pair, 0, keepdims=False).astype(FULL)
            for j in range(1, pairs):
                mine += pair_shift(
                    lax.dynamic_index_in_dim(blocks, (pair + j) % pairs, 0, keepdims=False), j
                ).astype(FULL)
            mine = mine.astype(LOW)
            result = jnp.zeros((pairs,) + mine.shape, LOW)
            for j in range(pairs):
                piece = pair_shift(mine, j) if j else mine
                result = lax.dynamic_update_slice(
                    result, piece[None], ((pair - j) % pairs,) + (0,) * mine.ndim
                )
            result = result.reshape(value.shape)
            other = swap(result)
            first = side == 0
            return jnp.where(first, result, other), jnp.where(first, other, result)

        grad_hidden = grad_output[0].astype(FULL)
        weight_grads = [None] * layers
        small_grads = [None] * layers
        for layer in reversed(range(layers)):
            v = vectors[layer]
            attn, proj_up, proj_down = gathered[layer]
            proj_out = attn[:, :width].reshape(ranks, slab, width)
            proj_qkv = attn[:, width : width + 3 * slab]
            normed_one, inverse_one, attn_in, qkv, lse, attended, normed_two, inverse_two, mlp_in, pre_act, activated = stored[layer]
            grad_mine = grad_hidden.astype(LOW)
            grad_low = jnp.concatenate([grad_mine, swap(grad_mine)], axis=0)
            g_down_bias = jnp.sum(grad_hidden, axis=0)
            grad_pre = gelu_back(pre_act, mm_cols(grad_low, proj_down))
            g_up_bias = jnp.sum(grad_pre, axis=0)
            grad_pre_low = grad_pre.astype(LOW)
            mixed = mm_cols(grad_pre_low, proj_up)
            grad_mid = mixed[:tokens] + swap(mixed[tokens:].astype(LOW)).astype(FULL)
            g_down = scatter(mm_rows(activated, grad_low))
            g_up = scatter(mm_rows(mlp_in, grad_pre_low))
            grad_norm_two, g_gain_two, g_bias_two = normalize_back(
                grad_mid, normed_two, inverse_two, v["gain_two"]
            )
            grad_after = grad_hidden + grad_norm_two
            g_out_bias = jnp.sum(grad_after, axis=0)
            after_low = grad_after.astype(LOW)
            grad_attended = lax.dot_general(
                proj_out, after_low, (((2,), (1,)), ((), ())), preferred_element_type=FULL
            )
            grad_attended = grad_attended.astype(LOW).transpose(0, 2, 1)
            grad_heads = jnp.concatenate(
                [lax.dynamic_index_in_dim(grad_attended, me, 0, keepdims=False)]
                + [
                    shift(lax.dynamic_index_in_dim(grad_attended, rank_at(j), 0, keepdims=False), j)
                    for j in range(1, ranks)
                ],
                axis=0,
            )
            g_out = scatter(
                lax.dot_general(
                    attended, after_low, (((1,), (0,)), ((), ())), preferred_element_type=FULL
                ).reshape(width, width)
            )
            grad_qkv = attend_backward(qkv, grad_heads, lse)
            grad_proj = jnp.concatenate([grad_qkv[i] for i in range(3)], axis=1)
            partial_in = mm_cols(grad_proj, proj_qkv)
            grad_in = partial_in[:tokens]
            for j in range(1, ranks):
                grad_in += shift(partial_in[j * tokens : (j + 1) * tokens].astype(LOW), -j).astype(FULL)
            g_qkv = scatter(mm_rows(attn_in, grad_proj))
            g_q_bias = jnp.sum(grad_qkv[0].astype(FULL), axis=0)
            g_v_bias = jnp.sum(grad_qkv[2].astype(FULL), axis=0)
            grad_norm_one, g_gain_one, g_bias_one = normalize_back(
                grad_in, normed_one, inverse_one, v["gain_one"]
            )
            grad_hidden = grad_after + grad_norm_one

            down_halves = sum_pairs(g_down)
            g_down = jnp.concatenate(down_halves, axis=0)[:hidden_part]
            up_halves = sum_pairs(g_up)
            g_up = jnp.concatenate(
                [u.reshape(part, owners, half) for u in up_halves], axis=2
            )[:, :, :hidden_part].reshape(part, owners * hidden_part)
            g_out = sum_ranks(g_out)
            g_qkv = gather_ranks(g_qkv).reshape(ranks, part, 3, slab).transpose(1, 2, 0, 3).reshape(part, 3 * width)
            weight_grads[layer] = tuple(g.astype(FULL) for g in (g_qkv, g_out, g_up, g_down))

            zeros = jnp.zeros((width,), FULL)
            q_row = lax.dynamic_update_slice(zeros, g_q_bias, (me * slab,))
            v_row = lax.dynamic_update_slice(zeros, g_v_bias, (me * slab,))
            up_row = lax.dynamic_update_slice(
                jnp.zeros((owners, 2 * half), FULL), g_up_bias.reshape(owners, half), (0, side * half)
            )
            rows = jnp.stack(
                [g_gain_one, g_bias_one, q_row, v_row, g_out_bias, g_gain_two, g_bias_two, g_down_bias]
            )
            rows = rows.reshape(8, owners, part).transpose(1, 0, 2).reshape(owners, 8 * part)
            small_grads[layer] = jnp.concatenate([rows, up_row], axis=1)

        small_sum = jnp.concatenate(small_grads, axis=1)
        small_sum = jnp.pad(small_sum, ((0, 0), (0, -small_sum.shape[1] % 128)))
        small_sum = jnp.sum(
            lax.all_to_all(small_sum, "fsdp", split_axis=0, concat_axis=0, tiled=True), axis=0
        )
        total = small_sum
        for j in range(1, ranks):
            total = total + shift(small_sum, j)
        each = 8 * part + 2 * half
        small_out = [[] for _ in range(9)]
        for layer in range(layers):
            mine = total[layer * each : (layer + 1) * each]
            rows = mine[: 8 * part].reshape(8, part)
            for i in range(8):
                small_out[i].append(rows[i])
            small_out[8].append(mine[8 * part : 8 * part + hidden_part])
        s = [jnp.stack(entry) for entry in small_out]
        w = [jnp.stack([weight_grads[layer][i] for layer in range(layers)]) for i in range(4)]
        return (
            block_output,
            grad_hidden[None],
            s[0],
            s[1],
            w[0],
            jnp.stack([s[2], s[3]], axis=1),
            w[1],
            s[4],
            s[5],
            s[6],
            w[2],
            s[8],
            w[3],
            s[7],
        )

    return body


def solution(mesh):
    row, cols, deep = P(None, "fsdp"), P("fsdp", "seq", None), P(None, "fsdp", None)
    last = P(None, None, "fsdp")
    return jax.shard_map(
        make_body(mesh.shape["seq"], mesh.shape["fsdp"]),
        mesh=mesh,
        in_specs=(cols, cols, row, row, deep, last, deep, row, row, row, deep, row, deep, row),
        out_specs=(cols, cols, row, row, deep, last, deep, row, row, row, deep, row, deep, row),
        check_vma=False,
    )
```

```python
import functools
import math

import jax
import jax.numpy as jnp
from jax import lax
from jax.experimental import pallas as pl
from jax.experimental.pallas import tpu as pltpu
from jax.sharding import PartitionSpec as P

HEAD_DIM = 72
EPSILON = 1e-06
LOW = jnp.bfloat16
FULL = jnp.float32


def normalize(hidden):
    center = hidden - jnp.mean(hidden, axis=-1, keepdims=True)
    variance = jnp.mean(center * center, axis=-1, keepdims=True)
    inverse_std = lax.rsqrt(variance + EPSILON)
    return center * inverse_std, inverse_std


def normalize_back(upstream, normed, inverse_std, gain):
    scaled = upstream * gain
    grad_hidden = inverse_std * (
        scaled
        - jnp.mean(scaled, axis=-1, keepdims=True)
        - normed * jnp.mean(scaled * normed, axis=-1, keepdims=True)
    )
    return (
        grad_hidden,
        jnp.sum(upstream * normed, axis=0, keepdims=True),
        jnp.sum(upstream, axis=0, keepdims=True),
    )


def tangent_gelu(values):
    return jax.nn.gelu(values, approximate=True)


def gelu_back(values, upstream):
    return jax.vjp(tangent_gelu, values)[1](upstream)[0]


def mm(left, right):
    return jnp.dot(left, right, preferred_element_type=FULL)


def mm_rows(left, right):
    return lax.dot_general(left, right, (((0,), (0,)), ((), ())), preferred_element_type=FULL)


def mm_cols(left, right):
    return lax.dot_general(left, right, (((1,), (1,)), ((), ())), preferred_element_type=FULL)


def head_window(head, width):
    low = head * HEAD_DIM // 128 * 128
    high = min(-(-(head + 1) * HEAD_DIM // 128) * 128, width)
    return low, high


def head_mask(head, low, high):
    lane = lax.broadcasted_iota(jnp.int32, (1, high - low), 1) + low
    return (lane >= head * HEAD_DIM) & (lane < (head + 1) * HEAD_DIM)


def attend_forward_kernel(qkv_ref, o_ref, lse_ref, acc_ref):
    tokens, width = o_ref.shape
    rows = min(256, tokens)
    scaling = HEAD_DIM ** (-0.5)
    acc_ref[...] = jnp.zeros_like(acc_ref)
    for head in range(width // HEAD_DIM):
        low, high = head_window(head, width)
        mask = head_mask(head, low, high)
        keys = qkv_ref[1, :, low:high]
        values = jnp.where(mask, qkv_ref[2, :, low:high], jnp.zeros((), LOW))
        for start in range(0, tokens, rows):
            queries = jnp.where(mask, qkv_ref[0, start : start + rows, low:high], jnp.zeros((), LOW))
            scores = mm_cols(queries, keys) * scaling
            peak = jnp.max(scores, axis=-1, keepdims=True)
            total = jnp.sum(jnp.exp(scores - peak), axis=-1, keepdims=True)
            lse = peak + jnp.log(total)
            probability = jnp.exp(scores - lse).astype(LOW)
            acc_ref[start : start + rows, low:high] += mm(probability, values)
            lse_ref[start : start + rows, head : head + 1] = lse
    o_ref[...] = acc_ref[...].astype(LOW)


def attend_forward(qkv):
    _, tokens, width = qkv.shape
    heads = width // HEAD_DIM
    return pl.pallas_call(
        attend_forward_kernel,
        out_shape=(
            jax.ShapeDtypeStruct((tokens, width), LOW),
            jax.ShapeDtypeStruct((tokens, heads), FULL),
        ),
        in_specs=[pl.BlockSpec(memory_space=pltpu.VMEM)],
        out_specs=(pl.BlockSpec(memory_space=pltpu.VMEM),) * 2,
        scratch_shapes=[pltpu.VMEM((tokens, width), FULL)],
        compiler_params=pltpu.CompilerParams(vmem_limit_bytes=40 << 20),
        cost_estimate=pl.CostEstimate(
            flops=4 * heads * tokens * tokens * 128,
            transcendentals=2 * heads * tokens * tokens,
            bytes_accessed=8 * tokens * width,
        ),
        name="attend_forward",
    )(qkv)


def attend_backward_kernel(
    qkv_ref, do_ref, lse_ref, proj_ref, grad_ref, leave_ref, q_bias_ref, v_bias_ref, dq_ref, dk_ref, dv_ref
):
    tokens, width = do_ref.shape
    rows = min(256, tokens)
    scaling = HEAD_DIM ** (-0.5)
    for ref in (dq_ref, dk_ref, dv_ref):
        ref[...] = jnp.zeros_like(ref)
    zero = jnp.zeros((), LOW)
    for head in range(width // HEAD_DIM):
        low, high = head_window(head, width)
        mask = head_mask(head, low, high)
        keys = qkv_ref[1, :, low:high]
        values = qkv_ref[2, :, low:high]
        keys_masked = jnp.where(mask, keys, zero)
        for start in range(0, tokens, rows):
            span = slice(start, start + rows)
            queries = jnp.where(mask, qkv_ref[0, span, low:high], zero)
            upstream = jnp.where(mask, do_ref[span, low:high], zero)
            scores = mm_cols(queries, keys) * scaling
            probability = jnp.exp(scores - lse_ref[span, head : head + 1])
            grad_prob = mm_cols(upstream, values)
            inner = jnp.sum(probability * grad_prob, axis=-1, keepdims=True)
            grad_scores = (probability * (grad_prob - inner)).astype(LOW)
            dv_ref[:, low:high] += mm_rows(probability.astype(LOW), upstream)
            dk_ref[:, low:high] += mm_rows(grad_scores, queries)
            dq_ref[span, low:high] += mm(grad_scores, keys_masked)
    dq = (dq_ref[...] * scaling).astype(LOW)
    dv = dv_ref[...].astype(LOW)
    grad_ref[:, :width] = dq
    grad_ref[:, width : 2 * width] = (dk_ref[...] * scaling).astype(LOW)
    grad_ref[:, 2 * width :] = dv
    q_bias_ref[...] = jnp.sum(dq.astype(FULL), axis=0, keepdims=True)
    v_bias_ref[...] = jnp.sum(dv.astype(FULL), axis=0, keepdims=True)
    ranks, block, _ = leave_ref.shape
    for rank in range(ranks):
        leave_ref[rank] = mm_cols(grad_ref[rank * block : (rank + 1) * block], proj_ref[...]).astype(LOW)


def attend_backward(qkv, upstream, lse, proj, ranks):
    _, tokens, width = qkv.shape
    heads = width // HEAD_DIM
    model = proj.shape[0]
    return pl.pallas_call(
        attend_backward_kernel,
        out_shape=(
            jax.ShapeDtypeStruct((tokens, 3 * width), LOW),
            jax.ShapeDtypeStruct((ranks, tokens // ranks, model), LOW),
            jax.ShapeDtypeStruct((1, width), FULL),
            jax.ShapeDtypeStruct((1, width), FULL),
        ),
        in_specs=[pl.BlockSpec(memory_space=pltpu.VMEM)] * 4,
        out_specs=(pl.BlockSpec(memory_space=pltpu.VMEM),) * 4,
        scratch_shapes=[pltpu.VMEM((tokens, width), FULL)] * 3,
        compiler_params=pltpu.CompilerParams(vmem_limit_bytes=48 << 20),
        cost_estimate=pl.CostEstimate(flops=0, transcendentals=0, bytes_accessed=24 << 20),
        name="attend_backward",
    )(qkv, upstream, lse, proj)


def attn_share_kernel(me_ref, out_w_ref, qkv_ref, *refs, layers, with_small, ranks):
    out_ref = refs[-1]
    part, width = out_w_ref.shape
    slab = width // ranks
    out_ref[:part, :width] = out_w_ref[...]
    for rank in range(ranks):

        @pl.when(me_ref[0] == rank)
        def _():
            for i in range(3):
                source = (i * ranks + rank) * slab
                target = width + i * slab
                out_ref[:part, target : target + slab] = qkv_ref[:, source : source + slab]

    if with_small:
        out_ref[part:, :] = jnp.zeros((out_ref.shape[0] - part, out_ref.shape[1]), LOW)
        for layer in range(layers):
            target = 0
            for ref in refs[:-1]:
                count = ref.shape[-1]
                for row in range(ref.shape[0] // layers):
                    source = layer * (ref.shape[0] // layers) + row
                    out_ref[part + layer : part + layer + 1, target : target + count] = ref[source : source + 1, :]
                    target += count


def attn_share(me, out_w, qkv_w, small, layers, ranks):
    part, width = out_w.shape
    rows = part + 8 * (len(small) > 0)
    return pl.pallas_call(
        functools.partial(attn_share_kernel, layers=layers, with_small=len(small) > 0, ranks=ranks),
        out_shape=jax.ShapeDtypeStruct((rows, width + 3 * width // ranks), LOW),
        in_specs=[pl.BlockSpec(memory_space=pltpu.SMEM)]
        + [pl.BlockSpec(memory_space=pltpu.VMEM)] * (2 + len(small)),
        out_specs=pl.BlockSpec(memory_space=pltpu.VMEM),
        compiler_params=pltpu.CompilerParams(vmem_limit_bytes=24 << 20),
        cost_estimate=pl.CostEstimate(flops=1, transcendentals=0, bytes_accessed=1),
        name="attn_share",
    )(me.reshape(1), out_w, qkv_w, *small)


def share_kernel(side_ref, up_ref, down_ref, out_ref, *, owners, layer, half):
    part = up_ref.shape[0]
    hidden_part, _, width = down_ref.shape
    flank = owners // 2 * half
    out_ref[...] = jnp.zeros_like(out_ref)
    for side in range(2):

        @pl.when(side_ref[0] == side)
        def _():
            first = side * half
            count = min(half, hidden_part - first)
            out_ref[:count, :width] = down_ref[first : first + count, layer, :]
            for owner in range(owners):
                source = owner * hidden_part + first
                target = width + owner * half - (owner >= owners // 2) * flank
                row = (owner >= owners // 2) * part
                out_ref[row : row + part, target : target + count] = up_ref[:, source : source + count]


def feed_share(side, up, down, layer, owners, half):
    part, (hidden_part, _, width) = up.shape[0], down.shape
    lanes = width + -(-owners // 2 * half // 128) * 128
    return pl.pallas_call(
        functools.partial(share_kernel, owners=owners, layer=layer, half=half),
        out_shape=jax.ShapeDtypeStruct((max(2 * part, half), lanes), LOW),
        in_specs=[pl.BlockSpec(memory_space=pltpu.SMEM)] + [pl.BlockSpec(memory_space=pltpu.VMEM)] * 2,
        out_specs=pl.BlockSpec(memory_space=pltpu.VMEM),
        compiler_params=pltpu.CompilerParams(vmem_limit_bytes=24 << 20),
        cost_estimate=pl.CostEstimate(flops=1, transcendentals=0, bytes_accessed=1),
        name="feed_share",
    )(side.reshape(1), up, down)


def local_call(kernel, name, out_shape, *operands, scalars=(), scratch=()):
    moved = sum(math.prod(a.shape) * a.dtype.itemsize for a in (*operands, *jax.tree.leaves(out_shape)))
    return pl.pallas_call(
        kernel,
        out_shape=out_shape,
        in_specs=[pl.BlockSpec(memory_space=pltpu.SMEM)] * len(scalars)
        + [pl.BlockSpec(memory_space=pltpu.VMEM)] * len(operands),
        out_specs=jax.tree.map(lambda _: pl.BlockSpec(memory_space=pltpu.VMEM), out_shape),
        scratch_shapes=list(scratch),
        compiler_params=pltpu.CompilerParams(vmem_limit_bytes=48 << 20),
        cost_estimate=pl.CostEstimate(flops=20000000000, transcendentals=0, bytes_accessed=moved),
        name=name,
    )(*[s.reshape(1) for s in scalars], *operands)


def grad_kernel(*refs, owners, columns, total, split):
    core_ref, refs = (refs[0], refs[1:]) if split else (None, refs)
    count = len(columns)
    lefts, rights = refs[:count], refs[count : 2 * count]
    outs, flips = refs[2 * count : len(refs) - count], refs[len(refs) - count :]
    rows = lefts[0].shape[1] // owners
    for target, width in columns:
        gap = slice(target + width, min([t for t, _ in columns if t > target], default=total))
        if gap.stop > gap.start:
            for out in outs:
                out[..., gap] = jnp.zeros(out.shape[:-1] + (gap.stop - gap.start,), LOW)
    for left, right, flip, (target, width) in zip(lefts, rights, flips, columns, strict=True):
        flip[...] = left[...].T
        for start in range(0, width, 256):
            size = min(256, width - start)
            value = mm(flip[...], right[:, start : start + size]).astype(LOW)
            if not split:
                outs[0][:, target + start : target + start + size] = value
                continue
            for core in range(2):

                @pl.when(core_ref[0] == core)
                def _():
                    for owner in range(owners):
                        out = outs[(owner % 2 != core) * 1]
                        out[owner // 2, :, target + start : target + start + size] = value[
                            owner * rows : (owner + 1) * rows
                        ]


def weight_grad(pieces, owners, total, core=None):
    lefts, rights = [p[0] for p in pieces], [p[1] for p in pieces]
    rows = lefts[0].shape[1]
    split = core is not None
    shape = (owners // 2, rows // owners, total) if split else (rows, total)
    out = jax.ShapeDtypeStruct(shape, LOW)
    return local_call(
        functools.partial(
            grad_kernel,
            owners=owners,
            columns=[(p[2], p[1].shape[1]) for p in pieces],
            total=total,
            split=split,
        ),
        "weight_grad",
        (out, out) if split else out,
        *lefts,
        *rights,
        scalars=(core,) if split else (),
        scratch=[pltpu.VMEM((left.shape[1], left.shape[0]), LOW) for left in lefts],
    )


def feed_backward_kernel(
    mine_ref, other_ref, pre_ref, up_ref, down_ref, low_ref, grad_ref, keep_ref, leave_ref, bias_ref, acc_ref
):
    tokens = mine_ref.shape[0]
    low_ref[:tokens] = mine_ref[...]
    low_ref[tokens:] = other_ref[...]
    acc_ref[...] = jnp.zeros_like(acc_ref)
    scale = (2 / math.pi) ** 0.5
    units = pre_ref.shape[1]
    for start in range(0, units, 512):
        span = slice(start, min(start + 512, units))
        pre = pre_ref[:, span]
        square = pre * pre
        bend = jnp.tanh(scale * (pre + 0.044715 * pre * square))
        slope = 0.5 * (1 + bend) + 0.5 * pre * (1 - bend * bend) * (scale * (1 + 3 * 0.044715 * square))
        grad = mm_cols(low_ref[...], down_ref[span, :]) * slope
        bias_ref[:, span] = jnp.sum(grad, axis=0, keepdims=True)
        grad = grad.astype(LOW)
        grad_ref[:, span] = grad
        acc_ref[...] += mm_cols(grad, up_ref[:, span])
    keep_ref[...] = acc_ref[:tokens]
    leave_ref[...] = acc_ref[tokens:].astype(LOW)


def feed_backward(mine, other, pre_act, up, down):
    tokens, width = mine.shape
    units = pre_act.shape[1]
    return local_call(
        feed_backward_kernel,
        "feed_backward",
        (
            jax.ShapeDtypeStruct((2 * tokens, width), LOW),
            jax.ShapeDtypeStruct((2 * tokens, units), LOW),
            jax.ShapeDtypeStruct((tokens, width), FULL),
            jax.ShapeDtypeStruct((tokens, width), LOW),
            jax.ShapeDtypeStruct((1, units), FULL),
        ),
        mine,
        other,
        pre_act,
        up,
        down,
        scratch=[pltpu.VMEM((2 * tokens, width), FULL)],
    )


def mid_backward_kernel(
    side_ref, keep_ref, got_ref, normed_ref, inverse_ref, gain_ref, grad_ref, proj_ref, *outs
):
    after_ref, send_ref, mine_ref, other_ref, g_gain_ref, g_bias_ref, g_out_ref, g_down_ref = outs
    upstream = keep_ref[...] + got_ref[...].astype(FULL)
    grad = grad_ref[...]
    back, g_gain, g_bias = normalize_back(upstream, normed_ref[...], inverse_ref[...], gain_ref[...])
    after = grad + back
    after_ref[...] = after
    g_gain_ref[...] = g_gain
    g_bias_ref[...] = g_bias
    g_out_ref[...] = jnp.sum(after, axis=0, keepdims=True)
    g_down_ref[...] = jnp.sum(grad, axis=0, keepdims=True)
    low = after.astype(LOW)
    flank = mine_ref.shape[1]
    for side in range(2):

        @pl.when(side_ref[0] == side)
        def _():
            mine_ref[...] = low[:, side * flank : (side + 1) * flank]
            other_ref[...] = low[:, (1 - side) * flank : (2 - side) * flank]

    ranks, _, slab = send_ref.shape
    for rank in range(ranks):
        send_ref[rank] = mm_cols(low, proj_ref[rank * slab : (rank + 1) * slab, :]).astype(LOW)


def mid_backward(side, keep, got, normed, inverse, gain, grad, proj, ranks):
    tokens, width = keep.shape
    row = jax.ShapeDtypeStruct((1, width), FULL)
    half = jax.ShapeDtypeStruct((tokens, width // 2), LOW)
    return local_call(
        mid_backward_kernel,
        "mid_backward",
        (
            jax.ShapeDtypeStruct((tokens, width), FULL),
            jax.ShapeDtypeStruct((ranks, tokens, width // ranks), LOW),
            half,
            half,
            row,
            row,
            row,
            row,
        ),
        keep,
        got,
        normed,
        inverse,
        gain,
        grad,
        proj,
        scalars=(side,),
    )


def end_backward_kernel(got_ref, normed_ref, inverse_ref, gain_ref, after_ref, out_ref, low_ref, g_gain_ref, g_bias_ref):
    upstream = got_ref[0].astype(FULL)
    for rank in range(1, got_ref.shape[0]):
        upstream += got_ref[rank].astype(FULL)
    back, g_gain, g_bias = normalize_back(upstream, normed_ref[...], inverse_ref[...], gain_ref[...])
    total = after_ref[...] + back
    out_ref[...] = total
    low_ref[...] = total.astype(LOW)
    g_gain_ref[...] = g_gain
    g_bias_ref[...] = g_bias


def end_backward(got, normed, inverse, gain, after):
    tokens, width = after.shape
    row = jax.ShapeDtypeStruct((1, width), FULL)
    return local_call(
        end_backward_kernel,
        "end_backward",
        (
            jax.ShapeDtypeStruct((tokens, width), FULL),
            jax.ShapeDtypeStruct((tokens, width), LOW),
            row,
            row,
        ),
        got,
        normed,
        inverse,
        gain,
        after,
    )


def meet_kernel(chip_ref, keep_ref, got_ref, *outs):
    step = pl.program_id(0)
    for j, out in enumerate(outs):

        @pl.when(step == j)
        def _():
            out[...] = (keep_ref[0].astype(FULL) + got_ref[0].astype(FULL)).astype(LOW)


def meet_cores(chip, keep, got):
    chips, rows, columns = keep.shape
    block = pl.BlockSpec((1, rows, columns), lambda j, chip_ref: (chip_ref[0] ^ j, 0, 0))
    return pl.pallas_call(
        meet_kernel,
        grid_spec=pltpu.PrefetchScalarGridSpec(
            num_scalar_prefetch=1,
            grid=(chips,),
            in_specs=[block, block],
            out_specs=[pl.BlockSpec((rows, columns), lambda j, chip_ref: (0, 0))] * chips,
        ),
        out_shape=[jax.ShapeDtypeStruct((rows, columns), LOW)] * chips,
        compiler_params=pltpu.CompilerParams(vmem_limit_bytes=24 << 20),
        cost_estimate=pl.CostEstimate(flops=0, transcendentals=0, bytes_accessed=6 * chips * rows * columns),
        name="meet_cores",
    )(chip.reshape(1), keep, got)


def add_kernel(*refs):
    total = refs[0][...].astype(FULL)
    for ref in refs[1:-1]:
        total += ref[...].astype(FULL)
    refs[-1][...] = total.astype(LOW)


def add_all(*values):
    return local_call(add_kernel, "add_all", jax.ShapeDtypeStruct(values[0].shape, LOW), *values)


def up_kernel(side_ref, own_ref, across_ref, *refs, owners, half):
    out_ref = refs[-1]
    hidden_part = out_ref.shape[2] // owners
    for mine in range(2):

        @pl.when(side_ref[0] == mine)
        def _():
            for side in range(2):
                ref = own_ref if side == mine else across_ref
                first = side * half
                count = min(half, hidden_part - first)
                for owner in range(owners):
                    target = owner * hidden_part + first
                    source = owner * half
                    out_ref[0, :, target : target + count] = ref[:, source : source + count].astype(FULL)


def mixed_kernel(me_ref, sums_ref, others_ref, *refs, ranks, layers_seen, offset):
    shares, (qkv_out, out_out) = refs[:ranks], refs[-2:]
    width = out_out.shape[2]
    slab, flank, pairs = width // ranks, width // 2, ranks // 2
    for me in range(ranks):

        @pl.when(me_ref[0] == me)
        def _():
            side, pair = me % 2, me // 2
            for j in range(pairs):
                for flip in range(2):
                    rank = (pair - j) % pairs * 2 + (side ^ flip)
                    ref = shares[2 * j + flip]
                    for i in range(3):
                        target = (i * ranks + rank) * slab
                        qkv_out[0, :, target : target + slab] = ref[:, i * slab : (i + 1) * slab].astype(FULL)
            for flip, ref in enumerate((sums_ref, others_ref)):
                target = (side ^ flip) * flank
                out_out[0, :, target : target + flank] = ref[:, offset : offset + flank].astype(FULL)


def write_layer(kernel, name, layer, layers, shapes, earlier, scalar, *values):
    return pl.pallas_call(
        kernel,
        grid=(1,),
        out_shape=tuple(jax.ShapeDtypeStruct((layers,) + s, FULL) for s in shapes),
        in_specs=[pl.BlockSpec(memory_space=pltpu.SMEM)]
        + [pl.BlockSpec(v.shape, lambda i: (0, 0)) for v in values]
        + [pl.BlockSpec(memory_space=pl.ANY)] * len(earlier),
        out_specs=tuple(pl.BlockSpec((1,) + s, lambda i: (layer, 0, 0)) for s in shapes),
        input_output_aliases={1 + len(values) + i: i for i in range(len(earlier))},
        compiler_params=pltpu.CompilerParams(vmem_limit_bytes=40 << 20),
        cost_estimate=pl.CostEstimate(flops=0, transcendentals=0, bytes_accessed=8 << 20),
        name=name,
    )(scalar.reshape(1), *values, *earlier)


def down_kernel(side_ref, *refs):
    out_ref = refs[-1]
    half = refs[0].shape[0]
    hidden_part = out_ref.shape[0]
    for mine in range(2):

        @pl.when(side_ref[0] == mine)
        def _():
            for layer in range(len(refs) // 2):
                for side in range(2):
                    ref = refs[2 * layer + (side != mine)]
                    first = side * half
                    count = min(half, hidden_part - first)
                    out_ref[first : first + count, layer, :] = ref[:count].astype(FULL)


def pack_kernel(side_ref, *refs, owners, layers, half):
    out_ref = refs[-1]
    each = len(refs) // layers
    out_ref[...] = jnp.zeros_like(out_ref)
    target = 0
    for layer in range(layers):
        rows = refs[layer * each : (layer + 1) * each]
        for ref in rows[:-1]:
            part = ref.shape[1] // owners
            for owner in range(owners):
                out_ref[owner : owner + 1, target : target + part] = ref[:, owner * part : (owner + 1) * part]
            target += part
        for side in range(2):

            @pl.when(side_ref[0] == side)
            def _():
                for owner in range(owners):
                    first = target + side * half
                    out_ref[owner : owner + 1, first : first + half] = rows[-1][
                        :, owner * half : (owner + 1) * half
                    ]

        target += 2 * half


def unpack_kernel(first_ref, second_ref, *outs, layers, half):
    values = first_ref[...] + second_ref[...]
    part = outs[0].shape[1]
    target = 0
    for layer in range(layers):
        for out in outs[:-1]:
            out[layer : layer + 1, :] = values[:, target : target + part]
            target += part
        out = outs[-1]
        out[layer : layer + 1, :] = values[:, target : target + out.shape[1]]
        target += 2 * half


class Order:
    def __init__(self):
        self.last = ()

    def enter(self, *values):
        if not self.last:
            return values
        return lax.optimization_barrier(tuple(values) + self.last)[: len(values)]

    def leave(self, *values):
        self.last = tuple(values)


class Chain:
    def __init__(self, steps):
        self.steps = steps
        self.result = None
        self.step()

    def step(self):
        try:
            next(self.steps)
        except StopIteration as stop:
            self.result = stop.value


def make_body(ranks, owners):
    pairs, chips = ranks // 2, owners // 2

    def shift(value, step):
        return lax.ppermute(value, "seq", [(i, (i + step) % ranks) for i in range(ranks)])

    def swap(value):
        return lax.ppermute(value, "seq", [(i, i ^ 1) for i in range(ranks)])

    def pair_shift(value, step):
        return lax.ppermute(value, "seq", [(i, (i + 2 * step) % ranks) for i in range(ranks)])

    def owner_xor(value, bits):
        return lax.ppermute(value, "fsdp", [(i, i ^ bits) for i in range(owners)])

    def exchange(blocks):
        return lax.all_to_all(blocks, "seq", split_axis=0, concat_axis=0, tiled=True)

    def body(
        block_input,
        grad_output,
        attn_norm_gain,
        attn_norm_bias,
        qkv_weight,
        qv_bias,
        out_weight,
        out_bias,
        mlp_norm_gain,
        mlp_norm_bias,
        up_weight,
        up_bias,
        down_weight,
        down_bias,
    ):
        layers = qkv_weight.shape[0]
        tokens, width = block_input.shape[1:]
        slab, flank = width // ranks, width // 2
        part = qkv_weight.shape[1]
        hidden_part = down_weight.shape[1]
        half = -(-hidden_part // 32) * 16
        me = lax.axis_index("seq")
        owner = lax.axis_index("fsdp")
        core, chip = owner % 2, owner // 2
        side, pair = me % 2, me // 2

        def at(value, index, axis=0):
            return lax.dynamic_index_in_dim(value, index, axis, keepdims=False)

        def put(value, block, *index):
            return lax.dynamic_update_slice(
                value, block.reshape((1,) * len(index) + block.shape), index + (0,) * block.ndim
            )

        def rank_at(j):
            return (me + j) % ranks

        order = Order()

        def owner_steps(keep, send):
            got = owner_xor(send, 1)
            yield
            (got,) = order.enter(got)
            mine, *sends = meet_cores(chip, keep, got)
            order.leave(*sends)
            got = [owner_xor(send, 2 * j) for j, send in enumerate(sends, 1)]
            yield
            return add_all(mine, *order.enter(*got))

        def queue_steps(value):
            value = lax.psum_scatter(value, "fsdp", scatter_dimension=0, tiled=True)
            yield
            return order.enter(value)[0]

        def pair_steps(value):
            order.leave(value)
            got = [pair_shift(value, j) for j in range(1, pairs)]
            yield
            own = add_all(value, *order.enter(*got))
            order.leave(own)
            across = swap(own)
            yield
            return own, order.enter(across)[0]

        def mixed_steps(value):
            order.leave(value)
            share = value[:, : 3 * slab]
            got = [pair_shift(value, j) for j in range(1, pairs)]
            across = [swap(share)]
            yield
            got = order.enter(*got)
            total = add_all(*[v[:, offset:] for v in (value, *got)])
            sends = [g[:, : 3 * slab] for g in got]
            sends[0] = jnp.concatenate([got[0][:, :offset], total], axis=1)
            order.leave(*sends)
            across += [swap(send) for send in sends]
            yield
            across = list(order.enter(*across))
            shares = [share, across[0]]
            for piece, flipped in zip(got, across[1:], strict=True):
                shares += [piece, flipped]
            return sends[0], across[1], *shares

        def written(steps, stage, write):
            value = yield from steps
            value = yield from stage(value)
            value = write(*value)
            order.leave(*value)
            return value

        columns = width + 3 * slab
        offset = -(-3 * slab // 128) * 128

        def gather_tokens(mine):
            return [mine] + [shift(mine, j) for j in range(1, ranks)]

        def in_order(blocks):
            result = jnp.zeros((ranks,) + blocks[0].shape, LOW)
            for j, block in enumerate(blocks):
                result = put(result, block, rank_at(-j))
            return result.reshape(ranks * tokens, width)

        all_input = gather_tokens(block_input[0])
        small = (
            attn_norm_gain,
            attn_norm_bias,
            qv_bias.reshape(2 * layers, part),
            out_bias,
            mlp_norm_gain,
            mlp_norm_bias,
            down_bias,
            up_bias,
        )
        down_turned = down_weight.transpose(1, 0, 2)
        attn_shares, feed_shares = [], []
        for layer in range(layers):
            share = attn_share(
                me, out_weight[layer], *order.enter(qkv_weight[layer]), small if layer == 0 else (), layers, ranks
            )
            order.leave(share)
            attn_shares.append(lax.all_gather(share, "fsdp", axis=0))
            share = feed_share(side, *order.enter(up_weight[layer]), down_turned, layer, owners, half)
            order.leave(share)
            feed_shares.append(lax.all_gather(share, "fsdp", axis=0))
        small_all, *all_input = order.enter(attn_shares[0][:, part:], *all_input)
        rows_all = small_all[:, :layers, : 8 * part].reshape(owners, layers, 8, part)
        rows_all = rows_all.transpose(1, 2, 0, 3).reshape(layers, 8, width).astype(FULL)
        up_all = small_all[:, :layers, 8 * part : 8 * part + hidden_part].astype(FULL)
        up_all = jnp.pad(up_all, ((0, 0), (0, 0), (0, 2 * half - hidden_part)))

        vectors = []
        for layer in range(layers):
            rows = rows_all[layer]
            vectors.append(
                dict(
                    gain_one=rows[0],
                    bias_one=rows[1],
                    bias_q=lax.dynamic_slice(rows[2], (me * slab,), (slab,)),
                    bias_v=lax.dynamic_slice(rows[3], (me * slab,), (slab,)),
                    bias_out=rows[4],
                    gain_two=rows[5],
                    bias_two=rows[6],
                    bias_down=rows[7],
                    bias_up=lax.dynamic_slice(
                        up_all[:, layer], (0, side * half), (owners, half)
                    ).reshape(owners * half),
                )
            )

        hidden = block_input[0].astype(FULL)
        stored = []
        for layer in range(layers):
            v = vectors[layer]
            normed_one, inverse_one = normalize(hidden)
            if layer == 0:
                normed_all, _ = normalize(in_order(all_input).astype(FULL))
                attn_in = (normed_all * v["gain_one"] + v["bias_one"]).astype(LOW)
            else:
                attn_mine = (normed_one * v["gain_one"] + v["bias_one"]).astype(LOW)
                order.leave(attn_mine)
                attn_in = in_order(order.enter(*gather_tokens(attn_mine)))
            attn = order.enter(attn_shares[layer])[0][:, :part].reshape(width, columns)
            proj_out, proj_qkv = lax.optimization_barrier((attn[:, :width], attn[:, width:]))
            bias_row = jnp.concatenate([v["bias_q"], jnp.zeros((slab,), FULL), v["bias_v"]])
            projected = (mm(attn_in, proj_qkv) + bias_row).astype(LOW)
            qkv = jnp.stack([projected[:, i * slab : (i + 1) * slab] for i in range(3)])
            out_heads, lse = attend_forward(qkv)
            out_heads = out_heads.reshape(ranks, tokens, slab)
            order.leave(out_heads)
            (attended,) = order.enter(exchange(out_heads))
            after_attn = (
                hidden
                + lax.dot_general(
                    attended,
                    proj_out.reshape(ranks, slab, width),
                    (((0, 2), (0, 1)), ((), ())),
                    preferred_element_type=FULL,
                )
                + v["bias_out"]
            )
            normed_two, inverse_two = normalize(after_attn)
            mlp_mine = (normed_two * v["gain_two"] + v["bias_two"]).astype(LOW)
            order.leave(mlp_mine)
            attended_other = swap(order.enter(attended)[0])
            mlp_other, attended_other, feed = order.enter(swap(mlp_mine), attended_other, feed_shares[layer])
            attended_pair = jnp.concatenate([attended, attended_other], axis=1)
            proj_up = jnp.concatenate(
                [feed[:, i * part : (i + 1) * part, width : width + owners // 2 * half] for i in range(2)], axis=2
            ).reshape(width, owners * half)
            proj_down = feed[:, :half, :width].reshape(owners * half, width)
            proj_up, proj_down = lax.optimization_barrier((proj_up, proj_down))
            mlp_in = jnp.concatenate([mlp_mine, mlp_other], axis=0)
            pre_act = mm(mlp_in, proj_up) + v["bias_up"]
            activated = tangent_gelu(pre_act).astype(LOW)
            mixed = mm(activated, proj_down)
            leaving = mixed[tokens:].astype(LOW)
            order.leave(leaving)
            other = swap(leaving)
            if layer < layers - 1:
                (other,) = order.enter(other)
            hidden = after_attn + mixed[:tokens] + other.astype(FULL) + v["bias_down"]
            stored.append(
                (
                    (proj_qkv, proj_out, proj_up, proj_down),
                    (normed_one, inverse_one, attn_in, qkv, lse, attended_pair),
                    (normed_two, inverse_two, mlp_in, pre_act, activated),
                )
            )
        block_output = hidden.astype(LOW)[None]

        def writer(key, kernel, layer, scalar, *shapes):
            def write(*values):
                outs[key] = write_layer(
                    kernel, "write_" + key, layer, layers, shapes, outs[key], scalar, *values
                )
                return outs[key]

            return write

        def held(*values):
            return values

        def sum_rows(value):
            return jnp.sum(value, axis=0, keepdims=True)

        grad_hidden, grad_mine = grad_output[0].astype(FULL), grad_output[0]
        small_grads = [None] * layers
        downs = [None] * layers
        outs = dict(up=(), mixed=())
        before = None
        for layer in reversed(range(layers)):
            v = vectors[layer]
            proj_qkv, proj_out, proj_up, proj_down = stored[layer][0]
            normed_one, inverse_one, attn_in, qkv, lse, attended_pair = stored[layer][1]
            normed_two, inverse_two, mlp_in, pre_act, activated = stored[layer][2]
            grad_other = swap(grad_mine)
            if before:
                before["down"].step()
            (grad_other,) = order.enter(grad_other)
            grad_low, grad_pre_low, mixed, leaving, g_up_bias = feed_backward(
                grad_mine, grad_other, pre_act, proj_up, proj_down
            )
            order.leave(leaving)
            other = swap(leaving)
            g_down = weight_grad([(activated, order.enter(grad_low)[0], 0)], owners, width)
            order.leave(g_down)
            down_chain = Chain(written(queue_steps(g_down), pair_steps, held))
            keep, send = weight_grad([(mlp_in, order.enter(grad_pre_low)[0], 0)], owners, half * owners, core)
            order.leave(send)
            up_chain = Chain(
                written(
                    owner_steps(keep, send),
                    pair_steps,
                    writer(
                        "up",
                        functools.partial(up_kernel, owners=owners, half=half),
                        layer,
                        side,
                        (part, owners * hidden_part),
                    ),
                )
            )
            (other,) = order.enter(other)
            order.leave(other)
            if before:
                before["up"].step()
            grad_after, sends, after_mine, after_send, g_gain_two, g_bias_two, g_out_bias, g_down_bias = mid_backward(
                side,
                mixed,
                *order.enter(other),
                normed_two,
                inverse_two,
                v["gain_two"].reshape(1, width),
                grad_hidden,
                proj_out,
                ranks,
            )
            order.leave(sends)
            grad_heads = exchange(sends)
            after_other = swap(after_send)
            up_chain.step()
            grad_heads, after_other = order.enter(grad_heads, after_other)
            order.leave(grad_heads)
            if before:
                before["down"].step()
            grad_proj, leaving, g_q_bias, g_v_bias = attend_backward(
                qkv, order.enter(grad_heads)[0].reshape(ranks * tokens, slab), lse, proj_qkv, ranks
            )
            order.leave(leaving)
            arrived = exchange(leaving)
            if before:
                before["mixed"].step()
            (grad_proj,) = order.enter(grad_proj)
            after_pair = jnp.concatenate([after_mine, after_other], axis=0)
            attended_flat = attended_pair.transpose(1, 0, 2).reshape(2 * tokens, width)
            g_mixed = weight_grad(
                [(attn_in, grad_proj, 0), (attended_flat, after_pair, offset)],
                owners,
                offset + flank,
                core if before else None,
            )
            order.leave(*(g_mixed if before else (g_mixed,)))
            mixed_chain = Chain(
                written(
                    owner_steps(*g_mixed) if before else queue_steps(g_mixed),
                    mixed_steps,
                    writer(
                        "mixed",
                        functools.partial(mixed_kernel, ranks=ranks, layers_seen=layers, offset=offset),
                        layer,
                        me,
                        (part, 3 * width),
                        (part, width),
                    ),
                )
            )
            if before:
                mixed_chain.step()
            (arrived,) = order.enter(arrived)
            grad_hidden, grad_mine, g_gain_one, g_bias_one = end_backward(
                arrived, normed_one, inverse_one, v["gain_one"].reshape(1, width), grad_after
            )
            order.leave(grad_mine)
            up_chain.step()
            if before:
                before["up"].step()
                before["down"].step()
                before["mixed"].step()
                down_chain.step()
            last, before = before, dict(up=up_chain, down=down_chain, mixed=mixed_chain)
            downs[layer] = down_chain

            zeros = jnp.zeros((1, width), FULL)
            small_grads[layer] = (
                g_gain_one,
                g_bias_one,
                lax.dynamic_update_slice(zeros, g_q_bias, (0, me * slab)),
                lax.dynamic_update_slice(zeros, g_v_bias, (0, me * slab)),
                g_out_bias,
                g_gain_two,
                g_bias_two,
                g_down_bias,
                g_up_bias,
            )

        each = 8 * part + 2 * half
        small_sum = local_call(
            functools.partial(pack_kernel, owners=owners, layers=layers, half=half),
            "pack_small",
            jax.ShapeDtypeStruct((owners, -(-layers * each // 128) * 128), FULL),
            *order.enter(*[row for grads in small_grads for row in grads]),
            scalars=(side,),
        )
        order.leave(small_sum)
        small_sum = lax.all_to_all(small_sum, "fsdp", split_axis=0, concat_axis=0, tiled=True)
        before["up"].step()
        last["mixed"].step()
        before["mixed"].step()
        before["down"].step()
        small_sum = sum_rows(order.enter(small_sum)[0])
        order.leave(small_sum)
        total = small_sum
        for j in range(1, pairs):
            total = total + pair_shift(small_sum, j)
        before["up"].step()
        before["mixed"].step()
        (total,) = order.enter(total)
        order.leave(total)
        total_other = swap(total)
        before["down"].step()
        down_out = local_call(
            down_kernel,
            "write_down",
            jax.ShapeDtypeStruct((hidden_part, layers, width), FULL),
            *order.enter(*[piece for chain in downs for piece in chain.result]),
            scalars=(side,),
        )
        order.leave(down_out)
        s = local_call(
            functools.partial(unpack_kernel, layers=layers, half=half),
            "unpack_small",
            tuple(jax.ShapeDtypeStruct((layers, n), FULL) for n in [part] * 8 + [hidden_part]),
            *order.enter(total, total_other),
        )
        order.leave(*s)
        before["mixed"].step()
        return (
            block_output,
            grad_hidden[None],
            s[0],
            s[1],
            outs["mixed"][0],
            jnp.stack([s[2], s[3]], axis=1),
            outs["mixed"][1],
            s[4],
            s[5],
            s[6],
            outs["up"][0],
            s[8],
            down_out.transpose(1, 0, 2),
            s[7],
        )

    return body


def solution(mesh):
    row, cols, deep = P(None, "fsdp"), P("fsdp", "seq", None), P(None, "fsdp", None)
    last = P(None, None, "fsdp")
    return jax.shard_map(
        make_body(mesh.shape["seq"], mesh.shape["fsdp"]),
        mesh=mesh,
        in_specs=(cols, cols, row, row, deep, last, deep, row, row, row, deep, row, deep, row),
        out_specs=(cols, cols, row, row, deep, last, deep, row, row, row, deep, row, deep, row),
        check_vma=False,
    )
```

```python
import functools
import math

import jax
import jax.numpy as jnp
from jax import lax
from jax.experimental import pallas as pl
from jax.experimental.pallas import tpu as pltpu
from jax.sharding import PartitionSpec as P

HEAD_DIM = 72
EPSILON = 1e-06
LOW = jnp.bfloat16
FULL = jnp.float32
HEAVY = pl.CostEstimate(flops=20_000_000_000, transcendentals=0, bytes_accessed=1)
LIGHT = pl.CostEstimate(flops=1, transcendentals=0, bytes_accessed=1)


def normalize(hidden):
    center = hidden - jnp.mean(hidden, axis=-1, keepdims=True)
    variance = jnp.mean(center * center, axis=-1, keepdims=True)
    inverse_std = lax.rsqrt(variance + EPSILON)
    return center * inverse_std, inverse_std


def normalize_back(upstream, normed, inverse_std, gain):
    scaled = upstream * gain
    grad_hidden = inverse_std * (
        scaled
        - jnp.mean(scaled, axis=-1, keepdims=True)
        - normed * jnp.mean(scaled * normed, axis=-1, keepdims=True)
    )
    return (
        grad_hidden,
        jnp.sum(upstream * normed, axis=0, keepdims=True),
        jnp.sum(upstream, axis=0, keepdims=True),
    )


def tangent_gelu(values):
    return jax.nn.gelu(values, approximate=True)


def gelu_back(values, upstream):
    return jax.vjp(tangent_gelu, values)[1](upstream)[0]


def mm(left, right):
    return jnp.dot(left, right, preferred_element_type=FULL)


def mm_rows(left, right):
    return lax.dot_general(left, right, (((0,), (0,)), ((), ())), preferred_element_type=FULL)


def mm_cols(left, right):
    return lax.dot_general(left, right, (((1,), (1,)), ((), ())), preferred_element_type=FULL)


def head_window(head, width):
    low = head * HEAD_DIM // 128 * 128
    high = min(-(-(head + 1) * HEAD_DIM // 128) * 128, width)
    return low, high


def head_mask(head, low, high):
    lane = lax.broadcasted_iota(jnp.int32, (1, high - low), 1) + low
    return (lane >= head * HEAD_DIM) & (lane < (head + 1) * HEAD_DIM)


def attend_forward_kernel(qkv_ref, o_ref, lse_ref, acc_ref):
    tokens, width = acc_ref.shape
    rows = min(256, tokens)
    scaling = HEAD_DIM ** (-0.5)
    acc_ref[...] = jnp.zeros_like(acc_ref)
    for head in range(width // HEAD_DIM):
        low, high = head_window(head, width)
        mask = head_mask(head, low, high)
        keys = qkv_ref[1, :, low:high]
        values = jnp.where(mask, qkv_ref[2, :, low:high], jnp.zeros((), LOW))
        for start in range(0, tokens, rows):
            queries = jnp.where(mask, qkv_ref[0, start : start + rows, low:high], jnp.zeros((), LOW))
            scores = mm_cols(queries, keys) * scaling
            peak = jnp.max(scores, axis=-1, keepdims=True)
            total = jnp.sum(jnp.exp(scores - peak), axis=-1, keepdims=True)
            lse = peak + jnp.log(total)
            probability = jnp.exp(scores - lse).astype(LOW)
            acc_ref[start : start + rows, low:high] += mm(probability, values)
            lse_ref[start : start + rows, head : head + 1] = lse
    ranks, _, block = o_ref.shape
    for rank in range(ranks):
        o_ref[rank] = acc_ref[rank * block : (rank + 1) * block].astype(LOW).T


def attend_forward(qkv, ranks):
    _, tokens, width = qkv.shape
    heads = width // HEAD_DIM
    return pl.pallas_call(
        attend_forward_kernel,
        out_shape=(
            jax.ShapeDtypeStruct((ranks, width, tokens // ranks), LOW),
            jax.ShapeDtypeStruct((tokens, heads), FULL),
        ),
        in_specs=[pl.BlockSpec(memory_space=pltpu.VMEM)],
        out_specs=(pl.BlockSpec(memory_space=pltpu.VMEM),) * 2,
        scratch_shapes=[pltpu.VMEM((tokens, width), FULL)],
        compiler_params=pltpu.CompilerParams(vmem_limit_bytes=24 << 20),
        cost_estimate=LIGHT,
        name="attend_forward",
    )(qkv)


def attend_backward_kernel(
    qkv_ref, got_ref, lse_ref, proj_ref, grad_ref, leave_ref, q_bias_ref, v_bias_ref, dq_ref, dk_ref, dv_ref, do_ref
):
    tokens, width = do_ref.shape
    ranks, _, block = got_ref.shape
    for rank in range(ranks):
        do_ref[rank * block : (rank + 1) * block] = got_ref[rank].T
    rows = min(256, tokens)
    scaling = HEAD_DIM ** (-0.5)
    for ref in (dq_ref, dk_ref, dv_ref):
        ref[...] = jnp.zeros_like(ref)
    zero = jnp.zeros((), LOW)
    for head in range(width // HEAD_DIM):
        low, high = head_window(head, width)
        mask = head_mask(head, low, high)
        keys = qkv_ref[1, :, low:high]
        values = qkv_ref[2, :, low:high]
        keys_masked = jnp.where(mask, keys, zero)
        for start in range(0, tokens, rows):
            span = slice(start, start + rows)
            queries = jnp.where(mask, qkv_ref[0, span, low:high], zero)
            upstream = jnp.where(mask, do_ref[span, low:high], zero)
            scores = mm_cols(queries, keys) * scaling
            probability = jnp.exp(scores - lse_ref[span, head : head + 1])
            grad_prob = mm_cols(upstream, values)
            inner = jnp.sum(probability * grad_prob, axis=-1, keepdims=True)
            grad_scores = (probability * (grad_prob - inner)).astype(LOW)
            dv_ref[:, low:high] += mm_rows(probability.astype(LOW), upstream)
            dk_ref[:, low:high] += mm_rows(grad_scores, queries)
            dq_ref[span, low:high] += mm(grad_scores, keys_masked)
    dq = (dq_ref[...] * scaling).astype(LOW)
    dv = dv_ref[...].astype(LOW)
    grad_ref[:, :width] = dq
    grad_ref[:, width : 2 * width] = (dk_ref[...] * scaling).astype(LOW)
    grad_ref[:, 2 * width :] = dv
    q_bias_ref[...] = jnp.sum(dq.astype(FULL), axis=0, keepdims=True)
    v_bias_ref[...] = jnp.sum(dv.astype(FULL), axis=0, keepdims=True)
    for rank in range(ranks):
        leave_ref[rank] = mm_cols(grad_ref[rank * block : (rank + 1) * block], proj_ref[...]).astype(LOW)


def attend_backward(qkv, upstream, lse, proj, ranks):
    _, tokens, width = qkv.shape
    heads = width // HEAD_DIM
    model = proj.shape[0]
    return pl.pallas_call(
        attend_backward_kernel,
        out_shape=(
            jax.ShapeDtypeStruct((tokens, 3 * width), LOW),
            jax.ShapeDtypeStruct((ranks, tokens // ranks, model), LOW),
            jax.ShapeDtypeStruct((1, width), FULL),
            jax.ShapeDtypeStruct((1, width), FULL),
        ),
        in_specs=[pl.BlockSpec(memory_space=pltpu.VMEM)] * 4,
        out_specs=(pl.BlockSpec(memory_space=pltpu.VMEM),) * 4,
        scratch_shapes=[pltpu.VMEM((tokens, width), FULL)] * 3 + [pltpu.VMEM((tokens, width), LOW)],
        compiler_params=pltpu.CompilerParams(vmem_limit_bytes=24 << 20),
        cost_estimate=HEAVY,
        name="attend_backward",
    )(qkv, upstream, lse, proj)


def attn_share_kernel(me_ref, out_w_ref, qkv_ref, *refs, layers, with_small, ranks):
    out_ref = refs[-1]
    part, width = out_w_ref.shape
    slab = width // ranks
    out_ref[:part, :width] = out_w_ref[...]
    for rank in range(ranks):

        @pl.when(me_ref[0] == rank)
        def _():
            for i in range(3):
                source = (i * ranks + rank) * slab
                target = width + i * slab
                out_ref[:part, target : target + slab] = qkv_ref[:, source : source + slab]

    if with_small:
        out_ref[part:, :] = jnp.zeros((out_ref.shape[0] - part, out_ref.shape[1]), LOW)
        for layer in range(layers):
            target = 0
            for ref in refs[:-1]:
                count = ref.shape[-1]
                for row in range(ref.shape[0] // layers):
                    source = layer * (ref.shape[0] // layers) + row
                    out_ref[part + layer : part + layer + 1, target : target + count] = ref[source : source + 1, :]
                    target += count


def attn_share(me, out_w, qkv_w, small, layers, ranks):
    part, width = out_w.shape
    rows = part + 8 * (len(small) > 0)
    return pl.pallas_call(
        functools.partial(attn_share_kernel, layers=layers, with_small=len(small) > 0, ranks=ranks),
        out_shape=jax.ShapeDtypeStruct((rows, width + 3 * width // ranks), LOW),
        in_specs=[pl.BlockSpec(memory_space=pltpu.SMEM)]
        + [pl.BlockSpec(memory_space=pltpu.VMEM)] * (2 + len(small)),
        out_specs=pl.BlockSpec(memory_space=pltpu.VMEM),
        compiler_params=pltpu.CompilerParams(vmem_limit_bytes=16 << 20),
        cost_estimate=LIGHT,
        name="attn_share",
    )(me.reshape(1), out_w, qkv_w, *small)


def share_kernel(side_ref, up_ref, down_ref, out_ref, *, owners, layer, half):
    part = up_ref.shape[0]
    hidden_part, _, width = down_ref.shape
    flank = owners // 2 * half
    out_ref[...] = jnp.zeros_like(out_ref)
    for side in range(2):

        @pl.when(side_ref[0] == side)
        def _():
            first = side * half
            count = min(half, hidden_part - first)
            out_ref[:count, :width] = down_ref[first : first + count, layer, :]
            for owner in range(owners):
                source = owner * hidden_part + first
                target = width + owner * half - (owner >= owners // 2) * flank
                row = (owner >= owners // 2) * part
                out_ref[row : row + part, target : target + count] = up_ref[:, source : source + count]


def feed_share(side, up, down, layer, owners, half):
    part, (hidden_part, _, width) = up.shape[0], down.shape
    lanes = width + -(-owners // 2 * half // 128) * 128
    return pl.pallas_call(
        functools.partial(share_kernel, owners=owners, layer=layer, half=half),
        out_shape=jax.ShapeDtypeStruct((max(2 * part, half), lanes), LOW),
        in_specs=[pl.BlockSpec(memory_space=pltpu.SMEM)] + [pl.BlockSpec(memory_space=pltpu.VMEM)] * 2,
        out_specs=pl.BlockSpec(memory_space=pltpu.VMEM),
        compiler_params=pltpu.CompilerParams(vmem_limit_bytes=16 << 20),
        cost_estimate=LIGHT,
        name="feed_share",
    )(side.reshape(1), up, down)


def local_call(kernel, name, out_shape, *operands, scalars=(), scratch=(), cost=HEAVY):
    return pl.pallas_call(
        kernel,
        out_shape=out_shape,
        in_specs=[pl.BlockSpec(memory_space=pltpu.SMEM)] * len(scalars)
        + [pl.BlockSpec(memory_space=pltpu.VMEM)] * len(operands),
        out_specs=jax.tree.map(lambda _: pl.BlockSpec(memory_space=pltpu.VMEM), out_shape),
        scratch_shapes=list(scratch),
        compiler_params=pltpu.CompilerParams(vmem_limit_bytes=24 << 20),
        cost_estimate=cost,
        name=name,
    )(*[s.reshape(1) for s in scalars], *operands)


def grad_kernel(*refs, owners, pieces, total, split):
    refs = list(refs)
    core_ref = refs.pop(0) if split else None
    operands = []
    for lefts, rights, turned, target in pieces:
        operands.append(([refs.pop(0) for _ in range(lefts)], [refs.pop(0) for _ in range(rights)], turned, target))
    outs = [refs.pop(0) for _ in range(2 if split else 1)]
    filled = []
    for lefts, rights, turned, target in operands:
        left_ref, right_ref = refs.pop(0), refs.pop(0)
        start = 0
        for ref in lefts:
            count = ref.shape[1 if turned else 0]
            left_ref[:, start : start + count] = ref[...] if turned else ref[...].T
            start += count
        start = 0
        for ref in rights:
            right_ref[start : start + ref.shape[0]] = ref[...]
            start += ref.shape[0]
        filled.append((left_ref, right_ref, target, target + right_ref.shape[1]))
    ends = [f[2] for f in filled[1:]] + [total]
    for (left_ref, right_ref, target, stop), end in zip(filled, ends, strict=True):
        if end > stop:
            for out in outs:
                out[..., stop:end] = jnp.zeros(out.shape[:-1] + (end - stop,), LOW)
        rows = left_ref.shape[0] // owners
        width = right_ref.shape[1]
        for start in range(0, width, 256):
            size = min(256, width - start)
            value = mm(left_ref[...], right_ref[:, start : start + size]).astype(LOW)
            if not split:
                outs[0][:, target + start : target + start + size] = value
                continue
            for core in range(2):

                @pl.when(core_ref[0] == core)
                def _():
                    for owner in range(owners):
                        out = outs[(owner % 2 != core) * 1]
                        out[owner // 2, :, target + start : target + start + size] = value[
                            owner * rows : (owner + 1) * rows
                        ]


def weight_grad(pieces, owners, total, core=None, cost=HEAVY):
    split = core is not None
    operands, shapes, scratch = [], [], []
    for lefts, rights, turned, target in pieces:
        operands += [*lefts, *rights]
        shapes.append((len(lefts), len(rights), turned, target))
        rows = lefts[0].shape[0 if turned else 1]
        tokens = sum(r.shape[0] for r in rights)
        scratch += [pltpu.VMEM((rows, tokens), LOW), pltpu.VMEM((tokens, rights[0].shape[1]), LOW)]
    out = jax.ShapeDtypeStruct((owners // 2, rows // owners, total) if split else (rows, total), LOW)
    return local_call(
        functools.partial(grad_kernel, owners=owners, pieces=shapes, total=total, split=split),
        "weight_grad",
        (out, out) if split else out,
        *operands,
        scalars=(core,) if split else (),
        scratch=scratch,
        cost=cost,
    )


def spread_kernel(all_ref, out_ref, qkv_ref, *small):
    owners, _, _ = all_ref.shape
    width = out_ref.shape[1]
    part = out_ref.shape[0] // owners
    for owner in range(owners):
        rows = slice(owner * part, (owner + 1) * part)
        out_ref[rows] = all_ref[owner, :part, :width]
        qkv_ref[rows] = all_ref[owner, :part, width:]
        for ref in small:
            ref[owner] = all_ref[owner, part:, :]


def spread(gathered, part, width):
    owners, rows, columns = gathered.shape
    return local_call(
        spread_kernel,
        "spread",
        [
            jax.ShapeDtypeStruct((owners * part, width), LOW),
            jax.ShapeDtypeStruct((owners * part, columns - width), LOW),
        ]
        + [jax.ShapeDtypeStruct((owners, rows - part, columns), LOW)] * (rows > part),
        gathered,
        cost=LIGHT,
    )


def unit_tiles(owners, half):
    flank = owners // 2 * half
    return [
        (side * flank + start, min(512, flank - start), side, start)
        for side in range(2)
        for start in range(0, flank, 512)
    ]


def up_tile(feed_ref, tile, part, width):
    _, count, side, start = tile
    lanes = slice(width + start, width + start + count)
    rows = slice(side * part, (side + 1) * part)
    return jnp.concatenate([feed_ref[owner, rows, lanes] for owner in range(feed_ref.shape[0])], axis=0)


def down_tile(feed_ref, tile, half, width):
    first, count, _, _ = tile
    pieces = []
    while count:
        owner, row = divmod(first, half)
        size = min(count, half - row)
        pieces.append(feed_ref[owner, row : row + size, :width])
        first, count = first + size, count - size
    return jnp.concatenate(pieces, axis=0)


GELU_SCALE = (2 / math.pi) ** 0.5


def feed_forward_kernel(mine_ref, other_ref, feed_ref, bias_ref, pre_ref, act_ref, *refs, half):
    tokens, width = mine_ref.shape
    owners = feed_ref.shape[0]
    part = width // owners
    both = jnp.concatenate([mine_ref[...], other_ref[...]], axis=0)
    if refs:
        keep_ref, leave_ref, acc_ref = refs
        acc_ref[...] = jnp.zeros_like(acc_ref)
    for tile in unit_tiles(owners, half):
        span = slice(tile[0], tile[0] + tile[1])
        pre = mm(both, up_tile(feed_ref, tile, part, width)) + bias_ref[:, span]
        pre_ref[:, span] = pre
        act = (0.5 * pre * (1 + jnp.tanh(GELU_SCALE * (pre + 0.044715 * (pre * pre * pre))))).astype(LOW)
        act_ref[:, span] = act
        if refs:
            acc_ref[...] += mm(act, down_tile(feed_ref, tile, half, width))
    if refs:
        keep_ref[...] = acc_ref[:tokens]
        leave_ref[...] = acc_ref[tokens:].astype(LOW)


def feed_forward(mine, other, feed, bias, half, mixed):
    tokens, width = mine.shape
    units = feed.shape[0] * half
    shapes = [jax.ShapeDtypeStruct((2 * tokens, units), FULL), jax.ShapeDtypeStruct((2 * tokens, units), LOW)]
    if mixed:
        shapes += [jax.ShapeDtypeStruct((tokens, width), FULL), jax.ShapeDtypeStruct((tokens, width), LOW)]
    return local_call(
        functools.partial(feed_forward_kernel, half=half),
        "feed_forward",
        shapes,
        mine,
        other,
        feed,
        bias,
        scratch=[pltpu.VMEM((2 * tokens, width), FULL)] * mixed,
    )


def feed_out_kernel(act_ref, feed_ref, keep_ref, leave_ref, acc_ref, *, half):
    tokens, width = keep_ref.shape
    acc_ref[...] = jnp.zeros_like(acc_ref)
    for tile in unit_tiles(feed_ref.shape[0], half):
        acc_ref[...] += mm(act_ref[:, tile[0] : tile[0] + tile[1]], down_tile(feed_ref, tile, half, width))
    keep_ref[...] = acc_ref[:tokens]
    leave_ref[...] = acc_ref[tokens:].astype(LOW)


def feed_out(act, feed, width, half):
    tokens = act.shape[0] // 2
    return local_call(
        functools.partial(feed_out_kernel, half=half),
        "feed_out",
        (jax.ShapeDtypeStruct((tokens, width), FULL), jax.ShapeDtypeStruct((tokens, width), LOW)),
        act,
        feed,
        scratch=[pltpu.VMEM((2 * tokens, width), FULL)],
    )


def feed_backward_kernel(
    mine_ref, other_ref, pre_ref, feed_ref, low_ref, grad_ref, keep_ref, leave_ref, bias_ref, acc_ref, *, half
):
    tokens, width = mine_ref.shape
    owners = feed_ref.shape[0]
    part = width // owners
    low_ref[:tokens] = mine_ref[...]
    low_ref[tokens:] = other_ref[...]
    acc_ref[...] = jnp.zeros_like(acc_ref)
    for tile in unit_tiles(owners, half):
        span = slice(tile[0], tile[0] + tile[1])
        pre = pre_ref[:, span]
        square = pre * pre
        bend = jnp.tanh(GELU_SCALE * (pre + 0.044715 * pre * square))
        slope = 0.5 * (1 + bend) + 0.5 * pre * (1 - bend * bend) * (GELU_SCALE * (1 + 3 * 0.044715 * square))
        grad = mm_cols(low_ref[...], down_tile(feed_ref, tile, half, width)) * slope
        bias_ref[:, span] = jnp.sum(grad, axis=0, keepdims=True)
        grad = grad.astype(LOW)
        grad_ref[:, span] = grad
        acc_ref[...] += mm_cols(grad, up_tile(feed_ref, tile, part, width))
    keep_ref[...] = acc_ref[:tokens]
    leave_ref[...] = acc_ref[tokens:].astype(LOW)


def feed_backward(mine, other, pre_act, feed, half):
    tokens, width = mine.shape
    units = pre_act.shape[1]
    return local_call(
        functools.partial(feed_backward_kernel, half=half),
        "feed_backward",
        (
            jax.ShapeDtypeStruct((2 * tokens, width), LOW),
            jax.ShapeDtypeStruct((2 * tokens, units), LOW),
            jax.ShapeDtypeStruct((tokens, width), FULL),
            jax.ShapeDtypeStruct((tokens, width), LOW),
            jax.ShapeDtypeStruct((1, units), FULL),
        ),
        mine,
        other,
        pre_act,
        feed,
        scratch=[pltpu.VMEM((2 * tokens, width), FULL)],
    )


def mid_backward_kernel(
    side_ref, keep_ref, got_ref, normed_ref, inverse_ref, gain_ref, grad_ref, proj_ref, *outs
):
    after_ref, send_ref, mine_ref, other_ref, g_gain_ref, g_bias_ref, g_out_ref, g_down_ref = outs
    upstream = keep_ref[...] + got_ref[...].astype(FULL)
    grad = grad_ref[...]
    back, g_gain, g_bias = normalize_back(upstream, normed_ref[...], inverse_ref[...], gain_ref[...])
    after = grad + back
    after_ref[...] = after
    g_gain_ref[...] = g_gain
    g_bias_ref[...] = g_bias
    g_out_ref[...] = jnp.sum(after, axis=0, keepdims=True)
    g_down_ref[...] = jnp.sum(grad, axis=0, keepdims=True)
    low = after.astype(LOW)
    flank = mine_ref.shape[1]
    for side in range(2):

        @pl.when(side_ref[0] == side)
        def _():
            mine_ref[...] = low[:, side * flank : (side + 1) * flank]
            other_ref[...] = low[:, (1 - side) * flank : (2 - side) * flank]

    ranks, slab, _ = send_ref.shape
    for rank in range(ranks):
        send_ref[rank] = mm_cols(proj_ref[rank * slab : (rank + 1) * slab, :], low).astype(LOW)


def mid_backward(side, keep, got, normed, inverse, gain, grad, proj, ranks):
    tokens, width = keep.shape
    row = jax.ShapeDtypeStruct((1, width), FULL)
    half = jax.ShapeDtypeStruct((tokens, width // 2), LOW)
    return local_call(
        mid_backward_kernel,
        "mid_backward",
        (
            jax.ShapeDtypeStruct((tokens, width), FULL),
            jax.ShapeDtypeStruct((ranks, width // ranks, tokens), LOW),
            half,
            half,
            row,
            row,
            row,
            row,
        ),
        keep,
        got,
        normed,
        inverse,
        gain,
        grad,
        proj,
        scalars=(side,),
    )


def end_backward_kernel(got_ref, normed_ref, inverse_ref, gain_ref, after_ref, out_ref, low_ref, g_gain_ref, g_bias_ref):
    upstream = got_ref[0].astype(FULL)
    for rank in range(1, got_ref.shape[0]):
        upstream += got_ref[rank].astype(FULL)
    back, g_gain, g_bias = normalize_back(upstream, normed_ref[...], inverse_ref[...], gain_ref[...])
    total = after_ref[...] + back
    out_ref[...] = total
    low_ref[...] = total.astype(LOW)
    g_gain_ref[...] = g_gain
    g_bias_ref[...] = g_bias


def end_backward(got, normed, inverse, gain, after):
    tokens, width = after.shape
    row = jax.ShapeDtypeStruct((1, width), FULL)
    return local_call(
        end_backward_kernel,
        "end_backward",
        (
            jax.ShapeDtypeStruct((tokens, width), FULL),
            jax.ShapeDtypeStruct((tokens, width), LOW),
            row,
            row,
        ),
        got,
        normed,
        inverse,
        gain,
        after,
    )


def meet_kernel(chip_ref, keep_ref, got_ref, *outs):
    step = pl.program_id(0)
    for j, out in enumerate(outs):

        @pl.when(step == j)
        def _():
            out[...] = (keep_ref[0].astype(FULL) + got_ref[0].astype(FULL)).astype(LOW)


def meet_cores(chip, keep, got):
    chips, rows, columns = keep.shape
    block = pl.BlockSpec((1, rows, columns), lambda j, chip_ref: (chip_ref[0] ^ j, 0, 0))
    return pl.pallas_call(
        meet_kernel,
        grid_spec=pltpu.PrefetchScalarGridSpec(
            num_scalar_prefetch=1,
            grid=(chips,),
            in_specs=[block, block],
            out_specs=[pl.BlockSpec((rows, columns), lambda j, chip_ref: (0, 0))] * chips,
        ),
        out_shape=[jax.ShapeDtypeStruct((rows, columns), LOW)] * chips,
        compiler_params=pltpu.CompilerParams(vmem_limit_bytes=24 << 20),
        cost_estimate=LIGHT,
        name="meet_cores",
    )(chip.reshape(1), keep, got)


def add_kernel(*refs):
    total = refs[0][...].astype(FULL)
    for ref in refs[1:-1]:
        total += ref[...].astype(FULL)
    refs[-1][...] = total.astype(LOW)


def add_all(*values):
    return local_call(add_kernel, "add_all", jax.ShapeDtypeStruct(values[0].shape, LOW), *values, cost=LIGHT)


def up_kernel(side_ref, own_ref, across_ref, *refs, owners, half):
    out_ref = refs[-1]
    hidden_part = out_ref.shape[2] // owners
    for mine in range(2):

        @pl.when(side_ref[0] == mine)
        def _():
            for side in range(2):
                ref = own_ref if side == mine else across_ref
                first = side * half
                count = min(half, hidden_part - first)
                for owner in range(owners):
                    target = owner * hidden_part + first
                    source = owner * half
                    out_ref[0, :, target : target + count] = ref[:, source : source + count].astype(FULL)


def mixed_kernel(me_ref, own_ref, across_ref, *refs, ranks, offset):
    qkv_out, out_out = refs[-2:]
    width = out_out.shape[2]
    slab, flank, pairs = width // ranks, width // 2, ranks // 2
    for me in range(ranks):

        @pl.when(me_ref[0] == me)
        def _():
            side, pair = me % 2, me // 2
            for flip, ref in enumerate((own_ref, across_ref)):
                for j in range(pairs):
                    rank = (pair - j) % pairs * 2 + (side ^ flip)
                    for i in range(3):
                        target = (i * ranks + rank) * slab
                        source = j * offset + i * slab
                        qkv_out[0, :, target : target + slab] = ref[:, source : source + slab].astype(FULL)
                target = (side ^ flip) * flank
                out_out[0, :, target : target + flank] = ref[:, pairs * offset :].astype(FULL)


def write_layer(kernel, name, layer, layers, shapes, earlier, scalar, *values):
    return pl.pallas_call(
        kernel,
        grid=(1,),
        out_shape=tuple(jax.ShapeDtypeStruct((layers,) + s, FULL) for s in shapes),
        in_specs=[pl.BlockSpec(memory_space=pltpu.SMEM)]
        + [pl.BlockSpec(v.shape, lambda i: (0, 0)) for v in values]
        + [pl.BlockSpec(memory_space=pl.ANY)] * len(earlier),
        out_specs=tuple(pl.BlockSpec((1,) + s, lambda i: (layer, 0, 0)) for s in shapes),
        input_output_aliases={1 + len(values) + i: i for i in range(len(earlier))},
        compiler_params=pltpu.CompilerParams(vmem_limit_bytes=40 << 20),
        cost_estimate=LIGHT,
        name=name,
    )(scalar.reshape(1), *values, *earlier)


def down_kernel(side_ref, *refs):
    out_ref = refs[-1]
    half = refs[0].shape[0]
    hidden_part = out_ref.shape[0]
    for mine in range(2):

        @pl.when(side_ref[0] == mine)
        def _():
            for layer in range(len(refs) // 2):
                for side in range(2):
                    ref = refs[2 * layer + (side != mine)]
                    first = side * half
                    count = min(half, hidden_part - first)
                    out_ref[first : first + count, layer, :] = ref[:count].astype(FULL)


def pack_kernel(side_ref, *refs, owners, layers, half):
    out_ref = refs[-1]
    each = len(refs) // layers
    out_ref[...] = jnp.zeros_like(out_ref)
    target = 0
    for layer in range(layers):
        rows = refs[layer * each : (layer + 1) * each]
        for ref in rows[:-1]:
            part = ref.shape[1] // owners
            for owner in range(owners):
                out_ref[owner : owner + 1, target : target + part] = ref[:, owner * part : (owner + 1) * part]
            target += part
        for side in range(2):

            @pl.when(side_ref[0] == side)
            def _():
                for owner in range(owners):
                    first = target + side * half
                    out_ref[owner : owner + 1, first : first + half] = rows[-1][
                        :, owner * half : (owner + 1) * half
                    ]

        target += 2 * half


def unpack_kernel(first_ref, second_ref, *outs, layers, half):
    values = first_ref[...] + second_ref[...]
    part = outs[0].shape[1]
    target = 0
    for layer in range(layers):
        for out in outs[:-1]:
            out[layer : layer + 1, :] = values[:, target : target + part]
            target += part
        out = outs[-1]
        out[layer : layer + 1, :] = values[:, target : target + out.shape[1]]
        target += 2 * half


class Order:
    def __init__(self):
        self.last = ()

    def enter(self, *values):
        if not self.last:
            return values
        return lax.optimization_barrier(tuple(values) + self.last)[: len(values)]

    def leave(self, *values):
        self.last = tuple(values)


class Chain:
    def __init__(self, steps):
        self.steps = steps
        self.result = None
        self.step()

    def step(self):
        try:
            next(self.steps)
        except StopIteration as stop:
            self.result = stop.value


def make_body(ranks, owners):
    pairs, chips = ranks // 2, owners // 2

    def shift(value, step):
        return lax.ppermute(value, "seq", [(i, (i + step) % ranks) for i in range(ranks)])

    def swap(value):
        return lax.ppermute(value, "seq", [(i, i ^ 1) for i in range(ranks)])

    def pair_shift(value, step):
        return lax.ppermute(value, "seq", [(i, (i + 2 * step) % ranks) for i in range(ranks)])

    def owner_xor(value, bits):
        return lax.ppermute(value, "fsdp", [(i, i ^ bits) for i in range(owners)])

    def exchange(blocks):
        return lax.all_to_all(blocks, "seq", split_axis=0, concat_axis=0, tiled=True)

    def body(
        block_input,
        grad_output,
        attn_norm_gain,
        attn_norm_bias,
        qkv_weight,
        qv_bias,
        out_weight,
        out_bias,
        mlp_norm_gain,
        mlp_norm_bias,
        up_weight,
        up_bias,
        down_weight,
        down_bias,
    ):
        layers = qkv_weight.shape[0]
        tokens, width = block_input.shape[1:]
        slab, flank = width // ranks, width // 2
        part = qkv_weight.shape[1]
        hidden_part = down_weight.shape[1]
        half = -(-hidden_part // 32) * 16
        me = lax.axis_index("seq")
        owner = lax.axis_index("fsdp")
        core, chip = owner % 2, owner // 2
        side, pair = me % 2, me // 2

        def at(value, index, axis=0):
            return lax.dynamic_index_in_dim(value, index, axis, keepdims=False)

        def put(value, block, *index):
            return lax.dynamic_update_slice(
                value, block.reshape((1,) * len(index) + block.shape), index + (0,) * block.ndim
            )

        def rank_at(j):
            return (me + j) % ranks

        order = Order()

        def owner_steps(keep, send):
            got = owner_xor(send, 1)
            yield
            (got,) = order.enter(got)
            mine, *sends = meet_cores(chip, keep, got)
            order.leave(*sends)
            got = [owner_xor(send, 2 * j) for j, send in enumerate(sends, 1)]
            yield
            return add_all(mine, *order.enter(*got))

        def queue_steps(value):
            value = lax.psum_scatter(value, "fsdp", scatter_dimension=0, tiled=True)
            yield
            return order.enter(value)[0]

        def pair_steps(value):
            order.leave(value)
            got = [pair_shift(value, j) for j in range(1, pairs)]
            yield
            own = add_all(value, *order.enter(*got))
            order.leave(own)
            across = swap(own)
            yield
            return own, order.enter(across)[0]

        def mixed_steps(value):
            order.leave(value)
            got = [pair_shift(value, j) for j in range(1, pairs)]
            yield
            got = order.enter(*got)
            total = add_all(*[v[:, offset:] for v in (value, *got)])
            shares = [v[:, :offset] for v in (value, *got)]
            send = jnp.concatenate([*shares, total], axis=1)
            order.leave(send)
            across = swap(send)
            yield
            (across,) = order.enter(across)
            return send, across

        def written(steps, stage, write):
            value = yield from steps
            value = yield from stage(value)
            value = write(*value)
            order.leave(*value)
            return value

        columns = width + 3 * slab
        offset = -(-3 * slab // 128) * 128

        def gather_tokens(mine):
            return exchange(jnp.broadcast_to(mine, (ranks,) + mine.shape))

        all_input = gather_tokens(block_input[0])
        small = (
            attn_norm_gain,
            attn_norm_bias,
            qv_bias.reshape(2 * layers, part),
            out_bias,
            mlp_norm_gain,
            mlp_norm_bias,
            down_bias,
            up_bias,
        )
        down_turned = down_weight.transpose(1, 0, 2)

        attn_shares, feeds = [], []
        for layer in range(layers):
            share = attn_share(
                me, out_weight[layer], *order.enter(qkv_weight[layer]), small if layer == 0 else (), layers, ranks
            )
            order.leave(share)
            attn_shares.append(lax.all_gather(share, "fsdp", axis=0))
            share = feed_share(side, *order.enter(up_weight[layer]), down_turned, layer, owners, half)
            order.leave(share)
            feeds.append(lax.all_gather(share, "fsdp", axis=0))
        (all_input,) = order.enter(all_input)
        normed_all, _ = normalize(all_input.reshape(ranks * tokens, width).astype(FULL))
        order.leave(normed_all)
        *weights, small_all = spread(*order.enter(attn_shares[0]), part, width)
        order.leave(*weights, small_all)
        rows_all = small_all[:, :layers, : 8 * part].reshape(owners, layers, 8, part)
        rows_all = rows_all.transpose(1, 2, 0, 3).reshape(layers, 8, width).astype(FULL)
        up_all = small_all[:, :layers, 8 * part : 8 * part + hidden_part].astype(FULL)
        up_all = jnp.pad(up_all, ((0, 0), (0, 0), (0, 2 * half - hidden_part)))

        vectors = []
        for layer in range(layers):
            rows = rows_all[layer]
            vectors.append(
                dict(
                    gain_one=rows[0],
                    bias_one=rows[1],
                    bias_q=lax.dynamic_slice(rows[2], (me * slab,), (slab,)),
                    bias_v=lax.dynamic_slice(rows[3], (me * slab,), (slab,)),
                    bias_out=rows[4],
                    gain_two=rows[5],
                    bias_two=rows[6],
                    bias_down=rows[7],
                    bias_up=lax.dynamic_slice(
                        up_all[:, layer], (0, side * half), (owners, half)
                    ).reshape(owners * half),
                )
            )

        hidden = block_input[0].astype(FULL)
        stored = []
        for layer in range(layers):
            v = vectors[layer]
            last_layer = layer == layers - 1
            normed_one, inverse_one = normalize(hidden)
            if layer == 0:
                attn_in = (normed_all * v["gain_one"] + v["bias_one"]).astype(LOW)
            else:
                attn_mine = (normed_one * v["gain_one"] + v["bias_one"]).astype(LOW)
                order.leave(attn_mine)
                attn_in = gather_tokens(attn_mine)
                weights = spread(*order.enter(attn_shares[layer]), part, width)
                order.leave(*weights)
                attn_in = order.enter(attn_in)[0].reshape(ranks * tokens, width)
            proj_out, proj_qkv = weights
            bias_row = jnp.concatenate([v["bias_q"], jnp.zeros((slab,), FULL), v["bias_v"]])
            projected = (mm(attn_in, proj_qkv) + bias_row).astype(LOW)
            qkv = jnp.stack([projected[:, i * slab : (i + 1) * slab] for i in range(3)])
            out_heads, lse = attend_forward(qkv, ranks)
            order.leave(out_heads)
            attended = order.enter(exchange(out_heads))[0].reshape(width, tokens)
            after_attn = hidden + mm_rows(attended, proj_out) + v["bias_out"]
            normed_two, inverse_two = normalize(after_attn)
            mlp_mine = (normed_two * v["gain_two"] + v["bias_two"]).astype(LOW)
            order.leave(mlp_mine)
            mlp_other = swap(mlp_mine)
            attended_other = swap(order.enter(attended)[0])
            mlp_other, attended_other = order.enter(mlp_other, attended_other)
            (feed,) = order.enter(feeds[layer])
            pre_act, activated, *mixed = feed_forward(
                mlp_mine, mlp_other, feed, v["bias_up"].reshape(1, owners * half), half, not last_layer
            )
            if last_layer:
                order.leave(pre_act, activated)
            else:
                mixed, leaving = mixed
                order.leave(leaving)
                (other,) = order.enter(swap(leaving))
                hidden = after_attn + mixed + other.astype(FULL) + v["bias_down"]
            stored.append(
                (
                    (proj_qkv, proj_out, feed),
                    (normed_one, inverse_one, attn_in, qkv, lse, attended, attended_other),
                    (normed_two, inverse_two, mlp_mine, mlp_other, pre_act, activated),
                )
            )

        def writer(key, kernel, layer, scalar, *shapes):
            def write(*values):
                outs[key] = write_layer(
                    kernel, "write_" + key, layer, layers, shapes, outs[key], scalar, *values
                )
                return outs[key]

            return write

        def held(*values):
            return values

        def sum_rows(value):
            return jnp.sum(value, axis=0, keepdims=True)

        grad_hidden, grad_mine = grad_output[0].astype(FULL), grad_output[0]
        small_grads = [None] * layers
        downs = [None] * layers
        outs = dict(up=(), mixed=())
        before = None
        for layer in reversed(range(layers)):
            v = vectors[layer]
            proj_qkv, proj_out, feed = stored[layer][0]
            normed_one, inverse_one, attn_in, qkv, lse, attended, attended_other = stored[layer][1]
            normed_two, inverse_two, mlp_mine, mlp_other, pre_act, activated = stored[layer][2]
            grad_other = swap(grad_mine)
            if before:
                before["down"].step()
            (grad_other,) = order.enter(grad_other)
            grad_low, grad_pre_low, mixed, leaving, g_up_bias = feed_backward(
                grad_mine, grad_other, pre_act, feed, half
            )
            order.leave(leaving)
            other = swap(leaving)
            g_down = weight_grad([((activated,), order.enter(grad_low), False, 0)], owners, width)
            order.leave(g_down)
            down_chain = Chain(written(queue_steps(g_down), pair_steps, held))
            keep, send = weight_grad(
                [((mlp_mine, mlp_other), order.enter(grad_pre_low), False, 0)],
                owners,
                half * owners,
                core,
                LIGHT,
            )
            order.leave(send)
            up_chain = Chain(
                written(
                    owner_steps(keep, send),
                    pair_steps,
                    writer(
                        "up",
                        functools.partial(up_kernel, owners=owners, half=half),
                        layer,
                        side,
                        (part, owners * hidden_part),
                    ),
                )
            )
            (other,) = order.enter(other)
            order.leave(other)
            if before:
                before["up"].step()
            grad_after, sends, after_mine, after_send, g_gain_two, g_bias_two, g_out_bias, g_down_bias = mid_backward(
                side,
                mixed,
                *order.enter(other),
                normed_two,
                inverse_two,
                v["gain_two"].reshape(1, width),
                grad_hidden,
                proj_out,
                ranks,
            )
            order.leave(sends)
            grad_heads = exchange(sends)
            after_other = swap(after_send)
            up_chain.step()
            grad_heads, after_other = order.enter(grad_heads, after_other)
            order.leave(grad_heads)
            if before:
                before["down"].step()
                before["mixed"].step()
            grad_proj, leaving, g_q_bias, g_v_bias = attend_backward(
                qkv, *order.enter(grad_heads), lse, proj_qkv, ranks
            )
            order.leave(leaving)
            arrived = exchange(leaving)
            if before:
                before["up"].step()
            (grad_proj,) = order.enter(grad_proj)
            g_mixed = weight_grad(
                [
                    ((attn_in,), (grad_proj,), False, 0),
                    ((attended, attended_other), (after_mine, after_other), True, offset),
                ],
                owners,
                offset + flank,
                core if before else None,
            )
            order.leave(*(g_mixed if before else (g_mixed,)))
            mixed_chain = Chain(
                written(
                    owner_steps(*g_mixed) if before else queue_steps(g_mixed),
                    mixed_steps,
                    writer(
                        "mixed",
                        functools.partial(mixed_kernel, ranks=ranks, offset=offset),
                        layer,
                        me,
                        (part, 3 * width),
                        (part, width),
                    ),
                )
            )
            if before:
                up_chain.step()
                down_chain.step()
                mixed_chain.step()
            else:
                final, leaving = feed_out(*order.enter(activated), feed, width, half)
                order.leave(leaving)
                final_other = swap(leaving)
            (arrived,) = order.enter(arrived)
            grad_hidden, grad_mine, g_gain_one, g_bias_one = end_backward(
                arrived, normed_one, inverse_one, v["gain_one"].reshape(1, width), grad_after
            )
            order.leave(grad_hidden)
            if before:
                before["mixed"].step()
                before["down"].step()
            else:
                up_chain.step()
            last, before = before, dict(up=up_chain, down=down_chain, mixed=mixed_chain)
            downs[layer] = down_chain

            zeros = jnp.zeros((1, width), FULL)
            small_grads[layer] = (
                g_gain_one,
                g_bias_one,
                lax.dynamic_update_slice(zeros, g_q_bias, (0, me * slab)),
                lax.dynamic_update_slice(zeros, g_v_bias, (0, me * slab)),
                g_out_bias,
                g_gain_two,
                g_bias_two,
                g_down_bias,
                g_up_bias,
            )

        each = 8 * part + 2 * half
        v = vectors[layers - 1]
        small_sum = local_call(
            functools.partial(pack_kernel, owners=owners, layers=layers, half=half),
            "pack_small",
            jax.ShapeDtypeStruct((owners, -(-layers * each // 128) * 128), FULL),
            *order.enter(*[row for grads in small_grads for row in grads]),
            scalars=(side,),
            cost=LIGHT,
        )
        order.leave(small_sum)
        small_sum = lax.all_to_all(small_sum, "fsdp", split_axis=0, concat_axis=0, tiled=True)
        before["up"].step()
        before["down"].step()
        last["mixed"].step()
        before["mixed"].step()
        small_sum = sum_rows(order.enter(small_sum)[0])
        order.leave(small_sum)
        total = small_sum
        for j in range(1, pairs):
            total = total + pair_shift(small_sum, j)
        before["up"].step()
        before["mixed"].step()
        before["down"].step()
        (total,) = order.enter(total)
        order.leave(total)
        total_other = swap(total)
        down_out = local_call(
            down_kernel,
            "write_down",
            jax.ShapeDtypeStruct((hidden_part, layers, width), FULL),
            *order.enter(*[piece for chain in downs for piece in chain.result]),
            scalars=(side,),
        )
        order.leave(down_out)
        (final_other,) = order.enter(final_other)
        block_output = (after_attn + final + final_other.astype(FULL) + v["bias_down"]).astype(LOW)[None]
        order.leave(block_output)
        s = local_call(
            functools.partial(unpack_kernel, layers=layers, half=half),
            "unpack_small",
            tuple(jax.ShapeDtypeStruct((layers, n), FULL) for n in [part] * 8 + [hidden_part]),
            *order.enter(total, total_other),
        )
        order.leave(*s)
        before["mixed"].step()
        return (
            block_output,
            grad_hidden[None],
            s[0],
            s[1],
            outs["mixed"][0],
            jnp.stack([s[2], s[3]], axis=1),
            outs["mixed"][1],
            s[4],
            s[5],
            s[6],
            outs["up"][0],
            s[8],
            down_out.transpose(1, 0, 2),
            s[7],
        )

    return body


def solution(mesh):
    row, cols, deep = P(None, "fsdp"), P("fsdp", "seq", None), P(None, "fsdp", None)
    last = P(None, None, "fsdp")
    return jax.shard_map(
        make_body(mesh.shape["seq"], mesh.shape["fsdp"]),
        mesh=mesh,
        in_specs=(cols, cols, row, row, deep, last, deep, row, row, row, deep, row, deep, row),
        out_specs=(cols, cols, row, row, deep, last, deep, row, row, row, deep, row, deep, row),
        check_vma=False,
    )
```

```python
import functools
import math

import jax
import jax.numpy as jnp
from jax import lax
from jax.experimental import pallas as pl
from jax.experimental.pallas import tpu as pltpu
from jax.sharding import PartitionSpec as P

HEAD_DIM = 72
EPSILON = 1e-06
LOW = jnp.bfloat16
FULL = jnp.float32
HEAVY = pl.CostEstimate(flops=20_000_000_000, transcendentals=0, bytes_accessed=1)
LIGHT = pl.CostEstimate(flops=1, transcendentals=0, bytes_accessed=1)
PLAN = {"final_early": 1, "other_late": 0, "sum_up_late": 1, "add_up_early": 1, "add_mixed_early": 1}


def cost_of(name):
    return HEAVY if PLAN.get(name, 0) else LIGHT


def normalize(hidden):
    center = hidden - jnp.mean(hidden, axis=-1, keepdims=True)
    variance = jnp.mean(center * center, axis=-1, keepdims=True)
    inverse_std = lax.rsqrt(variance + EPSILON)
    return center * inverse_std, inverse_std


def normalize_back(upstream, normed, inverse_std, gain):
    scaled = upstream * gain
    grad_hidden = inverse_std * (
        scaled
        - jnp.mean(scaled, axis=-1, keepdims=True)
        - normed * jnp.mean(scaled * normed, axis=-1, keepdims=True)
    )
    return (
        grad_hidden,
        jnp.sum(upstream * normed, axis=0, keepdims=True),
        jnp.sum(upstream, axis=0, keepdims=True),
    )


def tangent_gelu(values):
    return jax.nn.gelu(values, approximate=True)


def gelu_back(values, upstream):
    return jax.vjp(tangent_gelu, values)[1](upstream)[0]


def mm(left, right):
    return jnp.dot(left, right, preferred_element_type=FULL)


def mm_rows(left, right):
    return lax.dot_general(left, right, (((0,), (0,)), ((), ())), preferred_element_type=FULL)


def mm_cols(left, right):
    return lax.dot_general(left, right, (((1,), (1,)), ((), ())), preferred_element_type=FULL)


def head_window(head, width):
    low = head * HEAD_DIM // 128 * 128
    high = min(-(-(head + 1) * HEAD_DIM // 128) * 128, width)
    return low, high


def head_mask(head, low, high):
    lane = lax.broadcasted_iota(jnp.int32, (1, high - low), 1) + low
    return (lane >= head * HEAD_DIM) & (lane < (head + 1) * HEAD_DIM)


def attend_forward_kernel(qkv_ref, o_ref, lse_ref, acc_ref):
    tokens, width = acc_ref.shape
    rows = min(256, tokens)
    scaling = HEAD_DIM ** (-0.5)
    acc_ref[...] = jnp.zeros_like(acc_ref)
    for head in range(width // HEAD_DIM):
        low, high = head_window(head, width)
        mask = head_mask(head, low, high)
        keys = qkv_ref[1, :, low:high]
        values = jnp.where(mask, qkv_ref[2, :, low:high], jnp.zeros((), LOW))
        for start in range(0, tokens, rows):
            queries = jnp.where(mask, qkv_ref[0, start : start + rows, low:high], jnp.zeros((), LOW))
            scores = mm_cols(queries, keys) * scaling
            peak = jnp.max(scores, axis=-1, keepdims=True)
            total = jnp.sum(jnp.exp(scores - peak), axis=-1, keepdims=True)
            lse = peak + jnp.log(total)
            probability = jnp.exp(scores - lse).astype(LOW)
            acc_ref[start : start + rows, low:high] += mm(probability, values)
            lse_ref[start : start + rows, head : head + 1] = lse
    ranks, _, block = o_ref.shape
    for rank in range(ranks):
        o_ref[rank] = acc_ref[rank * block : (rank + 1) * block].astype(LOW).T


def attend_forward(qkv, ranks):
    _, tokens, width = qkv.shape
    heads = width // HEAD_DIM
    return pl.pallas_call(
        attend_forward_kernel,
        out_shape=(
            jax.ShapeDtypeStruct((ranks, width, tokens // ranks), LOW),
            jax.ShapeDtypeStruct((tokens, heads), FULL),
        ),
        in_specs=[pl.BlockSpec(memory_space=pltpu.VMEM)],
        out_specs=(pl.BlockSpec(memory_space=pltpu.VMEM),) * 2,
        scratch_shapes=[pltpu.VMEM((tokens, width), FULL)],
        compiler_params=pltpu.CompilerParams(vmem_limit_bytes=24 << 20),
        cost_estimate=LIGHT,
        name="attend_forward",
    )(qkv)


def attend_backward_kernel(
    qkv_ref, got_ref, lse_ref, proj_ref, grad_ref, leave_ref, q_bias_ref, v_bias_ref, dq_ref, dk_ref, dv_ref, do_ref
):
    tokens, width = do_ref.shape
    ranks, _, block = got_ref.shape
    for rank in range(ranks):
        do_ref[rank * block : (rank + 1) * block] = got_ref[rank].T
    rows = min(256, tokens)
    scaling = HEAD_DIM ** (-0.5)
    for ref in (dq_ref, dk_ref, dv_ref):
        ref[...] = jnp.zeros_like(ref)
    zero = jnp.zeros((), LOW)
    for head in range(width // HEAD_DIM):
        low, high = head_window(head, width)
        mask = head_mask(head, low, high)
        keys = qkv_ref[1, :, low:high]
        values = qkv_ref[2, :, low:high]
        keys_masked = jnp.where(mask, keys, zero)
        for start in range(0, tokens, rows):
            span = slice(start, start + rows)
            queries = jnp.where(mask, qkv_ref[0, span, low:high], zero)
            upstream = jnp.where(mask, do_ref[span, low:high], zero)
            scores = mm_cols(queries, keys) * scaling
            probability = jnp.exp(scores - lse_ref[span, head : head + 1])
            grad_prob = mm_cols(upstream, values)
            inner = jnp.sum(probability * grad_prob, axis=-1, keepdims=True)
            grad_scores = (probability * (grad_prob - inner)).astype(LOW)
            dv_ref[:, low:high] += mm_rows(probability.astype(LOW), upstream)
            dk_ref[:, low:high] += mm_rows(grad_scores, queries)
            dq_ref[span, low:high] += mm(grad_scores, keys_masked)
    dq = (dq_ref[...] * scaling).astype(LOW)
    dv = dv_ref[...].astype(LOW)
    grad_ref[:, :width] = dq
    grad_ref[:, width : 2 * width] = (dk_ref[...] * scaling).astype(LOW)
    grad_ref[:, 2 * width :] = dv
    q_bias_ref[...] = jnp.sum(dq.astype(FULL), axis=0, keepdims=True)
    v_bias_ref[...] = jnp.sum(dv.astype(FULL), axis=0, keepdims=True)
    for rank in range(ranks):
        leave_ref[rank] = mm_cols(grad_ref[rank * block : (rank + 1) * block], proj_ref[...]).astype(LOW)


def attend_backward(qkv, upstream, lse, proj, ranks):
    _, tokens, width = qkv.shape
    heads = width // HEAD_DIM
    model = proj.shape[0]
    return pl.pallas_call(
        attend_backward_kernel,
        out_shape=(
            jax.ShapeDtypeStruct((tokens, 3 * width), LOW),
            jax.ShapeDtypeStruct((ranks, tokens // ranks, model), LOW),
            jax.ShapeDtypeStruct((1, width), FULL),
            jax.ShapeDtypeStruct((1, width), FULL),
        ),
        in_specs=[pl.BlockSpec(memory_space=pltpu.VMEM)] * 4,
        out_specs=(pl.BlockSpec(memory_space=pltpu.VMEM),) * 4,
        scratch_shapes=[pltpu.VMEM((tokens, width), FULL)] * 3 + [pltpu.VMEM((tokens, width), LOW)],
        compiler_params=pltpu.CompilerParams(vmem_limit_bytes=24 << 20),
        cost_estimate=HEAVY,
        name="attend_backward",
    )(qkv, upstream, lse, proj)


def attn_share_kernel(me_ref, out_w_ref, qkv_ref, *refs, layers, with_small, ranks):
    out_ref = refs[-1]
    part, width = out_w_ref.shape
    slab = width // ranks
    out_ref[:part, :width] = out_w_ref[...]
    for rank in range(ranks):

        @pl.when(me_ref[0] == rank)
        def _():
            for i in range(3):
                source = (i * ranks + rank) * slab
                target = width + i * slab
                out_ref[:part, target : target + slab] = qkv_ref[:, source : source + slab]

    if with_small:
        out_ref[part:, :] = jnp.zeros((out_ref.shape[0] - part, out_ref.shape[1]), LOW)
        for layer in range(layers):
            target = 0
            for ref in refs[:-1]:
                count = ref.shape[-1]
                for row in range(ref.shape[0] // layers):
                    source = layer * (ref.shape[0] // layers) + row
                    out_ref[part + layer : part + layer + 1, target : target + count] = ref[source : source + 1, :]
                    target += count


def attn_share(me, out_w, qkv_w, small, layers, ranks):
    part, width = out_w.shape
    rows = part + 8 * (len(small) > 0)
    return pl.pallas_call(
        functools.partial(attn_share_kernel, layers=layers, with_small=len(small) > 0, ranks=ranks),
        out_shape=jax.ShapeDtypeStruct((rows, width + 3 * width // ranks), LOW),
        in_specs=[pl.BlockSpec(memory_space=pltpu.SMEM)]
        + [pl.BlockSpec(memory_space=pltpu.VMEM)] * (2 + len(small)),
        out_specs=pl.BlockSpec(memory_space=pltpu.VMEM),
        compiler_params=pltpu.CompilerParams(vmem_limit_bytes=16 << 20),
        cost_estimate=LIGHT,
        name="attn_share",
    )(me.reshape(1), out_w, qkv_w, *small)


def share_kernel(side_ref, up_ref, down_ref, out_ref, *, owners, layer, half):
    part = up_ref.shape[0]
    hidden_part, _, width = down_ref.shape
    flank = owners // 2 * half
    out_ref[...] = jnp.zeros_like(out_ref)
    for side in range(2):

        @pl.when(side_ref[0] == side)
        def _():
            first = side * half
            count = min(half, hidden_part - first)
            out_ref[:count, :width] = down_ref[first : first + count, layer, :]
            for owner in range(owners):
                source = owner * hidden_part + first
                target = width + owner * half - (owner >= owners // 2) * flank
                row = (owner >= owners // 2) * part
                out_ref[row : row + part, target : target + count] = up_ref[:, source : source + count]


def feed_share(side, up, down, layer, owners, half):
    part, (hidden_part, _, width) = up.shape[0], down.shape
    lanes = width + -(-owners // 2 * half // 128) * 128
    return pl.pallas_call(
        functools.partial(share_kernel, owners=owners, layer=layer, half=half),
        out_shape=jax.ShapeDtypeStruct((max(2 * part, half), lanes), LOW),
        in_specs=[pl.BlockSpec(memory_space=pltpu.SMEM)] + [pl.BlockSpec(memory_space=pltpu.VMEM)] * 2,
        out_specs=pl.BlockSpec(memory_space=pltpu.VMEM),
        compiler_params=pltpu.CompilerParams(vmem_limit_bytes=16 << 20),
        cost_estimate=LIGHT,
        name="feed_share",
    )(side.reshape(1), up, down)


def local_call(kernel, name, out_shape, *operands, scalars=(), scratch=(), cost=HEAVY):
    return pl.pallas_call(
        kernel,
        out_shape=out_shape,
        in_specs=[pl.BlockSpec(memory_space=pltpu.SMEM)] * len(scalars)
        + [pl.BlockSpec(memory_space=pltpu.VMEM)] * len(operands),
        out_specs=jax.tree.map(lambda _: pl.BlockSpec(memory_space=pltpu.VMEM), out_shape),
        scratch_shapes=list(scratch),
        compiler_params=pltpu.CompilerParams(vmem_limit_bytes=24 << 20),
        cost_estimate=cost,
        name=name,
    )(*[s.reshape(1) for s in scalars], *operands)


def grad_kernel(*refs, owners, pieces, total, split):
    refs = list(refs)
    core_ref = refs.pop(0) if split else None
    operands = []
    for lefts, rights, turned, target in pieces:
        operands.append(([refs.pop(0) for _ in range(lefts)], [refs.pop(0) for _ in range(rights)], turned, target))
    outs = [refs.pop(0) for _ in range(2 if split else 1)]
    filled = []
    for lefts, rights, turned, target in operands:
        left_ref, right_ref = refs.pop(0), refs.pop(0)
        start = 0
        for ref in lefts:
            count = ref.shape[1 if turned else 0]
            left_ref[:, start : start + count] = ref[...] if turned else ref[...].T
            start += count
        start = 0
        for ref in rights:
            right_ref[start : start + ref.shape[0]] = ref[...]
            start += ref.shape[0]
        filled.append((left_ref, right_ref, target, target + right_ref.shape[1]))
    ends = [f[2] for f in filled[1:]] + [total]
    for (left_ref, right_ref, target, stop), end in zip(filled, ends, strict=True):
        if end > stop:
            for out in outs:
                out[..., stop:end] = jnp.zeros(out.shape[:-1] + (end - stop,), LOW)
        rows = left_ref.shape[0] // owners
        width = right_ref.shape[1]
        for start in range(0, width, 256):
            size = min(256, width - start)
            value = mm(left_ref[...], right_ref[:, start : start + size]).astype(LOW)
            if not split:
                outs[0][:, target + start : target + start + size] = value
                continue
            for core in range(2):

                @pl.when(core_ref[0] == core)
                def _():
                    for owner in range(owners):
                        out = outs[(owner % 2 != core) * 1]
                        out[owner // 2, :, target + start : target + start + size] = value[
                            owner * rows : (owner + 1) * rows
                        ]


def weight_grad(pieces, owners, total, core=None, cost=HEAVY):
    split = core is not None
    operands, shapes, scratch = [], [], []
    for lefts, rights, turned, target in pieces:
        operands += [*lefts, *rights]
        shapes.append((len(lefts), len(rights), turned, target))
        rows = lefts[0].shape[0 if turned else 1]
        tokens = sum(r.shape[0] for r in rights)
        scratch += [pltpu.VMEM((rows, tokens), LOW), pltpu.VMEM((tokens, rights[0].shape[1]), LOW)]
    out = jax.ShapeDtypeStruct((owners // 2, rows // owners, total) if split else (rows, total), LOW)
    return local_call(
        functools.partial(grad_kernel, owners=owners, pieces=shapes, total=total, split=split),
        "weight_grad",
        (out, out) if split else out,
        *operands,
        scalars=(core,) if split else (),
        scratch=scratch,
        cost=cost,
    )


def spread_kernel(all_ref, out_ref, qkv_ref, *small):
    owners, _, _ = all_ref.shape
    width = out_ref.shape[1]
    part = out_ref.shape[0] // owners
    for owner in range(owners):
        rows = slice(owner * part, (owner + 1) * part)
        out_ref[rows] = all_ref[owner, :part, :width]
        qkv_ref[rows] = all_ref[owner, :part, width:]
        for ref in small:
            ref[owner] = all_ref[owner, part:, :]


def spread(gathered, part, width):
    owners, rows, columns = gathered.shape
    return local_call(
        spread_kernel,
        "spread",
        [
            jax.ShapeDtypeStruct((owners * part, width), LOW),
            jax.ShapeDtypeStruct((owners * part, columns - width), LOW),
        ]
        + [jax.ShapeDtypeStruct((owners, rows - part, columns), LOW)] * (rows > part),
        gathered,
        cost=LIGHT,
    )


def unit_tiles(owners, half):
    flank = owners // 2 * half
    return [
        (side * flank + start, min(512, flank - start), side, start)
        for side in range(2)
        for start in range(0, flank, 512)
    ]


def up_tile(feed_ref, tile, part, width):
    _, count, side, start = tile
    lanes = slice(width + start, width + start + count)
    rows = slice(side * part, (side + 1) * part)
    return jnp.concatenate([feed_ref[owner, rows, lanes] for owner in range(feed_ref.shape[0])], axis=0)


def down_tile(feed_ref, tile, half, width):
    first, count, _, _ = tile
    pieces = []
    while count:
        owner, row = divmod(first, half)
        size = min(count, half - row)
        pieces.append(feed_ref[owner, row : row + size, :width])
        first, count = first + size, count - size
    return jnp.concatenate(pieces, axis=0)


GELU_SCALE = (2 / math.pi) ** 0.5


def feed_forward_kernel(mine_ref, other_ref, feed_ref, bias_ref, pre_ref, act_ref, *refs, half):
    tokens, width = mine_ref.shape
    owners = feed_ref.shape[0]
    part = width // owners
    both = jnp.concatenate([mine_ref[...], other_ref[...]], axis=0)
    if refs:
        keep_ref, leave_ref, acc_ref = refs
        acc_ref[...] = jnp.zeros_like(acc_ref)
    for tile in unit_tiles(owners, half):
        span = slice(tile[0], tile[0] + tile[1])
        pre = mm(both, up_tile(feed_ref, tile, part, width)) + bias_ref[:, span]
        pre_ref[:, span] = pre
        act = (0.5 * pre * (1 + jnp.tanh(GELU_SCALE * (pre + 0.044715 * (pre * pre * pre))))).astype(LOW)
        act_ref[:, span] = act
        if refs:
            acc_ref[...] += mm(act, down_tile(feed_ref, tile, half, width))
    if refs:
        keep_ref[...] = acc_ref[:tokens]
        leave_ref[...] = acc_ref[tokens:].astype(LOW)


def feed_forward(mine, other, feed, bias, half, mixed):
    tokens, width = mine.shape
    units = feed.shape[0] * half
    shapes = [jax.ShapeDtypeStruct((2 * tokens, units), FULL), jax.ShapeDtypeStruct((2 * tokens, units), LOW)]
    if mixed:
        shapes += [jax.ShapeDtypeStruct((tokens, width), FULL), jax.ShapeDtypeStruct((tokens, width), LOW)]
    return local_call(
        functools.partial(feed_forward_kernel, half=half),
        "feed_forward",
        shapes,
        mine,
        other,
        feed,
        bias,
        scratch=[pltpu.VMEM((2 * tokens, width), FULL)] * mixed,
    )


def feed_out_kernel(act_ref, feed_ref, keep_ref, leave_ref, acc_ref, *, half):
    tokens, width = keep_ref.shape
    acc_ref[...] = jnp.zeros_like(acc_ref)
    for tile in unit_tiles(feed_ref.shape[0], half):
        acc_ref[...] += mm(act_ref[:, tile[0] : tile[0] + tile[1]], down_tile(feed_ref, tile, half, width))
    keep_ref[...] = acc_ref[:tokens]
    leave_ref[...] = acc_ref[tokens:].astype(LOW)


def feed_out(act, feed, width, half):
    tokens = act.shape[0] // 2
    return local_call(
        functools.partial(feed_out_kernel, half=half),
        "feed_out",
        (jax.ShapeDtypeStruct((tokens, width), FULL), jax.ShapeDtypeStruct((tokens, width), LOW)),
        act,
        feed,
        scratch=[pltpu.VMEM((2 * tokens, width), FULL)],
    )


def feed_backward_kernel(
    mine_ref, other_ref, pre_ref, feed_ref, low_ref, grad_ref, keep_ref, leave_ref, bias_ref, acc_ref, *, half
):
    tokens, width = mine_ref.shape
    owners = feed_ref.shape[0]
    part = width // owners
    low_ref[:tokens] = mine_ref[...]
    low_ref[tokens:] = other_ref[...]
    acc_ref[...] = jnp.zeros_like(acc_ref)
    for tile in unit_tiles(owners, half):
        span = slice(tile[0], tile[0] + tile[1])
        pre = pre_ref[:, span]
        square = pre * pre
        bend = jnp.tanh(GELU_SCALE * (pre + 0.044715 * pre * square))
        slope = 0.5 * (1 + bend) + 0.5 * pre * (1 - bend * bend) * (GELU_SCALE * (1 + 3 * 0.044715 * square))
        grad = mm_cols(low_ref[...], down_tile(feed_ref, tile, half, width)) * slope
        bias_ref[:, span] = jnp.sum(grad, axis=0, keepdims=True)
        grad = grad.astype(LOW)
        grad_ref[:, span] = grad
        acc_ref[...] += mm_cols(grad, up_tile(feed_ref, tile, part, width))
    keep_ref[...] = acc_ref[:tokens]
    leave_ref[...] = acc_ref[tokens:].astype(LOW)


def feed_backward(mine, other, pre_act, feed, half):
    tokens, width = mine.shape
    units = pre_act.shape[1]
    return local_call(
        functools.partial(feed_backward_kernel, half=half),
        "feed_backward",
        (
            jax.ShapeDtypeStruct((2 * tokens, width), LOW),
            jax.ShapeDtypeStruct((2 * tokens, units), LOW),
            jax.ShapeDtypeStruct((tokens, width), FULL),
            jax.ShapeDtypeStruct((tokens, width), LOW),
            jax.ShapeDtypeStruct((1, units), FULL),
        ),
        mine,
        other,
        pre_act,
        feed,
        scratch=[pltpu.VMEM((2 * tokens, width), FULL)],
    )


def mid_backward_kernel(
    side_ref, keep_ref, got_ref, normed_ref, inverse_ref, gain_ref, grad_ref, proj_ref, *outs
):
    after_ref, send_ref, mine_ref, other_ref, g_gain_ref, g_bias_ref, g_out_ref, g_down_ref = outs
    upstream = keep_ref[...] + got_ref[...].astype(FULL)
    grad = grad_ref[...]
    back, g_gain, g_bias = normalize_back(upstream, normed_ref[...], inverse_ref[...], gain_ref[...])
    after = grad + back
    after_ref[...] = after
    g_gain_ref[...] = g_gain
    g_bias_ref[...] = g_bias
    g_out_ref[...] = jnp.sum(after, axis=0, keepdims=True)
    g_down_ref[...] = jnp.sum(grad, axis=0, keepdims=True)
    low = after.astype(LOW)
    flank = mine_ref.shape[1]
    for side in range(2):

        @pl.when(side_ref[0] == side)
        def _():
            mine_ref[...] = low[:, side * flank : (side + 1) * flank]
            other_ref[...] = low[:, (1 - side) * flank : (2 - side) * flank]

    ranks, slab, _ = send_ref.shape
    for rank in range(ranks):
        send_ref[rank] = mm_cols(proj_ref[rank * slab : (rank + 1) * slab, :], low).astype(LOW)


def mid_backward(side, keep, got, normed, inverse, gain, grad, proj, ranks):
    tokens, width = keep.shape
    row = jax.ShapeDtypeStruct((1, width), FULL)
    half = jax.ShapeDtypeStruct((tokens, width // 2), LOW)
    return local_call(
        mid_backward_kernel,
        "mid_backward",
        (
            jax.ShapeDtypeStruct((tokens, width), FULL),
            jax.ShapeDtypeStruct((ranks, width // ranks, tokens), LOW),
            half,
            half,
            row,
            row,
            row,
            row,
        ),
        keep,
        got,
        normed,
        inverse,
        gain,
        grad,
        proj,
        scalars=(side,),
    )


def end_backward_kernel(got_ref, normed_ref, inverse_ref, gain_ref, after_ref, out_ref, low_ref, g_gain_ref, g_bias_ref):
    upstream = got_ref[0].astype(FULL)
    for rank in range(1, got_ref.shape[0]):
        upstream += got_ref[rank].astype(FULL)
    back, g_gain, g_bias = normalize_back(upstream, normed_ref[...], inverse_ref[...], gain_ref[...])
    total = after_ref[...] + back
    out_ref[...] = total
    low_ref[...] = total.astype(LOW)
    g_gain_ref[...] = g_gain
    g_bias_ref[...] = g_bias


def end_backward(got, normed, inverse, gain, after):
    tokens, width = after.shape
    row = jax.ShapeDtypeStruct((1, width), FULL)
    return local_call(
        end_backward_kernel,
        "end_backward",
        (
            jax.ShapeDtypeStruct((tokens, width), FULL),
            jax.ShapeDtypeStruct((tokens, width), LOW),
            row,
            row,
        ),
        got,
        normed,
        inverse,
        gain,
        after,
    )


def meet_kernel(chip_ref, keep_ref, got_ref, *outs):
    step = pl.program_id(0)
    for j, out in enumerate(outs):

        @pl.when(step == j)
        def _():
            out[...] = (keep_ref[0].astype(FULL) + got_ref[0].astype(FULL)).astype(LOW)


def meet_cores(chip, keep, got):
    chips, rows, columns = keep.shape
    block = pl.BlockSpec((1, rows, columns), lambda j, chip_ref: (chip_ref[0] ^ j, 0, 0))
    return pl.pallas_call(
        meet_kernel,
        grid_spec=pltpu.PrefetchScalarGridSpec(
            num_scalar_prefetch=1,
            grid=(chips,),
            in_specs=[block, block],
            out_specs=[pl.BlockSpec((rows, columns), lambda j, chip_ref: (0, 0))] * chips,
        ),
        out_shape=[jax.ShapeDtypeStruct((rows, columns), LOW)] * chips,
        compiler_params=pltpu.CompilerParams(vmem_limit_bytes=24 << 20),
        cost_estimate=LIGHT,
        name="meet_cores",
    )(chip.reshape(1), keep, got)


def add_kernel(*refs):
    total = refs[0][...].astype(FULL)
    for ref in refs[1:-1]:
        total += ref[...].astype(FULL)
    refs[-1][...] = total.astype(LOW)


def add_all(*values, cost=LIGHT):
    return local_call(add_kernel, "add_all", jax.ShapeDtypeStruct(values[0].shape, LOW), *values, cost=cost)


def up_kernel(side_ref, own_ref, across_ref, *refs, owners, half):
    out_ref = refs[-1]
    hidden_part = out_ref.shape[2] // owners
    for mine in range(2):

        @pl.when(side_ref[0] == mine)
        def _():
            for side in range(2):
                ref = own_ref if side == mine else across_ref
                first = side * half
                count = min(half, hidden_part - first)
                for owner in range(owners):
                    target = owner * hidden_part + first
                    source = owner * half
                    out_ref[0, :, target : target + count] = ref[:, source : source + count].astype(FULL)


def mixed_kernel(me_ref, own_ref, across_ref, *refs, ranks, offset):
    qkv_out, out_out = refs[-2:]
    width = out_out.shape[2]
    slab, flank, pairs = width // ranks, width // 2, ranks // 2
    for me in range(ranks):

        @pl.when(me_ref[0] == me)
        def _():
            side, pair = me % 2, me // 2
            for flip, ref in enumerate((own_ref, across_ref)):
                for j in range(pairs):
                    rank = (pair - j) % pairs * 2 + (side ^ flip)
                    for i in range(3):
                        target = (i * ranks + rank) * slab
                        source = j * offset + i * slab
                        qkv_out[0, :, target : target + slab] = ref[:, source : source + slab].astype(FULL)
                target = (side ^ flip) * flank
                out_out[0, :, target : target + flank] = ref[:, pairs * offset :].astype(FULL)


def write_layer(kernel, name, layer, layers, shapes, earlier, scalar, *values):
    return pl.pallas_call(
        kernel,
        grid=(1,),
        out_shape=tuple(jax.ShapeDtypeStruct((layers,) + s, FULL) for s in shapes),
        in_specs=[pl.BlockSpec(memory_space=pltpu.SMEM)]
        + [pl.BlockSpec(v.shape, lambda i: (0, 0)) for v in values]
        + [pl.BlockSpec(memory_space=pl.ANY)] * len(earlier),
        out_specs=tuple(pl.BlockSpec((1,) + s, lambda i: (layer, 0, 0)) for s in shapes),
        input_output_aliases={1 + len(values) + i: i for i in range(len(earlier))},
        compiler_params=pltpu.CompilerParams(vmem_limit_bytes=40 << 20),
        cost_estimate=cost_of(name + str(layer)),
        name=name,
    )(scalar.reshape(1), *values, *earlier)


def down_kernel(side_ref, *refs):
    out_ref = refs[-1]
    half = refs[0].shape[0]
    hidden_part = out_ref.shape[0]
    for mine in range(2):

        @pl.when(side_ref[0] == mine)
        def _():
            for layer in range(len(refs) // 2):
                for side in range(2):
                    ref = refs[2 * layer + (side != mine)]
                    first = side * half
                    count = min(half, hidden_part - first)
                    out_ref[first : first + count, layer, :] = ref[:count].astype(FULL)


def pack_kernel(side_ref, *refs, owners, layers, half):
    out_ref = refs[-1]
    each = len(refs) // layers
    out_ref[...] = jnp.zeros_like(out_ref)
    target = 0
    for layer in range(layers):
        rows = refs[layer * each : (layer + 1) * each]
        for ref in rows[:-1]:
            part = ref.shape[1] // owners
            for owner in range(owners):
                out_ref[owner : owner + 1, target : target + part] = ref[:, owner * part : (owner + 1) * part]
            target += part
        for side in range(2):

            @pl.when(side_ref[0] == side)
            def _():
                for owner in range(owners):
                    first = target + side * half
                    out_ref[owner : owner + 1, first : first + half] = rows[-1][
                        :, owner * half : (owner + 1) * half
                    ]

        target += 2 * half


def unpack_kernel(first_ref, second_ref, *outs, layers, half):
    values = first_ref[...] + second_ref[...]
    part = outs[0].shape[1]
    target = 0
    for layer in range(layers):
        for out in outs[:-1]:
            out[layer : layer + 1, :] = values[:, target : target + part]
            target += part
        out = outs[-1]
        out[layer : layer + 1, :] = values[:, target : target + out.shape[1]]
        target += 2 * half


class Order:
    def __init__(self):
        self.last = ()

    def enter(self, *values):
        if not self.last:
            return values
        return lax.optimization_barrier(tuple(values) + self.last)[: len(values)]

    def leave(self, *values):
        self.last = tuple(values)


class Chain:
    def __init__(self, steps):
        self.steps = steps
        self.result = None
        self.step()

    def step(self):
        try:
            next(self.steps)
        except StopIteration as stop:
            self.result = stop.value


def make_body(ranks, owners):
    pairs, chips = ranks // 2, owners // 2

    def shift(value, step):
        return lax.ppermute(value, "seq", [(i, (i + step) % ranks) for i in range(ranks)])

    def swap(value):
        return lax.ppermute(value, "seq", [(i, i ^ 1) for i in range(ranks)])

    def pair_shift(value, step):
        return lax.ppermute(value, "seq", [(i, (i + 2 * step) % ranks) for i in range(ranks)])

    def owner_xor(value, bits):
        return lax.ppermute(value, "fsdp", [(i, i ^ bits) for i in range(owners)])

    def exchange(blocks):
        return lax.all_to_all(blocks, "seq", split_axis=0, concat_axis=0, tiled=True)

    def body(
        block_input,
        grad_output,
        attn_norm_gain,
        attn_norm_bias,
        qkv_weight,
        qv_bias,
        out_weight,
        out_bias,
        mlp_norm_gain,
        mlp_norm_bias,
        up_weight,
        up_bias,
        down_weight,
        down_bias,
    ):
        layers = qkv_weight.shape[0]
        tokens, width = block_input.shape[1:]
        slab, flank = width // ranks, width // 2
        part = qkv_weight.shape[1]
        hidden_part = down_weight.shape[1]
        half = -(-hidden_part // 32) * 16
        me = lax.axis_index("seq")
        owner = lax.axis_index("fsdp")
        core, chip = owner % 2, owner // 2
        side, pair = me % 2, me // 2

        def at(value, index, axis=0):
            return lax.dynamic_index_in_dim(value, index, axis, keepdims=False)

        def put(value, block, *index):
            return lax.dynamic_update_slice(
                value, block.reshape((1,) * len(index) + block.shape), index + (0,) * block.ndim
            )

        def rank_at(j):
            return (me + j) % ranks

        order = Order()

        def owner_steps(keep, send, tag):
            got = owner_xor(send, 1)
            yield
            (got,) = order.enter(got)
            mine, *sends = meet_cores(chip, keep, got)
            order.leave(*sends)
            got = [owner_xor(send, 2 * j) for j, send in enumerate(sends, 1)]
            yield
            return add_all(mine, *order.enter(*got), cost=cost_of("sum_" + tag))

        def queue_steps(value):
            value = lax.psum_scatter(value, "fsdp", scatter_dimension=0, tiled=True)
            yield
            return order.enter(value)[0]

        def pair_steps(value, tag):
            order.leave(value)
            got = [pair_shift(value, j) for j in range(1, pairs)]
            yield
            own = add_all(value, *order.enter(*got), cost=cost_of("add_" + tag))
            order.leave(own)
            across = swap(own)
            yield
            return own, order.enter(across)[0]

        def mixed_steps(value, tag):
            order.leave(value)
            got = [pair_shift(value, j) for j in range(1, pairs)]
            yield
            got = order.enter(*got)
            total = add_all(*[v[:, offset:] for v in (value, *got)], cost=cost_of("add_" + tag))
            shares = [v[:, :offset] for v in (value, *got)]
            send = jnp.concatenate([*shares, total], axis=1)
            order.leave(send)
            across = swap(send)
            yield
            (across,) = order.enter(across)
            return send, across

        def written(steps, stage, write, tag):
            value = yield from steps
            value = yield from stage(value, tag)
            value = write(*value)
            order.leave(*value)
            return value

        columns = width + 3 * slab
        offset = -(-3 * slab // 128) * 128

        def gather_tokens(mine):
            return exchange(jnp.broadcast_to(mine, (ranks,) + mine.shape))

        all_input = gather_tokens(block_input[0])
        small = (
            attn_norm_gain,
            attn_norm_bias,
            qv_bias.reshape(2 * layers, part),
            out_bias,
            mlp_norm_gain,
            mlp_norm_bias,
            down_bias,
            up_bias,
        )
        down_turned = down_weight.transpose(1, 0, 2)

        attn_shares, feeds = [], []
        for layer in range(layers):
            share = attn_share(
                me, out_weight[layer], *order.enter(qkv_weight[layer]), small if layer == 0 else (), layers, ranks
            )
            order.leave(share)
            attn_shares.append(lax.all_gather(share, "fsdp", axis=0))
            share = feed_share(side, *order.enter(up_weight[layer]), down_turned, layer, owners, half)
            order.leave(share)
            feeds.append(lax.all_gather(share, "fsdp", axis=0))
        (all_input,) = order.enter(all_input)
        normed_all, _ = normalize(all_input.reshape(ranks * tokens, width).astype(FULL))
        order.leave(normed_all)
        *weights, small_all = spread(*order.enter(attn_shares[0]), part, width)
        order.leave(*weights, small_all)
        rows_all = small_all[:, :layers, : 8 * part].reshape(owners, layers, 8, part)
        rows_all = rows_all.transpose(1, 2, 0, 3).reshape(layers, 8, width).astype(FULL)
        up_all = small_all[:, :layers, 8 * part : 8 * part + hidden_part].astype(FULL)
        up_all = jnp.pad(up_all, ((0, 0), (0, 0), (0, 2 * half - hidden_part)))

        vectors = []
        for layer in range(layers):
            rows = rows_all[layer]
            vectors.append(
                dict(
                    gain_one=rows[0],
                    bias_one=rows[1],
                    bias_q=lax.dynamic_slice(rows[2], (me * slab,), (slab,)),
                    bias_v=lax.dynamic_slice(rows[3], (me * slab,), (slab,)),
                    bias_out=rows[4],
                    gain_two=rows[5],
                    bias_two=rows[6],
                    bias_down=rows[7],
                    bias_up=lax.dynamic_slice(
                        up_all[:, layer], (0, side * half), (owners, half)
                    ).reshape(owners * half),
                )
            )

        hidden = block_input[0].astype(FULL)
        stored = []
        for layer in range(layers):
            v = vectors[layer]
            last_layer = layer == layers - 1
            normed_one, inverse_one = normalize(hidden)
            if layer == 0:
                attn_in = (normed_all * v["gain_one"] + v["bias_one"]).astype(LOW)
            else:
                attn_mine = (normed_one * v["gain_one"] + v["bias_one"]).astype(LOW)
                order.leave(attn_mine)
                attn_in = gather_tokens(attn_mine)
                weights = spread(*order.enter(attn_shares[layer]), part, width)
                order.leave(*weights)
                attn_in = order.enter(attn_in)[0].reshape(ranks * tokens, width)
            proj_out, proj_qkv = weights
            bias_row = jnp.concatenate([v["bias_q"], jnp.zeros((slab,), FULL), v["bias_v"]])
            projected = (mm(attn_in, proj_qkv) + bias_row).astype(LOW)
            qkv = jnp.stack([projected[:, i * slab : (i + 1) * slab] for i in range(3)])
            out_heads, lse = attend_forward(qkv, ranks)
            order.leave(out_heads)
            attended = order.enter(exchange(out_heads))[0].reshape(width, tokens)
            after_attn = hidden + mm_rows(attended, proj_out) + v["bias_out"]
            normed_two, inverse_two = normalize(after_attn)
            mlp_mine = (normed_two * v["gain_two"] + v["bias_two"]).astype(LOW)
            order.leave(mlp_mine)
            mlp_other = swap(mlp_mine)
            attended_other = swap(order.enter(attended)[0])
            mlp_other, attended_other = order.enter(mlp_other, attended_other)
            (feed,) = order.enter(feeds[layer])
            pre_act, activated, *mixed = feed_forward(
                mlp_mine, mlp_other, feed, v["bias_up"].reshape(1, owners * half), half, not last_layer
            )
            if last_layer:
                order.leave(pre_act, activated)
            else:
                mixed, leaving = mixed
                order.leave(leaving)
                (other,) = order.enter(swap(leaving))
                hidden = after_attn + mixed + other.astype(FULL) + v["bias_down"]
            stored.append(
                (
                    (proj_qkv, proj_out, feed),
                    (normed_one, inverse_one, attn_in, qkv, lse, attended, attended_other),
                    (normed_two, inverse_two, mlp_mine, mlp_other, pre_act, activated),
                )
            )

        def writer(key, kernel, layer, scalar, *shapes):
            def write(*values):
                outs[key] = write_layer(
                    kernel, "write_" + key, layer, layers, shapes, outs[key], scalar, *values
                )
                return outs[key]

            return write

        def held(*values):
            return values

        def sum_rows(value):
            return jnp.sum(value, axis=0, keepdims=True)

        grad_hidden, grad_mine = grad_output[0].astype(FULL), grad_output[0]
        small_grads = [None] * layers
        downs = [None] * layers
        outs = dict(up=(), mixed=())
        before = None
        for layer in reversed(range(layers)):
            v = vectors[layer]
            tag = "_late" if before else "_early"
            proj_qkv, proj_out, feed = stored[layer][0]
            normed_one, inverse_one, attn_in, qkv, lse, attended, attended_other = stored[layer][1]
            normed_two, inverse_two, mlp_mine, mlp_other, pre_act, activated = stored[layer][2]
            grad_other = swap(grad_mine)
            if before:
                before["down"].step()
                if PLAN.get("final_early", 0):
                    grad_other, final_other = order.enter(grad_other, final_other)
            (grad_other,) = order.enter(grad_other)
            grad_low, grad_pre_low, mixed, leaving, g_up_bias = feed_backward(
                grad_mine, grad_other, pre_act, feed, half
            )
            order.leave(leaving)
            other = swap(leaving)
            g_down = weight_grad([((activated,), order.enter(grad_low), False, 0)], owners, width)
            order.leave(g_down)
            down_chain = Chain(written(queue_steps(g_down), pair_steps, held, "down" + tag))
            keep, send = weight_grad(
                [((mlp_mine, mlp_other), order.enter(grad_pre_low), False, 0)],
                owners,
                half * owners,
                core,
                cost_of("wgu" + tag),
            )
            order.leave(send)
            up_chain = Chain(
                written(
                    owner_steps(keep, send, "up" + tag),
                    pair_steps,
                    writer(
                        "up",
                        functools.partial(up_kernel, owners=owners, half=half),
                        layer,
                        side,
                        (part, owners * hidden_part),
                    ),
                    "up" + tag,
                )
            )
            (other,) = order.enter(other)
            order.leave(other)
            if before:
                before["up"].step()
            grad_after, sends, after_mine, after_send, g_gain_two, g_bias_two, g_out_bias, g_down_bias = mid_backward(
                side,
                mixed,
                *order.enter(other),
                normed_two,
                inverse_two,
                v["gain_two"].reshape(1, width),
                grad_hidden,
                proj_out,
                ranks,
            )
            order.leave(sends)
            grad_heads = exchange(sends)
            after_other = swap(after_send)
            up_chain.step()
            if PLAN.get("other" + tag, 1):
                grad_heads, after_other = order.enter(grad_heads, after_other)
            else:
                (grad_heads,) = order.enter(grad_heads)
            order.leave(grad_heads)
            if before:
                before["down"].step()
                before["mixed"].step()
            grad_proj, leaving, g_q_bias, g_v_bias = attend_backward(
                qkv, *order.enter(grad_heads), lse, proj_qkv, ranks
            )
            order.leave(leaving)
            arrived = exchange(leaving)
            if before:
                before["up"].step()
            grad_proj, after_other = order.enter(grad_proj, after_other)
            g_mixed = weight_grad(
                [
                    ((attn_in,), (grad_proj,), False, 0),
                    ((attended, attended_other), (after_mine, after_other), True, offset),
                ],
                owners,
                offset + flank,
                core if before else None,
            )
            order.leave(*(g_mixed if before else (g_mixed,)))
            mixed_chain = Chain(
                written(
                    owner_steps(*g_mixed, "mixed" + tag) if before else queue_steps(g_mixed),
                    mixed_steps,
                    writer(
                        "mixed",
                        functools.partial(mixed_kernel, ranks=ranks, offset=offset),
                        layer,
                        me,
                        (part, 3 * width),
                        (part, width),
                    ),
                    "mixed" + tag,
                )
            )
            if before:
                if PLAN.get("sum_in", 1):
                    up_chain.step()
                if PLAN.get("down_in", 1):
                    down_chain.step()
                mixed_chain.step()
            else:
                final, leaving = feed_out(*order.enter(activated), feed, width, half)
                order.leave(leaving)
                final_other = swap(leaving)
            (arrived,) = order.enter(arrived)
            grad_hidden, grad_mine, g_gain_one, g_bias_one = end_backward(
                arrived, normed_one, inverse_one, v["gain_one"].reshape(1, width), grad_after
            )
            order.leave(grad_hidden)
            if before:
                if not PLAN.get("sum_in", 1):
                    up_chain.step()
                if not PLAN.get("down_in", 1):
                    down_chain.step()
                before["mixed"].step()
                before["down"].step()
            else:
                up_chain.step()
            last, before = before, dict(up=up_chain, down=down_chain, mixed=mixed_chain)
            downs[layer] = down_chain

            zeros = jnp.zeros((1, width), FULL)
            small_grads[layer] = (
                g_gain_one,
                g_bias_one,
                lax.dynamic_update_slice(zeros, g_q_bias, (0, me * slab)),
                lax.dynamic_update_slice(zeros, g_v_bias, (0, me * slab)),
                g_out_bias,
                g_gain_two,
                g_bias_two,
                g_down_bias,
                g_up_bias,
            )

        each = 8 * part + 2 * half
        v = vectors[layers - 1]
        small_sum = local_call(
            functools.partial(pack_kernel, owners=owners, layers=layers, half=half),
            "pack_small",
            jax.ShapeDtypeStruct((owners, -(-layers * each // 128) * 128), FULL),
            *order.enter(*[row for grads in small_grads for row in grads]),
            scalars=(side,),
            cost=LIGHT,
        )
        order.leave(small_sum)
        small_sum = lax.all_to_all(small_sum, "fsdp", split_axis=0, concat_axis=0, tiled=True)
        steps = dict(d=before["down"], m=before["mixed"], u=before["up"], w=last["mixed"])
        for key in PLAN.get("tail", "udwm"):
            steps[key].step()
        small_sum = sum_rows(order.enter(small_sum)[0])
        order.leave(small_sum)
        total = small_sum
        for j in range(1, pairs):
            total = total + pair_shift(small_sum, j)
        before["up"].step()
        before["mixed"].step()
        before["down"].step()
        (total,) = order.enter(total)
        order.leave(total)
        total_other = swap(total)
        down_out = local_call(
            down_kernel,
            "write_down",
            jax.ShapeDtypeStruct((hidden_part, layers, width), FULL),
            *order.enter(*[piece for chain in downs for piece in chain.result]),
            scalars=(side,),
        )
        order.leave(down_out)
        (final_other,) = order.enter(final_other)
        block_output = (after_attn + final + final_other.astype(FULL) + v["bias_down"]).astype(LOW)[None]
        order.leave(block_output)
        s = local_call(
            functools.partial(unpack_kernel, layers=layers, half=half),
            "unpack_small",
            tuple(jax.ShapeDtypeStruct((layers, n), FULL) for n in [part] * 8 + [hidden_part]),
            *order.enter(total, total_other),
        )
        order.leave(*s)
        before["mixed"].step()
        return (
            block_output,
            grad_hidden[None],
            s[0],
            s[1],
            outs["mixed"][0],
            jnp.stack([s[2], s[3]], axis=1),
            outs["mixed"][1],
            s[4],
            s[5],
            s[6],
            outs["up"][0],
            s[8],
            down_out.transpose(1, 0, 2),
            s[7],
        )

    return body


def solution(mesh):
    row, cols, deep = P(None, "fsdp"), P("fsdp", "seq", None), P(None, "fsdp", None)
    last = P(None, None, "fsdp")
    return jax.shard_map(
        make_body(mesh.shape["seq"], mesh.shape["fsdp"]),
        mesh=mesh,
        in_specs=(cols, cols, row, row, deep, last, deep, row, row, row, deep, row, deep, row),
        out_specs=(cols, cols, row, row, deep, last, deep, row, row, row, deep, row, deep, row),
        check_vma=False,
    )
```

```python
import functools
import math

import jax
import jax.numpy as jnp
from jax import lax
from jax.experimental import pallas as pl
from jax.experimental.pallas import tpu as pltpu
from jax.sharding import PartitionSpec as P

HEAD_DIM = 72
EPSILON = 1e-06
LOW = jnp.bfloat16
FULL = jnp.float32
HEAVY = pl.CostEstimate(flops=20_000_000_000, transcendentals=0, bytes_accessed=1)
MEDIUM = pl.CostEstimate(flops=2_300_000_000, transcendentals=0, bytes_accessed=1)
LIGHT = pl.CostEstimate(flops=1, transcendentals=0, bytes_accessed=1)
PLAN = {"final_early": 1, "other_late": 0, "sum_up_late": 1, "add_up_early": 1, "add_mixed_early": 1}


def cost_of(name):
    return HEAVY if PLAN.get(name, 0) else LIGHT


def normalize(hidden):
    center = hidden - jnp.mean(hidden, axis=-1, keepdims=True)
    variance = jnp.mean(center * center, axis=-1, keepdims=True)
    inverse_std = lax.rsqrt(variance + EPSILON)
    return center * inverse_std, inverse_std


def normalize_back(upstream, normed, inverse_std, gain):
    scaled = upstream * gain
    grad_hidden = inverse_std * (
        scaled
        - jnp.mean(scaled, axis=-1, keepdims=True)
        - normed * jnp.mean(scaled * normed, axis=-1, keepdims=True)
    )
    return (
        grad_hidden,
        jnp.sum(upstream * normed, axis=0, keepdims=True),
        jnp.sum(upstream, axis=0, keepdims=True),
    )


def tangent_gelu(values):
    return jax.nn.gelu(values, approximate=True)


def gelu_back(values, upstream):
    return jax.vjp(tangent_gelu, values)[1](upstream)[0]


def mm(left, right):
    return jnp.dot(left, right, preferred_element_type=FULL)


def mm_rows(left, right):
    return lax.dot_general(left, right, (((0,), (0,)), ((), ())), preferred_element_type=FULL)


def mm_cols(left, right):
    return lax.dot_general(left, right, (((1,), (1,)), ((), ())), preferred_element_type=FULL)


def head_window(head, width):
    low = head * HEAD_DIM // 128 * 128
    high = min(-(-(head + 1) * HEAD_DIM // 128) * 128, width)
    return low, high


def head_mask(head, low, high):
    lane = lax.broadcasted_iota(jnp.int32, (1, high - low), 1) + low
    return (lane >= head * HEAD_DIM) & (lane < (head + 1) * HEAD_DIM)


def attend_forward_kernel(qkv_ref, o_ref, lse_ref, acc_ref):
    tokens, width = acc_ref.shape
    rows = min(256, tokens)
    scaling = HEAD_DIM ** (-0.5)
    acc_ref[...] = jnp.zeros_like(acc_ref)
    for head in range(width // HEAD_DIM):
        low, high = head_window(head, width)
        mask = head_mask(head, low, high)
        keys = qkv_ref[1, :, low:high]
        values = jnp.where(mask, qkv_ref[2, :, low:high], jnp.zeros((), LOW))
        for start in range(0, tokens, rows):
            queries = jnp.where(mask, qkv_ref[0, start : start + rows, low:high], jnp.zeros((), LOW))
            scores = mm_cols(queries, keys) * scaling
            peak = jnp.max(scores, axis=-1, keepdims=True)
            total = jnp.sum(jnp.exp(scores - peak), axis=-1, keepdims=True)
            lse = peak + jnp.log(total)
            probability = jnp.exp(scores - lse).astype(LOW)
            acc_ref[start : start + rows, low:high] += mm(probability, values)
            lse_ref[start : start + rows, head : head + 1] = lse
    ranks, _, block = o_ref.shape
    for rank in range(ranks):
        o_ref[rank] = acc_ref[rank * block : (rank + 1) * block].astype(LOW).T


def attend_forward(qkv, ranks):
    _, tokens, width = qkv.shape
    heads = width // HEAD_DIM
    return pl.pallas_call(
        attend_forward_kernel,
        out_shape=(
            jax.ShapeDtypeStruct((ranks, width, tokens // ranks), LOW),
            jax.ShapeDtypeStruct((tokens, heads), FULL),
        ),
        in_specs=[pl.BlockSpec(memory_space=pltpu.VMEM)],
        out_specs=(pl.BlockSpec(memory_space=pltpu.VMEM),) * 2,
        scratch_shapes=[pltpu.VMEM((tokens, width), FULL)],
        compiler_params=pltpu.CompilerParams(vmem_limit_bytes=24 << 20),
        cost_estimate=LIGHT,
        name="attend_forward",
    )(qkv)


def attend_backward_kernel(
    qkv_ref, got_ref, lse_ref, proj_ref, grad_ref, leave_ref, q_bias_ref, v_bias_ref, dq_ref, dk_ref, dv_ref, do_ref
):
    tokens, width = do_ref.shape
    ranks, _, block = got_ref.shape
    for rank in range(ranks):
        do_ref[rank * block : (rank + 1) * block] = got_ref[rank].T
    rows = min(256, tokens)
    scaling = HEAD_DIM ** (-0.5)
    for ref in (dq_ref, dk_ref, dv_ref):
        ref[...] = jnp.zeros_like(ref)
    zero = jnp.zeros((), LOW)
    for head in range(width // HEAD_DIM):
        low, high = head_window(head, width)
        mask = head_mask(head, low, high)
        keys = qkv_ref[1, :, low:high]
        values = qkv_ref[2, :, low:high]
        keys_masked = jnp.where(mask, keys, zero)
        for start in range(0, tokens, rows):
            span = slice(start, start + rows)
            queries = jnp.where(mask, qkv_ref[0, span, low:high], zero)
            upstream = jnp.where(mask, do_ref[span, low:high], zero)
            scores = mm_cols(queries, keys) * scaling
            probability = jnp.exp(scores - lse_ref[span, head : head + 1])
            grad_prob = mm_cols(upstream, values)
            inner = jnp.sum(probability * grad_prob, axis=-1, keepdims=True)
            grad_scores = (probability * (grad_prob - inner)).astype(LOW)
            dv_ref[:, low:high] += mm_rows(probability.astype(LOW), upstream)
            dk_ref[:, low:high] += mm_rows(grad_scores, queries)
            dq_ref[span, low:high] += mm(grad_scores, keys_masked)
    dq = (dq_ref[...] * scaling).astype(LOW)
    dv = dv_ref[...].astype(LOW)
    grad_ref[:, :width] = dq
    grad_ref[:, width : 2 * width] = (dk_ref[...] * scaling).astype(LOW)
    grad_ref[:, 2 * width :] = dv
    q_bias_ref[...] = jnp.sum(dq.astype(FULL), axis=0, keepdims=True)
    v_bias_ref[...] = jnp.sum(dv.astype(FULL), axis=0, keepdims=True)
    for rank in range(ranks):
        leave_ref[rank] = mm_cols(grad_ref[rank * block : (rank + 1) * block], proj_ref[...]).astype(LOW)


def attend_backward(qkv, upstream, lse, proj, ranks):
    _, tokens, width = qkv.shape
    heads = width // HEAD_DIM
    model = proj.shape[0]
    return pl.pallas_call(
        attend_backward_kernel,
        out_shape=(
            jax.ShapeDtypeStruct((tokens, 3 * width), LOW),
            jax.ShapeDtypeStruct((ranks, tokens // ranks, model), LOW),
            jax.ShapeDtypeStruct((1, width), FULL),
            jax.ShapeDtypeStruct((1, width), FULL),
        ),
        in_specs=[pl.BlockSpec(memory_space=pltpu.VMEM)] * 4,
        out_specs=(pl.BlockSpec(memory_space=pltpu.VMEM),) * 4,
        scratch_shapes=[pltpu.VMEM((tokens, width), FULL)] * 3 + [pltpu.VMEM((tokens, width), LOW)],
        compiler_params=pltpu.CompilerParams(vmem_limit_bytes=24 << 20),
        cost_estimate=HEAVY,
        name="attend_backward",
    )(qkv, upstream, lse, proj)


def attn_share_kernel(me_ref, out_w_ref, qkv_ref, *refs, layers, with_small, ranks):
    out_ref = refs[-1]
    part, width = out_w_ref.shape
    slab = width // ranks
    out_ref[:part, :width] = out_w_ref[...]
    for rank in range(ranks):

        @pl.when(me_ref[0] == rank)
        def _():
            for i in range(3):
                source = (i * ranks + rank) * slab
                target = width + i * slab
                out_ref[:part, target : target + slab] = qkv_ref[:, source : source + slab]

    if with_small:
        out_ref[part:, :] = jnp.zeros((out_ref.shape[0] - part, out_ref.shape[1]), LOW)
        for layer in range(layers):
            target = 0
            for ref in refs[:-1]:
                count = ref.shape[-1]
                for row in range(ref.shape[0] // layers):
                    source = layer * (ref.shape[0] // layers) + row
                    out_ref[part + layer : part + layer + 1, target : target + count] = ref[source : source + 1, :]
                    target += count


def attn_share(me, out_w, qkv_w, small, layers, ranks):
    part, width = out_w.shape
    rows = part + 8 * (len(small) > 0)
    return pl.pallas_call(
        functools.partial(attn_share_kernel, layers=layers, with_small=len(small) > 0, ranks=ranks),
        out_shape=jax.ShapeDtypeStruct((rows, width + 3 * width // ranks), LOW),
        in_specs=[pl.BlockSpec(memory_space=pltpu.SMEM)]
        + [pl.BlockSpec(memory_space=pltpu.VMEM)] * (2 + len(small)),
        out_specs=pl.BlockSpec(memory_space=pltpu.VMEM),
        compiler_params=pltpu.CompilerParams(vmem_limit_bytes=16 << 20),
        cost_estimate=LIGHT,
        name="attn_share",
    )(me.reshape(1), out_w, qkv_w, *small)


def share_kernel(side_ref, up_ref, down_ref, out_ref, *, owners, layer, half):
    part = up_ref.shape[0]
    hidden_part, _, width = down_ref.shape
    flank = owners // 2 * half
    out_ref[...] = jnp.zeros_like(out_ref)
    for side in range(2):

        @pl.when(side_ref[0] == side)
        def _():
            first = side * half
            count = min(half, hidden_part - first)
            out_ref[:count, :width] = down_ref[first : first + count, layer, :]
            for owner in range(owners):
                source = owner * hidden_part + first
                target = width + owner * half - (owner >= owners // 2) * flank
                row = (owner >= owners // 2) * part
                out_ref[row : row + part, target : target + count] = up_ref[:, source : source + count]


def feed_share(side, up, down, layer, owners, half):
    part, (hidden_part, _, width) = up.shape[0], down.shape
    lanes = width + -(-owners // 2 * half // 128) * 128
    return pl.pallas_call(
        functools.partial(share_kernel, owners=owners, layer=layer, half=half),
        out_shape=jax.ShapeDtypeStruct((max(2 * part, half), lanes), LOW),
        in_specs=[pl.BlockSpec(memory_space=pltpu.SMEM)] + [pl.BlockSpec(memory_space=pltpu.VMEM)] * 2,
        out_specs=pl.BlockSpec(memory_space=pltpu.VMEM),
        compiler_params=pltpu.CompilerParams(vmem_limit_bytes=16 << 20),
        cost_estimate=LIGHT,
        name="feed_share",
    )(side.reshape(1), up, down)


def local_call(kernel, name, out_shape, *operands, scalars=(), scratch=(), cost=HEAVY):
    return pl.pallas_call(
        kernel,
        out_shape=out_shape,
        in_specs=[pl.BlockSpec(memory_space=pltpu.SMEM)] * len(scalars)
        + [pl.BlockSpec(memory_space=pltpu.VMEM)] * len(operands),
        out_specs=jax.tree.map(lambda _: pl.BlockSpec(memory_space=pltpu.VMEM), out_shape),
        scratch_shapes=list(scratch),
        compiler_params=pltpu.CompilerParams(vmem_limit_bytes=24 << 20),
        cost_estimate=cost,
        name=name,
    )(*[s.reshape(1) for s in scalars], *operands)


def grad_kernel(*refs, owners, pieces, total, split):
    refs = list(refs)
    core_ref = refs.pop(0) if split else None
    operands = []
    for lefts, rights, turned, target in pieces:
        operands.append(([refs.pop(0) for _ in range(lefts)], [refs.pop(0) for _ in range(rights)], turned, target))
    outs = [refs.pop(0) for _ in range(2 if split else 1)]
    filled = []
    for lefts, rights, turned, target in operands:
        left_ref, right_ref = refs.pop(0), refs.pop(0)
        start = 0
        for ref in lefts:
            count = ref.shape[1 if turned else 0]
            left_ref[:, start : start + count] = ref[...] if turned else ref[...].T
            start += count
        start = 0
        for ref in rights:
            right_ref[start : start + ref.shape[0]] = ref[...]
            start += ref.shape[0]
        filled.append((left_ref, right_ref, target, target + right_ref.shape[1]))
    ends = [f[2] for f in filled[1:]] + [total]
    for (left_ref, right_ref, target, stop), end in zip(filled, ends, strict=True):
        if end > stop:
            for out in outs:
                out[..., stop:end] = jnp.zeros(out.shape[:-1] + (end - stop,), LOW)
        rows = left_ref.shape[0] // owners
        width = right_ref.shape[1]
        for start in range(0, width, 256):
            size = min(256, width - start)
            value = mm(left_ref[...], right_ref[:, start : start + size]).astype(LOW)
            if not split:
                outs[0][:, target + start : target + start + size] = value
                continue
            for core in range(2):

                @pl.when(core_ref[0] == core)
                def _():
                    for owner in range(owners):
                        out = outs[(owner % 2 != core) * 1]
                        out[owner // 2, :, target + start : target + start + size] = value[
                            owner * rows : (owner + 1) * rows
                        ]


def weight_grad(pieces, owners, total, core=None, cost=HEAVY):
    split = core is not None
    operands, shapes, scratch = [], [], []
    for lefts, rights, turned, target in pieces:
        operands += [*lefts, *rights]
        shapes.append((len(lefts), len(rights), turned, target))
        rows = lefts[0].shape[0 if turned else 1]
        tokens = sum(r.shape[0] for r in rights)
        scratch += [pltpu.VMEM((rows, tokens), LOW), pltpu.VMEM((tokens, rights[0].shape[1]), LOW)]
    out = jax.ShapeDtypeStruct((owners // 2, rows // owners, total) if split else (rows, total), LOW)
    return local_call(
        functools.partial(grad_kernel, owners=owners, pieces=shapes, total=total, split=split),
        "weight_grad",
        (out, out) if split else out,
        *operands,
        scalars=(core,) if split else (),
        scratch=scratch,
        cost=cost,
    )


def spread_kernel(all_ref, out_ref, qkv_ref, *small):
    owners, _, _ = all_ref.shape
    width = out_ref.shape[1]
    part = out_ref.shape[0] // owners
    for owner in range(owners):
        rows = slice(owner * part, (owner + 1) * part)
        out_ref[rows] = all_ref[owner, :part, :width]
        qkv_ref[rows] = all_ref[owner, :part, width:]
        for ref in small:
            ref[owner] = all_ref[owner, part:, :]


def spread(gathered, part, width):
    owners, rows, columns = gathered.shape
    return local_call(
        spread_kernel,
        "spread",
        [
            jax.ShapeDtypeStruct((owners * part, width), LOW),
            jax.ShapeDtypeStruct((owners * part, columns - width), LOW),
        ]
        + [jax.ShapeDtypeStruct((owners, rows - part, columns), LOW)] * (rows > part),
        gathered,
        cost=LIGHT,
    )


def unit_tiles(owners, half):
    flank = owners // 2 * half
    return [
        (side * flank + start, min(512, flank - start), side, start)
        for side in range(2)
        for start in range(0, flank, 512)
    ]


def up_tile(feed_ref, tile, part, width):
    _, count, side, start = tile
    lanes = slice(width + start, width + start + count)
    rows = slice(side * part, (side + 1) * part)
    return jnp.concatenate([feed_ref[owner, rows, lanes] for owner in range(feed_ref.shape[0])], axis=0)


def down_tile(feed_ref, tile, half, width):
    first, count, _, _ = tile
    pieces = []
    while count:
        owner, row = divmod(first, half)
        size = min(count, half - row)
        pieces.append(feed_ref[owner, row : row + size, :width])
        first, count = first + size, count - size
    return jnp.concatenate(pieces, axis=0)


GELU_SCALE = (2 / math.pi) ** 0.5


def feed_forward_kernel(mine_ref, other_ref, feed_ref, bias_ref, pre_ref, act_ref, *refs, half):
    tokens, width = mine_ref.shape
    owners = feed_ref.shape[0]
    part = width // owners
    both = jnp.concatenate([mine_ref[...], other_ref[...]], axis=0)
    if refs:
        keep_ref, leave_ref, acc_ref = refs
        acc_ref[...] = jnp.zeros_like(acc_ref)
    for tile in unit_tiles(owners, half):
        span = slice(tile[0], tile[0] + tile[1])
        pre = mm(both, up_tile(feed_ref, tile, part, width)) + bias_ref[:, span]
        pre_ref[:, span] = pre
        act = (0.5 * pre * (1 + jnp.tanh(GELU_SCALE * (pre + 0.044715 * (pre * pre * pre))))).astype(LOW)
        act_ref[:, span] = act
        if refs:
            acc_ref[...] += mm(act, down_tile(feed_ref, tile, half, width))
    if refs:
        keep_ref[...] = acc_ref[:tokens]
        leave_ref[...] = acc_ref[tokens:].astype(LOW)


def feed_forward(mine, other, feed, bias, half, mixed):
    tokens, width = mine.shape
    units = feed.shape[0] * half
    shapes = [jax.ShapeDtypeStruct((2 * tokens, units), FULL), jax.ShapeDtypeStruct((2 * tokens, units), LOW)]
    if mixed:
        shapes += [jax.ShapeDtypeStruct((tokens, width), FULL), jax.ShapeDtypeStruct((tokens, width), LOW)]
    return local_call(
        functools.partial(feed_forward_kernel, half=half),
        "feed_forward",
        shapes,
        mine,
        other,
        feed,
        bias,
        scratch=[pltpu.VMEM((2 * tokens, width), FULL)] * mixed,
    )


def feed_out_kernel(act_ref, feed_ref, keep_ref, leave_ref, acc_ref, *, half):
    tokens, width = keep_ref.shape
    acc_ref[...] = jnp.zeros_like(acc_ref)
    for tile in unit_tiles(feed_ref.shape[0], half):
        acc_ref[...] += mm(act_ref[:, tile[0] : tile[0] + tile[1]], down_tile(feed_ref, tile, half, width))
    keep_ref[...] = acc_ref[:tokens]
    leave_ref[...] = acc_ref[tokens:].astype(LOW)


def feed_out(act, feed, width, half):
    tokens = act.shape[0] // 2
    return local_call(
        functools.partial(feed_out_kernel, half=half),
        "feed_out",
        (jax.ShapeDtypeStruct((tokens, width), FULL), jax.ShapeDtypeStruct((tokens, width), LOW)),
        act,
        feed,
        scratch=[pltpu.VMEM((2 * tokens, width), FULL)],
    )


def feed_backward_kernel(
    mine_ref, other_ref, pre_ref, feed_ref, low_ref, grad_ref, keep_ref, leave_ref, bias_ref, acc_ref, *, half
):
    tokens, width = mine_ref.shape
    owners = feed_ref.shape[0]
    part = width // owners
    low_ref[:tokens] = mine_ref[...]
    low_ref[tokens:] = other_ref[...]
    acc_ref[...] = jnp.zeros_like(acc_ref)
    for tile in unit_tiles(owners, half):
        span = slice(tile[0], tile[0] + tile[1])
        pre = pre_ref[:, span]
        square = pre * pre
        bend = jnp.tanh(GELU_SCALE * (pre + 0.044715 * pre * square))
        slope = 0.5 * (1 + bend) + 0.5 * pre * (1 - bend * bend) * (GELU_SCALE * (1 + 3 * 0.044715 * square))
        grad = mm_cols(low_ref[...], down_tile(feed_ref, tile, half, width)) * slope
        bias_ref[:, span] = jnp.sum(grad, axis=0, keepdims=True)
        grad = grad.astype(LOW)
        grad_ref[:, span] = grad
        acc_ref[...] += mm_cols(grad, up_tile(feed_ref, tile, part, width))
    keep_ref[...] = acc_ref[:tokens]
    leave_ref[...] = acc_ref[tokens:].astype(LOW)


def feed_backward(mine, other, pre_act, feed, half):
    tokens, width = mine.shape
    units = pre_act.shape[1]
    return local_call(
        functools.partial(feed_backward_kernel, half=half),
        "feed_backward",
        (
            jax.ShapeDtypeStruct((2 * tokens, width), LOW),
            jax.ShapeDtypeStruct((2 * tokens, units), LOW),
            jax.ShapeDtypeStruct((tokens, width), FULL),
            jax.ShapeDtypeStruct((tokens, width), LOW),
            jax.ShapeDtypeStruct((1, units), FULL),
        ),
        mine,
        other,
        pre_act,
        feed,
        scratch=[pltpu.VMEM((2 * tokens, width), FULL)],
    )


def mid_backward_kernel(
    side_ref, keep_ref, got_ref, hidden_ref, gain_ref, grad_ref, proj_ref, *outs
):
    after_ref, send_ref, mine_ref, other_ref, g_gain_ref, g_bias_ref, g_out_ref, g_down_ref = outs
    upstream = keep_ref[...] + got_ref[...].astype(FULL)
    grad = grad_ref[...].astype(FULL)
    back, g_gain, g_bias = normalize_back(upstream, *normalize(hidden_ref[...]), gain_ref[...])
    after = grad + back
    after_ref[...] = after
    g_gain_ref[...] = g_gain
    g_bias_ref[...] = g_bias
    g_out_ref[...] = jnp.sum(after, axis=0, keepdims=True)
    g_down_ref[...] = jnp.sum(grad, axis=0, keepdims=True)
    low = after.astype(LOW)
    flank = mine_ref.shape[1]
    for side in range(2):

        @pl.when(side_ref[0] == side)
        def _():
            mine_ref[...] = low[:, side * flank : (side + 1) * flank]
            other_ref[...] = low[:, (1 - side) * flank : (2 - side) * flank]

    ranks, slab, _ = send_ref.shape
    for rank in range(ranks):
        send_ref[rank] = mm_cols(proj_ref[rank * slab : (rank + 1) * slab, :], low).astype(LOW)


def mid_backward(side, keep, got, hidden, gain, grad, proj, ranks):
    tokens, width = keep.shape
    row = jax.ShapeDtypeStruct((1, width), FULL)
    half = jax.ShapeDtypeStruct((tokens, width // 2), LOW)
    return local_call(
        mid_backward_kernel,
        "mid_backward",
        (
            jax.ShapeDtypeStruct((tokens, width), FULL),
            jax.ShapeDtypeStruct((ranks, width // ranks, tokens), LOW),
            half,
            half,
            row,
            row,
            row,
            row,
        ),
        keep,
        got,
        hidden,
        gain,
        grad,
        proj,
        scalars=(side,),
    )


def end_backward_kernel(got_ref, hidden_ref, gain_ref, after_ref, out_ref, low_ref, g_gain_ref, g_bias_ref):
    upstream = got_ref[0].astype(FULL)
    for rank in range(1, got_ref.shape[0]):
        upstream += got_ref[rank].astype(FULL)
    back, g_gain, g_bias = normalize_back(upstream, *normalize(hidden_ref[...].astype(FULL)), gain_ref[...])
    total = after_ref[...] + back
    out_ref[...] = total
    low_ref[...] = total.astype(LOW)
    g_gain_ref[...] = g_gain
    g_bias_ref[...] = g_bias


def end_backward(got, hidden, gain, after):
    tokens, width = after.shape
    row = jax.ShapeDtypeStruct((1, width), FULL)
    return local_call(
        end_backward_kernel,
        "end_backward",
        (
            jax.ShapeDtypeStruct((tokens, width), FULL),
            jax.ShapeDtypeStruct((tokens, width), LOW),
            row,
            row,
        ),
        got,
        hidden,
        gain,
        after,
    )


def meet_kernel(chip_ref, keep_ref, got_ref, *outs):
    step = pl.program_id(0)
    for j, out in enumerate(outs):

        @pl.when(step == j)
        def _():
            out[...] = (keep_ref[0].astype(FULL) + got_ref[0].astype(FULL)).astype(LOW)


def meet_cores(chip, keep, got):
    chips, rows, columns = keep.shape
    block = pl.BlockSpec((1, rows, columns), lambda j, chip_ref: (chip_ref[0] ^ j, 0, 0))
    return pl.pallas_call(
        meet_kernel,
        grid_spec=pltpu.PrefetchScalarGridSpec(
            num_scalar_prefetch=1,
            grid=(chips,),
            in_specs=[block, block],
            out_specs=[pl.BlockSpec((rows, columns), lambda j, chip_ref: (0, 0))] * chips,
        ),
        out_shape=[jax.ShapeDtypeStruct((rows, columns), LOW)] * chips,
        compiler_params=pltpu.CompilerParams(vmem_limit_bytes=24 << 20),
        cost_estimate=LIGHT,
        name="meet_cores",
    )(chip.reshape(1), keep, got)


def add_kernel(*refs):
    total = refs[0][...].astype(FULL)
    for ref in refs[1:-1]:
        total += ref[...].astype(FULL)
    refs[-1][...] = total.astype(LOW)


def add_all(*values, cost=LIGHT):
    return local_call(add_kernel, "add_all", jax.ShapeDtypeStruct(values[0].shape, LOW), *values, cost=cost)


def up_kernel(side_ref, own_ref, across_ref, *refs, owners, half):
    out_ref = refs[-1]
    hidden_part = out_ref.shape[2] // owners
    for mine in range(2):

        @pl.when(side_ref[0] == mine)
        def _():
            for side in range(2):
                ref = own_ref if side == mine else across_ref
                first = side * half
                count = min(half, hidden_part - first)
                for owner in range(owners):
                    target = owner * hidden_part + first
                    source = owner * half
                    out_ref[0, :, target : target + count] = ref[:, source : source + count].astype(FULL)


def mixed_kernel(me_ref, own_ref, across_ref, *refs, ranks, offset):
    qkv_out, out_out = refs[-2:]
    width = out_out.shape[2]
    slab, flank, pairs = width // ranks, width // 2, ranks // 2
    for me in range(ranks):

        @pl.when(me_ref[0] == me)
        def _():
            side, pair = me % 2, me // 2
            for flip, ref in enumerate((own_ref, across_ref)):
                for j in range(pairs):
                    rank = (pair - j) % pairs * 2 + (side ^ flip)
                    for i in range(3):
                        target = (i * ranks + rank) * slab
                        source = j * offset + i * slab
                        qkv_out[0, :, target : target + slab] = ref[:, source : source + slab].astype(FULL)
                target = (side ^ flip) * flank
                out_out[0, :, target : target + flank] = ref[:, pairs * offset :].astype(FULL)


def write_layer(kernel, name, layer, layers, shapes, earlier, scalar, *values):
    return pl.pallas_call(
        kernel,
        grid=(1,),
        out_shape=tuple(jax.ShapeDtypeStruct((layers,) + s, FULL) for s in shapes),
        in_specs=[pl.BlockSpec(memory_space=pltpu.SMEM)]
        + [pl.BlockSpec(v.shape, lambda i: (0, 0)) for v in values]
        + [pl.BlockSpec(memory_space=pl.ANY)] * len(earlier),
        out_specs=tuple(pl.BlockSpec((1,) + s, lambda i: (layer, 0, 0)) for s in shapes),
        input_output_aliases={1 + len(values) + i: i for i in range(len(earlier))},
        compiler_params=pltpu.CompilerParams(vmem_limit_bytes=40 << 20),
        cost_estimate=cost_of(name + str(layer)),
        name=name,
    )(scalar.reshape(1), *values, *earlier)


def down_kernel(side_ref, *refs):
    out_ref = refs[-1]
    half = refs[0].shape[0]
    hidden_part = out_ref.shape[0]
    for mine in range(2):

        @pl.when(side_ref[0] == mine)
        def _():
            for layer in range(len(refs) // 2):
                for side in range(2):
                    ref = refs[2 * layer + (side != mine)]
                    first = side * half
                    count = min(half, hidden_part - first)
                    out_ref[first : first + count, layer, :] = ref[:count].astype(FULL)


def pack_kernel(side_ref, *refs, owners, layers, half):
    out_ref = refs[-1]
    each = len(refs) // layers
    out_ref[...] = jnp.zeros_like(out_ref)
    target = 0
    for layer in range(layers):
        rows = refs[layer * each : (layer + 1) * each]
        for ref in rows[:-1]:
            part = ref.shape[1] // owners
            for owner in range(owners):
                out_ref[owner : owner + 1, target : target + part] = ref[:, owner * part : (owner + 1) * part]
            target += part
        for side in range(2):

            @pl.when(side_ref[0] == side)
            def _():
                for owner in range(owners):
                    first = target + side * half
                    out_ref[owner : owner + 1, first : first + half] = rows[-1][
                        :, owner * half : (owner + 1) * half
                    ]

        target += 2 * half


def unpack_kernel(first_ref, second_ref, *outs, layers, half):
    values = first_ref[...] + second_ref[...]
    part = outs[0].shape[1]
    target = 0
    for layer in range(layers):
        for out in outs[:-1]:
            out[layer : layer + 1, :] = values[:, target : target + part]
            target += part
        out = outs[-1]
        out[layer : layer + 1, :] = values[:, target : target + out.shape[1]]
        target += 2 * half


class Order:
    def __init__(self):
        self.last = ()

    def enter(self, *values):
        if not self.last:
            return values
        return lax.optimization_barrier(tuple(values) + self.last)[: len(values)]

    def leave(self, *values):
        self.last = tuple(values)


class Chain:
    def __init__(self, steps):
        self.steps = steps
        self.result = None
        self.step()

    def step(self):
        try:
            next(self.steps)
        except StopIteration as stop:
            self.result = stop.value


def make_body(ranks, owners):
    pairs, chips = ranks // 2, owners // 2

    def shift(value, step):
        return lax.ppermute(value, "seq", [(i, (i + step) % ranks) for i in range(ranks)])

    def swap(value):
        return lax.ppermute(value, "seq", [(i, i ^ 1) for i in range(ranks)])

    def pair_shift(value, step):
        return lax.ppermute(value, "seq", [(i, (i + 2 * step) % ranks) for i in range(ranks)])

    def owner_xor(value, bits):
        return lax.ppermute(value, "fsdp", [(i, i ^ bits) for i in range(owners)])

    def exchange(blocks):
        return lax.all_to_all(blocks, "seq", split_axis=0, concat_axis=0, tiled=True)

    def body(
        block_input,
        grad_output,
        attn_norm_gain,
        attn_norm_bias,
        qkv_weight,
        qv_bias,
        out_weight,
        out_bias,
        mlp_norm_gain,
        mlp_norm_bias,
        up_weight,
        up_bias,
        down_weight,
        down_bias,
    ):
        layers = qkv_weight.shape[0]
        tokens, width = block_input.shape[1:]
        slab, flank = width // ranks, width // 2
        part = qkv_weight.shape[1]
        hidden_part = down_weight.shape[1]
        half = -(-hidden_part // 32) * 16
        me = lax.axis_index("seq")
        owner = lax.axis_index("fsdp")
        core, chip = owner % 2, owner // 2
        side, pair = me % 2, me // 2

        def at(value, index, axis=0):
            return lax.dynamic_index_in_dim(value, index, axis, keepdims=False)

        def put(value, block, *index):
            return lax.dynamic_update_slice(
                value, block.reshape((1,) * len(index) + block.shape), index + (0,) * block.ndim
            )

        def rank_at(j):
            return (me + j) % ranks

        order = Order()

        def owner_steps(keep, send, tag):
            got = owner_xor(send, 1)
            yield
            (got,) = order.enter(got)
            mine, *sends = meet_cores(chip, keep, got)
            order.leave(*sends)
            got = [owner_xor(send, 2 * j) for j, send in enumerate(sends, 1)]
            yield
            return add_all(mine, *order.enter(*got), cost=cost_of("sum_" + tag))

        def queue_steps(value):
            value = lax.psum_scatter(value, "fsdp", scatter_dimension=0, tiled=True)
            yield
            return order.enter(value)[0]

        def pair_steps(value, tag):
            order.leave(value)
            got = [pair_shift(value, j) for j in range(1, pairs)]
            yield
            own = add_all(value, *order.enter(*got), cost=cost_of("add_" + tag))
            order.leave(own)
            across = swap(own)
            yield
            return own, order.enter(across)[0]

        def mixed_steps(value, tag):
            order.leave(value)
            got = [pair_shift(value, j) for j in range(1, pairs)]
            yield
            got = order.enter(*got)
            total = add_all(*[v[:, offset:] for v in (value, *got)], cost=cost_of("add_" + tag))
            shares = [v[:, :offset] for v in (value, *got)]
            send = jnp.concatenate([*shares, total], axis=1)
            order.leave(send)
            across = swap(send)
            yield
            (across,) = order.enter(across)
            return send, across

        def written(steps, stage, write, tag):
            value = yield from steps
            value = yield from stage(value, tag)
            value = write(*value)
            order.leave(*value)
            return value

        columns = width + 3 * slab
        offset = -(-3 * slab // 128) * 128

        def gather_tokens(mine):
            return exchange(jnp.broadcast_to(mine, (ranks,) + mine.shape))

        all_input = gather_tokens(block_input[0])
        small = (
            attn_norm_gain,
            attn_norm_bias,
            qv_bias.reshape(2 * layers, part),
            out_bias,
            mlp_norm_gain,
            mlp_norm_bias,
            down_bias,
            up_bias,
        )
        down_turned = down_weight.transpose(1, 0, 2)

        attn_shares, feeds = [], []
        for layer in range(layers):
            share = attn_share(
                me, out_weight[layer], *order.enter(qkv_weight[layer]), small if layer == 0 else (), layers, ranks
            )
            order.leave(share)
            attn_shares.append(lax.all_gather(share, "fsdp", axis=0))
            share = feed_share(side, *order.enter(up_weight[layer]), down_turned, layer, owners, half)
            order.leave(share)
            feeds.append(lax.all_gather(share, "fsdp", axis=0))
        (all_input,) = order.enter(all_input)
        normed_all, _ = normalize(all_input.reshape(ranks * tokens, width).astype(FULL))
        order.leave(normed_all)
        *weights, small_all = spread(*order.enter(attn_shares[0]), part, width)
        order.leave(*weights, small_all)
        rows_all = small_all[:, :layers, : 8 * part].reshape(owners, layers, 8, part)
        rows_all = rows_all.transpose(1, 2, 0, 3).reshape(layers, 8, width).astype(FULL)
        up_all = small_all[:, :layers, 8 * part : 8 * part + hidden_part].astype(FULL)
        up_all = jnp.pad(up_all, ((0, 0), (0, 0), (0, 2 * half - hidden_part)))

        vectors = []
        for layer in range(layers):
            rows = rows_all[layer]
            vectors.append(
                dict(
                    gain_one=rows[0],
                    bias_one=rows[1],
                    bias_q=lax.dynamic_slice(rows[2], (me * slab,), (slab,)),
                    bias_v=lax.dynamic_slice(rows[3], (me * slab,), (slab,)),
                    bias_out=rows[4],
                    gain_two=rows[5],
                    bias_two=rows[6],
                    bias_down=rows[7],
                    bias_up=lax.dynamic_slice(
                        up_all[:, layer], (0, side * half), (owners, half)
                    ).reshape(owners * half),
                )
            )

        hidden = block_input[0].astype(FULL)
        stored = []
        for layer in range(layers):
            v = vectors[layer]
            last_layer = layer == layers - 1
            hidden_in = hidden
            normed_one, _ = normalize(hidden)
            if layer == 0:
                attn_in = (normed_all * v["gain_one"] + v["bias_one"]).astype(LOW)
            else:
                attn_mine = (normed_one * v["gain_one"] + v["bias_one"]).astype(LOW)
                order.leave(attn_mine)
                attn_in = gather_tokens(attn_mine)
                weights = spread(*order.enter(attn_shares[layer]), part, width)
                order.leave(*weights)
                attn_in = order.enter(attn_in)[0].reshape(ranks * tokens, width)
            proj_out, proj_qkv = weights
            bias_row = jnp.concatenate([v["bias_q"], jnp.zeros((slab,), FULL), v["bias_v"]])
            projected = (mm(attn_in, proj_qkv) + bias_row).astype(LOW)
            qkv = jnp.stack([projected[:, i * slab : (i + 1) * slab] for i in range(3)])
            out_heads, lse = attend_forward(qkv, ranks)
            order.leave(out_heads)
            attended = order.enter(exchange(out_heads))[0].reshape(width, tokens)
            after_attn = hidden + mm_rows(attended, proj_out) + v["bias_out"]
            normed_two, _ = normalize(after_attn)
            mlp_mine = (normed_two * v["gain_two"] + v["bias_two"]).astype(LOW)
            order.leave(mlp_mine)
            mlp_other = swap(mlp_mine)
            attended_other = swap(order.enter(attended)[0])
            mlp_other, attended_other = order.enter(mlp_other, attended_other)
            (feed,) = order.enter(feeds[layer])
            pre_act, activated, *mixed = feed_forward(
                mlp_mine, mlp_other, feed, v["bias_up"].reshape(1, owners * half), half, not last_layer
            )
            if last_layer:
                order.leave(pre_act, activated)
            else:
                mixed, leaving = mixed
                order.leave(leaving)
                (other,) = order.enter(swap(leaving))
                hidden = after_attn + mixed + other.astype(FULL) + v["bias_down"]
            stored.append(
                (
                    (proj_qkv, proj_out, feed),
                    (block_input[0] if layer == 0 else hidden_in, attn_in, qkv, lse, attended, attended_other),
                    (after_attn, mlp_mine, mlp_other, pre_act, activated),
                )
            )

        def writer(key, kernel, layer, scalar, *shapes):
            def write(*values):
                outs[key] = write_layer(
                    kernel, "write_" + key, layer, layers, shapes, outs[key], scalar, *values
                )
                return outs[key]

            return write

        def held(*values):
            return values

        def sum_rows(value):
            return jnp.sum(value, axis=0, keepdims=True)

        grad_hidden = grad_mine = grad_output[0]
        small_grads = [None] * layers
        downs = [None] * layers
        outs = dict(up=(), mixed=())
        before = None
        for layer in reversed(range(layers)):
            v = vectors[layer]
            tag = "_late" if before else "_early"
            proj_qkv, proj_out, feed = stored[layer][0]
            hidden_in, attn_in, qkv, lse, attended, attended_other = stored[layer][1]
            mid_hidden, mlp_mine, mlp_other, pre_act, activated = stored[layer][2]
            grad_other = swap(grad_mine)
            if before:
                before["down"].step()
                if PLAN.get("final_early", 0):
                    grad_other, final_other = order.enter(grad_other, final_other)
            (grad_other,) = order.enter(grad_other)
            grad_low, grad_pre_low, mixed, leaving, g_up_bias = feed_backward(
                grad_mine, grad_other, pre_act, feed, half
            )
            order.leave(leaving)
            other = swap(leaving)
            g_down = weight_grad(
                [((activated,), order.enter(grad_low), False, 0)], owners, width
            )
            order.leave(g_down)
            down_chain = Chain(written(queue_steps(g_down), pair_steps, held, "down" + tag))
            keep, send = weight_grad(
                [((mlp_mine, mlp_other), order.enter(grad_pre_low), False, 0)],
                owners,
                half * owners,
                core,
                cost_of("wgu" + tag),
            )
            order.leave(send)
            up_chain = Chain(
                written(
                    owner_steps(keep, send, "up" + tag),
                    pair_steps,
                    writer(
                        "up",
                        functools.partial(up_kernel, owners=owners, half=half),
                        layer,
                        side,
                        (part, owners * hidden_part),
                    ),
                    "up" + tag,
                )
            )
            (other,) = order.enter(other)
            order.leave(other)
            if before:
                before["up"].step()
            grad_after, sends, after_mine, after_send, g_gain_two, g_bias_two, g_out_bias, g_down_bias = mid_backward(
                side,
                mixed,
                *order.enter(other),
                mid_hidden,
                v["gain_two"].reshape(1, width),
                grad_hidden,
                proj_out,
                ranks,
            )
            order.leave(sends)
            grad_heads = exchange(sends)
            after_other = swap(after_send)
            up_chain.step()
            if PLAN.get("other" + tag, 1):
                grad_heads, after_other = order.enter(grad_heads, after_other)
            else:
                (grad_heads,) = order.enter(grad_heads)
            order.leave(grad_heads)
            if before:
                before["down"].step()
                before["mixed"].step()
            grad_proj, leaving, g_q_bias, g_v_bias = attend_backward(
                qkv, *order.enter(grad_heads), lse, proj_qkv, ranks
            )
            order.leave(leaving)
            arrived = exchange(leaving)
            if before:
                before["up"].step()
            grad_proj, after_other = order.enter(grad_proj, after_other)
            g_mixed = weight_grad(
                [
                    ((attn_in,), (grad_proj,), False, 0),
                    ((attended, attended_other), (after_mine, after_other), True, offset),
                ],
                owners,
                offset + flank,
                core if before else None,
            )
            order.leave(*(g_mixed if before else (g_mixed,)))
            mixed_chain = Chain(
                written(
                    owner_steps(*g_mixed, "mixed" + tag) if before else queue_steps(g_mixed),
                    mixed_steps,
                    writer(
                        "mixed",
                        functools.partial(mixed_kernel, ranks=ranks, offset=offset),
                        layer,
                        me,
                        (part, 3 * width),
                        (part, width),
                    ),
                    "mixed" + tag,
                )
            )
            if before:
                if PLAN.get("sum_in", 1):
                    up_chain.step()
                if PLAN.get("down_in", 1):
                    down_chain.step()
                mixed_chain.step()
            else:
                final, leaving = feed_out(*order.enter(activated), feed, width, half)
                order.leave(leaving)
                final_other = swap(leaving)
            (arrived,) = order.enter(arrived)
            grad_hidden, grad_mine, g_gain_one, g_bias_one = end_backward(
                arrived, hidden_in, v["gain_one"].reshape(1, width), grad_after
            )
            order.leave(grad_hidden)
            if before:
                if not PLAN.get("sum_in", 1):
                    up_chain.step()
                if not PLAN.get("down_in", 1):
                    down_chain.step()
                before["mixed"].step()
                before["down"].step()
            else:
                up_chain.step()
            last, before = before, dict(up=up_chain, down=down_chain, mixed=mixed_chain)
            downs[layer] = down_chain

            zeros = jnp.zeros((1, width), FULL)
            small_grads[layer] = (
                g_gain_one,
                g_bias_one,
                lax.dynamic_update_slice(zeros, g_q_bias, (0, me * slab)),
                lax.dynamic_update_slice(zeros, g_v_bias, (0, me * slab)),
                g_out_bias,
                g_gain_two,
                g_bias_two,
                g_down_bias,
                g_up_bias,
            )

        each = 8 * part + 2 * half
        v = vectors[layers - 1]
        small_sum = local_call(
            functools.partial(pack_kernel, owners=owners, layers=layers, half=half),
            "pack_small",
            jax.ShapeDtypeStruct((owners, -(-layers * each // 128) * 128), FULL),
            *order.enter(*[row for grads in small_grads for row in grads]),
            scalars=(side,),
            cost=LIGHT,
        )
        order.leave(small_sum)
        small_sum = lax.all_to_all(small_sum, "fsdp", split_axis=0, concat_axis=0, tiled=True)
        steps = dict(d=before["down"], m=before["mixed"], u=before["up"], w=last["mixed"])
        for key in PLAN.get("tail", "udwm"):
            steps[key].step()
        small_sum = sum_rows(order.enter(small_sum)[0])
        order.leave(small_sum)
        total = small_sum
        for j in range(1, pairs):
            total = total + pair_shift(small_sum, j)
        before["up"].step()
        before["mixed"].step()
        before["down"].step()
        (total,) = order.enter(total)
        order.leave(total)
        total_other = swap(total)
        down_out = local_call(
            down_kernel,
            "write_down",
            jax.ShapeDtypeStruct((hidden_part, layers, width), FULL),
            *order.enter(*[piece for chain in downs for piece in chain.result]),
            scalars=(side,),
        )
        order.leave(down_out)
        (final_other,) = order.enter(final_other)
        block_output = (after_attn + final + final_other.astype(FULL) + v["bias_down"]).astype(LOW)[None]
        order.leave(block_output)
        s = local_call(
            functools.partial(unpack_kernel, layers=layers, half=half),
            "unpack_small",
            tuple(jax.ShapeDtypeStruct((layers, n), FULL) for n in [part] * 8 + [hidden_part]),
            *order.enter(total, total_other),
        )
        order.leave(*s)
        before["mixed"].step()
        return (
            block_output,
            grad_hidden[None],
            s[0],
            s[1],
            outs["mixed"][0],
            jnp.stack([s[2], s[3]], axis=1),
            outs["mixed"][1],
            s[4],
            s[5],
            s[6],
            outs["up"][0],
            s[8],
            down_out.transpose(1, 0, 2),
            s[7],
        )

    return body


def solution(mesh):
    row, cols, deep = P(None, "fsdp"), P("fsdp", "seq", None), P(None, "fsdp", None)
    last = P(None, None, "fsdp")
    return jax.shard_map(
        make_body(mesh.shape["seq"], mesh.shape["fsdp"]),
        mesh=mesh,
        in_specs=(cols, cols, row, row, deep, last, deep, row, row, row, deep, row, deep, row),
        out_specs=(cols, cols, row, row, deep, last, deep, row, row, row, deep, row, deep, row),
        check_vma=False,
    )
```
